32 devices in a mesh: ctx: 16 (over z, x, core), wt: 2 (over y).
Axes of the slice: x: 2, y: 2, z: 4, core: 2. Of those that a mesh axis runs over, the one named last changes fastest.
Arguments:
- content: bfloat16 [2, 2, 1024, 768], P('wt', None, 'ctx'), may hold values from -6 to 6
- query_stream: bfloat16 [2, 384, 768], P('wt', 'ctx'), may hold values from -6 to 6
- token_order: int32 [2, 2048], P('wt'), may hold values from 0 to 2047, each once within a row
- targets: int32 [2, 384], P('wt'), may hold values from 1 to 2047, as said below
- query_weight: bfloat16 [768, 768], P(None, 'wt'), may hold values from -0.21875 to 0.21875
- key_weight: bfloat16 [768, 768], P(None, 'wt'), may hold values from -0.21875 to 0.21875
- value_weight: bfloat16 [768, 768], P(None, 'wt'), may hold values from -0.21875 to 0.21875
- output_weight: bfloat16 [768, 768], P(None, 'wt'), may hold values from -1.75 to 1.75
- query_bias: bfloat16 [768], P('wt'), may hold values from -3 to 3
- value_bias: bfloat16 [768], P('wt'), may hold values from -2 to 2
- output_bias: bfloat16 [768], P('wt'), may hold values from -3 to 3
- bias_table: bfloat16 [32, 12], P('wt'), may hold values from -4 to 4
- first_gain: bfloat16 [768], P('wt'), may hold values from 0.099609375 to 1.8984375
- first_shift: bfloat16 [768], P('wt'), may hold values from -2 to 2
- inner_weight: bfloat16 [768, 3072], P(None, 'wt'), may hold values from -0.21875 to 0.21875
- inner_bias: bfloat16 [3072], P('wt'), may hold values from -3 to 3
- outer_weight: bfloat16 [3072, 768], P(None, 'wt'), may hold values from -0.109375 to 0.109375
- outer_bias: bfloat16 [768], P('wt'), may hold values from -3 to 3
- second_gain: bfloat16 [768], P('wt'), may hold values from 0.099609375 to 1.8984375
- second_shift: bfloat16 [768], P('wt'), may hold values from -2 to 2
- content_cotangent: bfloat16 [2, 2, 1024, 768], P('wt', None, 'ctx'), may hold values from -6 to 6
- query_cotangent: bfloat16 [2, 384, 768], P('wt', 'ctx'), may hold values from -6 to 6
Outputs:
- content_result: bfloat16 [2, 2, 1024, 768], P('wt', None, 'ctx')
- query_result: bfloat16 [2, 384, 768], P('wt', 'ctx')
- content_gradient: float32 [2, 2, 1024, 768], P('wt', None, 'ctx')
- query_gradient: float32 [2, 384, 768], P('wt', 'ctx')
- query_weight_gradient: float32 [768, 768], P(None, 'wt')
- key_weight_gradient: float32 [768, 768], P(None, 'wt')
- value_weight_gradient: float32 [768, 768], P(None, 'wt')
- output_weight_gradient: float32 [768, 768], P(None, 'wt')
- query_bias_gradient: float32 [768], P('wt')
- value_bias_gradient: float32 [768], P('wt')
- output_bias_gradient: float32 [768], P('wt')
- bias_table_gradient: float32 [32, 12], P('wt')
- first_gain_gradient: float32 [768], P('wt')
- first_shift_gradient: float32 [768], P('wt')
- inner_weight_gradient: float32 [768, 3072], P(None, 'wt')
- inner_bias_gradient: float32 [3072], P('wt')
- outer_weight_gradient: float32 [3072, 768], P(None, 'wt')
- outer_bias_gradient: float32 [768], P('wt')
- second_gain_gradient: float32 [768], P('wt')
- second_shift_gradient: float32 [768], P('wt')
The draws below stay inside these ranges and needn't reach their ends.
Inputs may be any that keep to these rules, and one draw needn't show every extreme that they name: `token_order`: each row is a permutation of the initial positions 0 to 2047. `targets`: places of the predicted tokens in the permuted order, all different within a sequence.
All inputs are finite; a program needn't handle non-finite values.
Results may differ from the reference program's by a relative error of at most 0.015.
The reference program's roundings to bfloat16 on the way count: a program that leaves them out, or rounds other values in their place, can miss the bound.
Values may be sent and summed in bfloat16 or wider, within the bound.
No kernel may reach another device: no remote copies, remote signals or barrier semaphores. Data moves between devices by JAX's collectives and lax.ppermute only.
A program may use at most 256 MiB of HBM per device.

```python
import jax
import jax.numpy as jnp
from jax import lax

D = 768
HEADS = 12
HEAD_DIM = 64
FF = 3072
BUCKETS = 32
TOK_DEV = 128
HALF_DEV = 64
Q_DEV = 24
SEQS = 2
SEQ_LEN = 2048
HALF = 1024
NQ = 384
N_CTX = 16


def draw_targets(key, part):
    places = jnp.broadcast_to(jnp.arange(2, SEQ_LEN - 1, dtype=jnp.int32), (SEQS, SEQ_LEN - 3))
    shuffled = jax.random.permutation(key, places, axis=1, independent=True)[:, :NQ - 2]
    ends = jnp.broadcast_to(jnp.array([SEQ_LEN - 1, 1], dtype=jnp.int32), (SEQS, 2))
    joined = jnp.concatenate([ends, shuffled], axis=1)
    return jax.random.permutation(jax.random.fold_in(key, 7), joined, axis=1, independent=True)


def block_levels(rng, shape, split, low, largest):
    factor_of, own = 1.0, jax.random.fold_in(rng, 6)
    for position, shards_of in split:
        draws = jnp.exp(jax.random.uniform(jax.random.fold_in(own, position), (shards_of,), jnp.float32, low / len(split), largest / len(split)))
        factor_of = factor_of * jnp.repeat(draws, shape[position] // shards_of).reshape([-1 if axis == position else 1 for axis in range(len(shape))])
    return factor_of


def normal_values(stream_key, dims, scale, most, pieces=(), held_as=jnp.bfloat16):
    drawn = jax.random.normal(stream_key, dims, jnp.float32) * scale
    if len(pieces) > 0:
        drawn = block_levels(stream_key, dims, pieces, -0.22, 0.18) * drawn
    return jnp.clip(drawn, min=-most, max=most).astype(held_as)


def setup_inputs(seed: int = 0) -> dict:
    seeds = jax.random.split(jax.random.key(seed), 23)
    return {
        "content": normal_values(seeds[0], (SEQS, 2, HALF, D), 1.0, 6.0, ((0, 2), (2, 16))),
        "query_stream": normal_values(seeds[1], (SEQS, NQ, D), 1.0, 6.0, ((0, 2), (1, 16))),
        "token_order": jax.vmap(lambda own: jax.random.permutation(own, SEQ_LEN))(jax.random.split(seeds[2], SEQS)).reshape((SEQS, SEQ_LEN)).astype(jnp.int32),
        "targets": draw_targets(jax.random.fold_in(seeds[22], 71), 0),
        "query_weight": normal_values(seeds[4], (D, D), D ** -0.5, 0.21875, ((1, 2),)),
        "key_weight": normal_values(seeds[5], (D, D), D ** -0.5, 0.21875, ((1, 2),)),
        "value_weight": normal_values(seeds[6], (D, D), D ** -0.5, 0.21875, ((1, 2),)),
        "output_weight": normal_values(seeds[7], (D, D), (max(D // 64, 1)) ** -0.5, 1.75, ((1, 2),)),
        "query_bias": normal_values(seeds[8], (D,), 0.5, 3.0, ((0, 2),)),
        "value_bias": normal_values(seeds[9], (D,), 0.3, 2.0, ((0, 2),)),
        "output_bias": normal_values(seeds[10], (D,), 0.5, 3.0, ((0, 2),)),
        "bias_table": normal_values(seeds[11], (BUCKETS, HEADS), 1.0, 4.0, ((0, 2),)),
        "first_gain": jnp.clip(1.0 + 0.18 * jax.random.normal(seeds[12], (D,), jnp.float32), 0.099609375, 1.8984375).astype(jnp.bfloat16),
        "first_shift": normal_values(seeds[13], (D,), 0.3, 2.0, ((0, 2),)),
        "inner_weight": normal_values(seeds[14], (D, FF), D ** -0.5, 0.21875, ((1, 2),)),
        "inner_bias": normal_values(seeds[15], (FF,), 0.5, 3.0, ((0, 2),)),
        "outer_weight": normal_values(seeds[16], (FF, D), FF ** -0.5, 0.109375, ((1, 2),)),
        "outer_bias": normal_values(seeds[17], (D,), 0.5, 3.0, ((0, 2),)),
        "second_gain": jnp.clip(1.0 + 0.18 * jax.random.normal(seeds[18], (D,), jnp.float32), 0.099609375, 1.8984375).astype(jnp.bfloat16),
        "second_shift": normal_values(seeds[19], (D,), 0.3, 2.0, ((0, 2),)),
        "content_cotangent": normal_values(seeds[20], (SEQS, 2, HALF, D), 1.0, 6.0, ((0, 2), (2, 16))),
        "query_cotangent": normal_values(seeds[21], (SEQS, NQ, D), 1.0, 6.0, ((0, 2), (1, 16))),
    }


@jax.custom_vjp
def low(v):
    return lax.optimization_barrier(v.astype(jnp.bfloat16)).astype(jnp.float32)

@jax.custom_vjp
def low_back(v):
    return v

def low_keep(v):
    return (low(v), None)

def low_pass(kept, grad):
    return (grad,)

def back_keep(v):
    return (v, None)

def back_low(kept, grad):
    return (low(grad),)
low.defvjp(low_keep, low_pass)
low_back.defvjp(back_keep, back_low)
EDGES = (1, 2, 3, 4, 5, 6, 7, 8, 12, 16, 23, 32, 46, 64, 91)
NEGATIVE = -1e+30
HIGHEST = lax.Precision.HIGHEST

def bucket_of(relative):
    magnitude = jnp.abs(relative)
    bucket_count = jnp.zeros(relative.shape, jnp.int32)
    for boundary in EDGES:
        bucket_count = bucket_count + (magnitude >= boundary).astype(jnp.int32)
    return bucket_count + 16 * (relative > 0).astype(jnp.int32)

def matmul(left, right):
    return jnp.matmul(left, right, precision=HIGHEST)

def layer_norm(hidden_rows, gain_row, shift_row):
    average = lax.optimization_barrier(jnp.mean(hidden_rows, axis=-1, keepdims=True))
    centered = hidden_rows - average
    variance = lax.optimization_barrier(jnp.mean(centered * centered, axis=-1, keepdims=True))
    return centered * lax.rsqrt(variance + 1e-05) * gain_row + shift_row

def slot_positions():
    slot_index = jnp.arange(N_CTX * TOK_DEV, dtype=jnp.int32)
    device_index = slot_index // TOK_DEV
    within_rows = slot_index % TOK_DEV
    forward_place = device_index * HALF_DEV + within_rows
    backward_place = SEQ_LEN - 1 - (device_index * HALF_DEV + within_rows - HALF_DEV)
    return jnp.where(within_rows < HALF_DEV, forward_place, backward_place)

def sequence(content_rows, query_rows, order_row, target_row, weights):
    query_weight, key_weight, value_weight, output_weight, query_bias, value_bias, output_bias, bias_table, first_gain, first_shift, inner_weight, inner_bias, outer_weight, outer_bias, second_gain, second_shift = weights
    rows_dev = TOK_DEV + Q_DEV
    slots = content_rows.reshape(2, N_CTX, HALF_DEV, D).transpose(1, 0, 2, 3).reshape(N_CTX * TOK_DEV, D)
    key_place = slot_positions()
    key_anchor = order_row[key_place]
    stacked = jnp.concatenate([slots.reshape(N_CTX, TOK_DEV, D), query_rows.reshape(N_CTX, Q_DEV, D)], axis=1)
    limits = jnp.concatenate([(key_place + 1).reshape(N_CTX, TOK_DEV), target_row.reshape(N_CTX, Q_DEV)], axis=1)
    row_anchor = jnp.concatenate([key_anchor.reshape(N_CTX, TOK_DEV), order_row[target_row].reshape(N_CTX, Q_DEV)], axis=1)
    queries = low_back(low((matmul(stacked, query_weight) + query_bias) * 0.125))
    keys = low_back(low(matmul(slots, key_weight))).reshape(SEQ_LEN, HEADS, HEAD_DIM)
    values = low_back(low(matmul(slots, value_weight) + value_bias)).reshape(SEQ_LEN, HEADS, HEAD_DIM)

    def attend(block_args):
        block_queries, block_limit, block_anchor = block_args
        scores = jnp.einsum('rhd,khd->hrk', block_queries.reshape(rows_dev, HEADS, HEAD_DIM), keys, precision=HIGHEST)
        bias_rows = jnp.take(bias_table, bucket_of(key_anchor[None, :] - block_anchor[:, None]), axis=0)
        scores = low_back(scores + jnp.transpose(bias_rows, (2, 0, 1)))
        allowed = key_place[None, :] < block_limit[:, None]
        scores = jnp.where(allowed[None], scores, NEGATIVE)
        log_total = jax.nn.logsumexp(scores, axis=-1, keepdims=True)
        probability = jnp.exp(scores - log_total)
        return jnp.einsum('hrk,khd->rhd', low(probability), values, precision=HIGHEST).reshape(rows_dev, D)
    mixed = low_back(low(lax.map(jax.checkpoint(attend), (queries, limits, row_anchor))))
    branch = low_back(matmul(mixed, output_weight) + output_bias)
    first_norm = layer_norm(stacked + branch, first_gain, first_shift)
    inner = low_back(matmul(low(first_norm), inner_weight) + inner_bias)
    hidden = low(jax.nn.gelu(inner, approximate=False))
    outer = low_back(matmul(hidden, outer_weight) + outer_bias)
    final_norm = layer_norm(first_norm + outer, second_gain, second_shift)
    content_final = final_norm[:, :TOK_DEV].reshape(N_CTX, 2, HALF_DEV, D).transpose(1, 0, 2, 3).reshape(2, N_CTX * HALF_DEV, D)
    query_final = final_norm[:, TOK_DEV:].reshape(N_CTX * Q_DEV, D)
    return (content_final, query_final)

def reference(content, query_stream, token_order, targets, query_weight, key_weight, value_weight, output_weight, query_bias, value_bias, output_bias, bias_table, first_gain, first_shift, inner_weight, inner_bias, outer_weight, outer_bias, second_gain, second_shift, content_cotangent, query_cotangent):
    primals = [content, query_stream, query_weight, key_weight, value_weight, output_weight, query_bias, value_bias, output_bias, bias_table, first_gain, first_shift, inner_weight, inner_bias, outer_weight, outer_bias, second_gain, second_shift]
    primals = [array.astype(jnp.float32) for array in primals]

    def forward(content_all, query_all, *weights):
        content_list = []
        query_list = []
        for sequence_index in range(SEQS):
            content_final, query_final = sequence(content_all[sequence_index], query_all[sequence_index], token_order[sequence_index], targets[sequence_index], weights)
            content_list.append(content_final)
            query_list.append(query_final)
        return (jnp.stack(content_list), jnp.stack(query_list))
    (content_final, query_final), pullback = jax.vjp(forward, *primals)
    grads = pullback((content_cotangent.astype(jnp.float32), query_cotangent.astype(jnp.float32)))
    return (content_final.astype(jnp.bfloat16), query_final.astype(jnp.bfloat16), grads[0], grads[1], grads[2], grads[3], grads[4], grads[5], grads[6], grads[7], grads[8], grads[9], grads[10], grads[11], grads[12], grads[13], grads[14], grads[15], grads[16], grads[17])
```

```python
import functools

import jax
import jax.numpy as jnp
from jax import lax
from jax.experimental import pallas as pl
from jax.experimental.pallas import tpu as pltpu
from jax.sharding import PartitionSpec as P

BF16 = jnp.bfloat16
F32 = jnp.float32
FAR_EDGES = (12, 16, 23, 32, 46, 64, 91)
NEGATIVE = -1e30
TILE = 256
ROWS = 640
GROUP = 16


def layer_norm(hidden_rows, gain_row, shift_row):
    average = jnp.mean(hidden_rows, axis=-1, keepdims=True)
    centered = hidden_rows - average
    variance = jnp.mean(centered * centered, axis=-1, keepdims=True)
    return centered * lax.rsqrt(variance + 1e-05) * gain_row + shift_row


def norm_of_sum(residual, branch_value, gain_row, shift_row):
    return layer_norm(residual + branch_value, gain_row, shift_row)


def gelu_exact(values):
    return jax.nn.gelu(values, approximate=False)


def dot(left, right):
    return jnp.dot(left, right, preferred_element_type=F32)


def contract_rows(left, right):
    return lax.dot_general(left, right, (((0,), (0,)), ((), ())), preferred_element_type=F32)


def times_transpose(left, right):
    return lax.dot_general(left, right, (((1,), (1,)), ((), ())), preferred_element_type=F32)


def transpose_low(block):
    return block.astype(F32).T.astype(BF16)


def tile_branches(tile_index, tiles, process):
    per_branch = tiles // 4
    for branch in range(4):
        pl.when(tile_index // per_branch == branch)(functools.partial(process, 128 * branch))


def forward_kernel(
    tiles,
    heads,
    seq_length,
    query_ref,
    kv_ref,
    anchor_ref,
    row_ref,
    table_ref,
    exp_ref,
    bucket_ref,
    low_ref,
    max_ref,
    mixed_ref,
    mixed_t_ref,
    total_ref,
    query_z,
    prob_ref,
    run_max,
    run_sum,
    scale_ref,
):
    tile_index = pl.program_id(0)
    half_tiles = tiles // 2
    part_tiles = half_tiles // 4

    @pl.when(tile_index == 0)
    def _():
        query_t = transpose_low(query_ref[...])
        part = lax.broadcasted_iota(jnp.int32, (256, ROWS), 0) // 64
        for head in range(heads):
            query_z[head] = jnp.where(part == head, query_t.astype(F32), 0.0).astype(BF16)
        run_max[...] = jnp.full(run_max.shape, NEGATIVE, F32)
        run_sum[...] = jnp.zeros(run_sum.shape, F32)
        mixed_t_ref[...] = jnp.zeros(mixed_t_ref.shape, F32)

    mirror = tile_index - half_tiles
    mirror_base = seq_length - 1 - TILE * (
        (3 - mirror // part_tiles) * part_tiles + mirror % part_tiles
    )
    place_base = jnp.where(tile_index < half_tiles, tile_index * TILE, mirror_base)
    place_sign = jnp.where(tile_index < half_tiles, 1, -1)
    value_t = transpose_low(kv_ref[:, 128:384])

    def process(offset):
        chunks = (ROWS - offset) // 128
        for head in range(heads):
            exp_ref[head, :, offset:] = dot(kv_ref[:, 0:256], query_z[head, :, offset:])

        def bias_group(group, tops):
            start = pl.multiple_of(group * GROUP, GROUP)
            keys = anchor_ref[pl.ds(start, GROUP), :]
            index = start + lax.broadcasted_iota(jnp.int32, (GROUP, 128), 0)
            place = place_base + place_sign * index
            new_tops = []
            for chunk in range(chunks):
                lanes = slice(offset + chunk * 128, offset + chunk * 128 + 128)
                relative = keys - row_ref[0:1, lanes]
                magnitude = jnp.abs(relative)
                bucket = jnp.minimum(magnitude, 8)
                for edge in FAR_EDGES:
                    bucket = bucket + jnp.where(magnitude >= edge, 1, 0)
                bucket = bucket + jnp.where(relative > 0, 16, 0)
                bucket_ref[pl.ds(start, GROUP), lanes] = bucket.astype(F32).astype(BF16)
                low_ref[pl.ds(start, GROUP), lanes] = (bucket & 3).astype(F32).astype(BF16)
                allowed = place < row_ref[1:2, lanes]
                for head in range(heads):
                    table = jnp.broadcast_to(table_ref[head : head + 1, :], (8, 128))
                    bias = jnp.concatenate(
                        [
                            jnp.take_along_axis(table, bucket[0:8], axis=1),
                            jnp.take_along_axis(table, bucket[8:16], axis=1),
                        ],
                        axis=0,
                    )
                    scores = exp_ref[head, pl.ds(start, GROUP), lanes] + bias
                    scores = jnp.where(allowed, scores, NEGATIVE)
                    exp_ref[head, pl.ds(start, GROUP), lanes] = scores
                    top = tops[chunk * heads + head]
                    new_tops.append(jnp.maximum(top, jnp.maximum(scores[0:8], scores[8:16])))
            return tuple(new_tops)

        tops = lax.fori_loop(
            0,
            TILE // GROUP,
            bias_group,
            tuple(jnp.full((8, 128), NEGATIVE, F32) for _ in range(chunks * heads)),
        )
        for chunk in range(chunks):
            lanes = slice(offset + chunk * 128, offset + chunk * 128 + 128)
            for head in range(heads):
                top = jnp.max(tops[chunk * heads + head], axis=0, keepdims=True)
                old = run_max[head : head + 1, lanes]
                new = jnp.maximum(old, top)
                scale_ref[head : head + 1, lanes] = jnp.exp(old - new)
                run_max[head : head + 1, lanes] = new
        max_ref[0] = run_max[...]

        def exp_group(group, sums):
            start = pl.multiple_of(group * GROUP, GROUP)
            new_sums = []
            for chunk in range(chunks):
                lanes = slice(offset + chunk * 128, offset + chunk * 128 + 128)
                for head in range(heads):
                    terms = jnp.exp(
                        exp_ref[head, pl.ds(start, GROUP), lanes] - run_max[head : head + 1, lanes]
                    )
                    exp_ref[head, pl.ds(start, GROUP), lanes] = terms
                    prob_ref[head, pl.ds(start, GROUP), lanes] = terms.astype(BF16)
                    new_sums.append(sums[chunk * heads + head] + (terms[0:8] + terms[8:16]))
            return tuple(new_sums)

        sums = lax.fori_loop(
            0,
            TILE // GROUP,
            exp_group,
            tuple(jnp.zeros((8, 128), F32) for _ in range(chunks * heads)),
        )
        for chunk in range(chunks):
            lanes = slice(offset + chunk * 128, offset + chunk * 128 + 128)
            for head in range(heads):
                run_sum[head : head + 1, lanes] = run_sum[head : head + 1, lanes] * scale_ref[
                    head : head + 1, lanes
                ] + jnp.sum(sums[chunk * heads + head], axis=0, keepdims=True)
        for head in range(heads):
            rows = slice(64 * head, 64 * head + 64)
            mixed_t_ref[rows, offset:] = mixed_t_ref[rows, offset:] * scale_ref[
                head : head + 1, offset:
            ] + dot(value_t[64 + 64 * head : 128 + 64 * head], prob_ref[head, :, offset:])

    tile_branches(tile_index, tiles, process)

    @pl.when(tile_index == tiles - 1)
    def _():
        for head in range(heads):
            rows = slice(64 * head, 64 * head + 64)
            mixed_t_ref[rows, :] = mixed_t_ref[rows, :] / run_sum[head : head + 1, :]
            total_ref[head : head + 1, :] = run_max[head : head + 1, :] + jnp.log(
                run_sum[head : head + 1, :]
            )
        mixed_ref[...] = mixed_t_ref[...].T.astype(BF16)


def attention_forward(query256, keys_values, key_anchor, row_info, tables, heads, seq_length):
    total_keys = keys_values.shape[0]
    tiles = total_keys // TILE
    return pl.pallas_call(
        functools.partial(forward_kernel, tiles, heads, seq_length),
        grid=(tiles,),
        in_specs=[
            pl.BlockSpec((ROWS, 256), lambda t: (0, 0)),
            pl.BlockSpec((TILE, 384), lambda t: (t, 0)),
            pl.BlockSpec((TILE, 128), lambda t: (t, 0)),
            pl.BlockSpec((8, ROWS), lambda t: (0, 0)),
            pl.BlockSpec((8, 128), lambda t: (0, 0)),
        ],
        out_specs=[
            pl.BlockSpec((heads, TILE, ROWS), lambda t: (0, t, 0)),
            pl.BlockSpec((TILE, ROWS), lambda t: (t, 0)),
            pl.BlockSpec((TILE, ROWS), lambda t: (t, 0)),
            pl.BlockSpec((1, 8, ROWS), lambda t: (t, 0, 0)),
            pl.BlockSpec((ROWS, 192), lambda t: (0, 0)),
            pl.BlockSpec((192, ROWS), lambda t: (0, 0)),
            pl.BlockSpec((8, ROWS), lambda t: (0, 0)),
        ],
        out_shape=[
            jax.ShapeDtypeStruct((heads, total_keys, ROWS), F32),
            jax.ShapeDtypeStruct((total_keys, ROWS), BF16),
            jax.ShapeDtypeStruct((total_keys, ROWS), BF16),
            jax.ShapeDtypeStruct((tiles, 8, ROWS), F32),
            jax.ShapeDtypeStruct((ROWS, 192), BF16),
            jax.ShapeDtypeStruct((192, ROWS), F32),
            jax.ShapeDtypeStruct((8, ROWS), F32),
        ],
        scratch_shapes=[
            pltpu.VMEM((heads, 256, ROWS), BF16),
            pltpu.VMEM((heads, TILE, ROWS), BF16),
            pltpu.VMEM((8, ROWS), F32),
            pltpu.VMEM((8, ROWS), F32),
            pltpu.VMEM((8, ROWS), F32),
        ],
        compiler_params=pltpu.CompilerParams(
            dimension_semantics=("arbitrary",), vmem_limit_bytes=32 << 20
        ),
        cost_estimate=pl.CostEstimate(
            flops=20 << 30, bytes_accessed=24 << 20, transcendentals=4 << 20
        ),
        name="attention_forward",
    )(query256, keys_values, key_anchor, row_info, tables)


def backward_kernel(
    tiles,
    heads,
    exp_ref,
    bucket_ref,
    low_ref,
    max_ref,
    total_ref,
    query_ref,
    grad_ref,
    mixed_t_ref,
    kv_ref,
    dkv_ref,
    dquery_ref,
    dtable_ref,
    grad_z,
    query_n,
    grad_n,
    dprob_ref,
    dscore_ref,
    prob_ref,
    high_hot,
    low_parts,
    delta_ref,
    scale_ref,
    dquery_t,
):
    tile_index = pl.program_id(0)

    @pl.when(tile_index == 0)
    def _():
        grad_t = grad_ref[...].astype(F32).T
        part = lax.broadcasted_iota(jnp.int32, (256, ROWS), 0) // 64
        lane_part = lax.broadcasted_iota(jnp.int32, (ROWS, 256), 1) // 64
        for head in range(heads):
            grad_z[head] = jnp.where(part == head + 1, grad_t, 0.0).astype(BF16)
            query_n[head] = jnp.where(lane_part == head, query_ref[...].astype(F32), 0.0).astype(BF16)
            grad_n[head] = jnp.where(lane_part == head + 1, grad_ref[...].astype(F32), 0.0).astype(
                BF16
            )
            delta_ref[head : head + 1, :] = jnp.sum(
                grad_t[64 + 64 * head : 128 + 64 * head] * mixed_t_ref[64 * head : 64 * head + 64],
                axis=0,
                keepdims=True,
            )
        dquery_t[...] = jnp.zeros(dquery_t.shape, F32)
        dtable_ref[...] = jnp.zeros(dtable_ref.shape, F32)

    key_t = transpose_low(kv_ref[:, 0:256])

    def process(offset):
        chunks = (ROWS - offset) // 128
        for head in range(heads):
            dprob_ref[head, :, offset:] = dot(kv_ref[:, 128:384], grad_z[head, :, offset:])
            scale_ref[head : head + 1, offset:] = jnp.exp(
                max_ref[0, head : head + 1, offset:] - total_ref[head : head + 1, offset:]
            )

        def score_group(group, carry):
            start = pl.multiple_of(group * GROUP, GROUP)
            for chunk in range(chunks):
                lanes = slice(offset + chunk * 128, offset + chunk * 128 + 128)
                bucket = bucket_ref[pl.ds(start, GROUP), lanes]
                low = low_ref[pl.ds(start, GROUP), lanes]
                one = jnp.ones((GROUP, 128), BF16)
                zero = jnp.zeros((GROUP, 128), BF16)
                for high in range(8):
                    hot = jnp.where(bucket >= jnp.asarray(4 * high, BF16), one, zero)
                    high_hot[group, GROUP * high : GROUP * high + GROUP, lanes] = hot
                matches = [low == jnp.asarray(value, BF16) for value in range(4)]
                for head in range(heads):
                    prob = (
                        exp_ref[head, pl.ds(start, GROUP), lanes]
                        * scale_ref[head : head + 1, lanes]
                    )
                    dscore = prob * (
                        dprob_ref[head, pl.ds(start, GROUP), lanes]
                        - delta_ref[head : head + 1, lanes]
                    )
                    dscore_low = dscore.astype(BF16)
                    prob_ref[head, pl.ds(start, GROUP), lanes] = prob.astype(BF16)
                    dscore_ref[head, pl.ds(start, GROUP), lanes] = dscore_low
                    for value in range(4):
                        row = GROUP * (value * heads + head)
                        low_parts[group, row : row + GROUP, lanes] = jnp.where(
                            matches[value], dscore_low, zero
                        )
            return carry

        lax.fori_loop(0, TILE // GROUP, score_group, 0)
        table_sum = dtable_ref[...]
        for group in range(TILE // GROUP):
            table_sum = table_sum + times_transpose(
                high_hot[group, :, offset:], low_parts[group, :, offset:]
            )
        dtable_ref[...] = table_sum
        dkey = jnp.zeros((TILE, 256), F32)
        dvalue = jnp.zeros((TILE, 256), F32)
        for head in range(heads):
            dkey = dkey + dot(dscore_ref[head, :, offset:], query_n[head, offset:, :])
            dvalue = dvalue + dot(prob_ref[head, :, offset:], grad_n[head, offset:, :])
            rows = slice(64 * head, 64 * head + 64)
            dquery_t[rows, offset:] = dquery_t[rows, offset:] + dot(
                key_t[rows], dscore_ref[head, :, offset:]
            )
        dkv_ref[:, 0:128] = dkey[:, 0:128]
        dkv_ref[:, 128:256] = dkey[:, 128:256] + dvalue[:, 0:128]
        dkv_ref[:, 256:384] = dvalue[:, 128:256]

    tile_branches(tile_index, tiles, process)

    @pl.when(tile_index == tiles - 1)
    def _():
        dquery_ref[...] = dquery_t[...].T.astype(BF16)


def attention_backward(
    exps, buckets, lows, maxima, totals, query256, grad256, mixed_t, keys_values, heads
):
    total_keys = keys_values.shape[0]
    tiles = total_keys // TILE
    groups = TILE // GROUP
    return pl.pallas_call(
        functools.partial(backward_kernel, tiles, heads),
        grid=(tiles,),
        in_specs=[
            pl.BlockSpec((heads, TILE, ROWS), lambda t: (0, t, 0)),
            pl.BlockSpec((TILE, ROWS), lambda t: (t, 0)),
            pl.BlockSpec((TILE, ROWS), lambda t: (t, 0)),
            pl.BlockSpec((1, 8, ROWS), lambda t: (t, 0, 0)),
            pl.BlockSpec((8, ROWS), lambda t: (0, 0)),
            pl.BlockSpec((ROWS, 256), lambda t: (0, 0)),
            pl.BlockSpec((ROWS, 256), lambda t: (0, 0)),
            pl.BlockSpec((192, ROWS), lambda t: (0, 0)),
            pl.BlockSpec((TILE, 384), lambda t: (t, 0)),
        ],
        out_specs=[
            pl.BlockSpec((TILE, 384), lambda t: (t, 0)),
            pl.BlockSpec((ROWS, 192), lambda t: (0, 0)),
            pl.BlockSpec((128, 64 * heads), lambda t: (0, 0)),
        ],
        out_shape=[
            jax.ShapeDtypeStruct((total_keys, 384), F32),
            jax.ShapeDtypeStruct((ROWS, 192), BF16),
            jax.ShapeDtypeStruct((128, 64 * heads), F32),
        ],
        scratch_shapes=[
            pltpu.VMEM((heads, 256, ROWS), BF16),
            pltpu.VMEM((heads, ROWS, 256), BF16),
            pltpu.VMEM((heads, ROWS, 256), BF16),
            pltpu.VMEM((heads, TILE, ROWS), F32),
            pltpu.VMEM((heads, TILE, ROWS), BF16),
            pltpu.VMEM((heads, TILE, ROWS), BF16),
            pltpu.VMEM((groups, 128, ROWS), BF16),
            pltpu.VMEM((groups, 64 * heads, ROWS), BF16),
            pltpu.VMEM((8, ROWS), F32),
            pltpu.VMEM((8, ROWS), F32),
            pltpu.VMEM((192, ROWS), F32),
        ],
        compiler_params=pltpu.CompilerParams(
            dimension_semantics=("arbitrary",), vmem_limit_bytes=40 << 20
        ),
        cost_estimate=pl.CostEstimate(
            flops=30 << 30, bytes_accessed=24 << 20, transcendentals=1 << 20
        ),
        name="attention_backward",
    )(exps, buckets, lows, maxima, totals, query256, grad256, mixed_t, keys_values)


def body(
    content,
    query_stream,
    token_order,
    targets,
    query_weight,
    key_weight,
    value_weight,
    output_weight,
    query_bias,
    value_bias,
    output_bias,
    bias_table,
    first_gain,
    first_shift,
    inner_weight,
    inner_bias,
    outer_weight,
    outer_bias,
    second_gain,
    second_shift,
    content_cotangent,
    query_cotangent,
):
    ctx = lax.axis_size("ctx")
    index = lax.axis_index("ctx")
    side = lax.axis_index("wt")
    members = ctx // 4
    plane = index // members
    member = index % members
    half_rows = content.shape[2]
    tok_rows = 2 * half_rows
    query_rows = query_stream.shape[1]
    rows_dev = tok_rows + query_rows
    width = content.shape[3]
    heads = bias_table.shape[1]
    my_heads = heads // 4
    head_width = my_heads * (width // heads)
    half_width = width // 2
    seq_length = tok_rows * ctx
    half_length = seq_length // 2
    order_row = token_order[0]
    target_row = targets[0]
    core_bit = (index & 1) == 1

    def swap(value, bit):
        return lax.ppermute(value, "ctx", [(i, i ^ bit) for i in range(ctx)])

    def swap_side(value):
        return lax.ppermute(value, "wt", [(0, 1), (1, 0)])

    def order_two(flag, mine, other, axis):
        low = jnp.where(flag, other, mine)
        high = jnp.where(flag, mine, other)
        return jnp.concatenate([low, high], axis=axis)

    def swap_side_shared(value):
        rows = value.shape[0] // 2
        mine = lax.dynamic_slice_in_dim(value, (index & 1) * rows, rows, 0)
        arrived = swap_side(mine)
        return order_two(core_bit, arrived, swap(arrived, 1), 0)

    def by_distance(blocks):
        flag = (plane & 1) == 1
        blocks = [jnp.where(flag, blocks[d ^ 1], blocks[d]) for d in range(4)]
        flag = (plane & 2) == 2
        return [jnp.where(flag, blocks[d ^ 2], blocks[d]) for d in range(4)]

    def exchange_planes(blocks):
        sent = by_distance(blocks)
        arrived = [sent[0]] + [swap(sent[d], d * members) for d in range(1, 4)]
        return by_distance(arrived)

    def pack_rows(rows):
        top = jnp.concatenate([rows[:half_rows], rows[half_rows:tok_rows]], axis=1)
        bottom = jnp.concatenate([rows[tok_rows:], jnp.zeros_like(rows[tok_rows:])], axis=1)
        return jnp.concatenate([top, bottom], axis=0)

    def unpack_rows(packed):
        return jnp.concatenate(
            [
                packed[:half_rows, :head_width],
                packed[:half_rows, head_width:],
                packed[half_rows:, :head_width],
            ],
            axis=0,
        )

    def plane_rows(blocks):
        pad = ROWS - 4 * rows_dev
        return jnp.concatenate(
            [blocks[d][:half_rows] for d in range(4)]
            + [blocks[3 - d][half_rows:tok_rows] for d in range(4)]
            + [blocks[d][tok_rows:] for d in range(4)]
            + [jnp.zeros((pad, blocks[0].shape[1]), blocks[0].dtype)],
            axis=0,
        )

    def split_rows(rows):
        blocks = []
        for d in range(4):
            parts = [
                rows[d * half_rows : (d + 1) * half_rows],
                rows[(7 - d) * half_rows : (8 - d) * half_rows],
            ]
            if rows.shape[0] > 4 * tok_rows:
                start = 4 * tok_rows + d * query_rows
                parts.append(rows[start : start + query_rows])
            blocks.append(jnp.concatenate(parts, axis=0))
        return blocks

    local_content = content[0].reshape(tok_rows, width)
    stacked = jnp.concatenate([local_content, query_stream[0]], axis=0)
    arrived_rows = [stacked] + [swap(stacked, d * members) for d in range(1, 4)]
    own_qkv = jnp.concatenate([query_weight, key_weight, value_weight], axis=1)
    other_qkv = swap_side_shared(own_qkv)
    vectors = jnp.stack(
        [
            query_bias,
            value_bias,
            output_bias,
            first_gain,
            first_shift,
            outer_bias,
            second_gain,
            second_shift,
        ],
        axis=0,
    )
    table_rows = jnp.pad(bias_table, ((0, 0), (0, half_width - heads)))
    own_vectors = jnp.concatenate([vectors, table_rows], axis=0)
    other_vectors = swap_side(own_vectors)
    side_flag = side == 1
    full_vectors = order_two(side_flag, own_vectors[:8], other_vectors[:8], 1).astype(F32)
    (
        full_query_bias,
        full_value_bias,
        full_output_bias,
        full_first_gain,
        full_first_shift,
        full_outer_bias,
        full_second_gain,
        full_second_shift,
    ) = [full_vectors[i] for i in range(8)]
    full_table = order_two(
        side_flag, own_vectors[8:, :heads], other_vectors[8:, :heads], 0
    ).astype(F32)
    buckets = full_table.shape[0]

    places = jnp.arange(half_length, dtype=jnp.int32)
    key_place = jnp.concatenate(
        [places, (seq_length - 1 - places).reshape(4, -1)[::-1].reshape(-1)]
    )
    key_anchor = jnp.concatenate(
        [
            order_row[:half_length],
            order_row[half_length:][::-1].reshape(4, -1)[::-1].reshape(-1),
        ]
    )

    def of_member(array, count):
        return lax.dynamic_index_in_dim(
            array.reshape(-1, members, count), member, 1, keepdims=False
        ).reshape(-1)

    plane_targets = of_member(target_row, query_rows)
    target_anchor = jnp.sum(
        jnp.where(
            jnp.arange(seq_length, dtype=jnp.int32)[:, None] == plane_targets[None],
            order_row[:, None],
            0,
        ),
        axis=0,
    )
    pad_rows = ROWS - 4 * rows_dev
    row_anchor = jnp.concatenate(
        [of_member(key_anchor, half_rows), target_anchor, jnp.zeros((pad_rows,), jnp.int32)]
    )
    row_limit = jnp.concatenate(
        [
            of_member(key_place, half_rows) + 1,
            plane_targets,
            jnp.ones((pad_rows,), jnp.int32),
        ]
    )
    row_info = jnp.concatenate(
        [row_anchor[None], row_limit[None], jnp.zeros((6, ROWS), jnp.int32)], axis=0
    )
    key_anchor_wide = jnp.broadcast_to(key_anchor[:, None], (seq_length, 128))
    head_start = plane * my_heads
    my_table = lax.dynamic_slice_in_dim(full_table, head_start, my_heads, 1)
    tables = jnp.pad(my_table.T, ((0, 8 - my_heads), (0, 128 - buckets)))

    owner = plane // 2
    odd_plane = (plane & 1) == 1
    qkv_shard = jnp.where(side == owner, own_qkv, other_qkv)
    head_weights = jnp.concatenate(
        [
            jnp.where(
                odd_plane,
                qkv_shard[:, i * half_width + head_width : (i + 1) * half_width],
                qkv_shard[:, i * half_width : i * half_width + head_width],
            )
            for i in range(3)
        ],
        axis=1,
    )
    plane_x = plane_rows(by_distance(arrived_rows))
    projected = dot(plane_x, head_weights)
    my_query_bias = lax.dynamic_slice_in_dim(full_query_bias, plane * head_width, head_width, 0)
    my_value_bias = lax.dynamic_slice_in_dim(full_value_bias, plane * head_width, head_width, 0)
    plane_query = ((projected[:, :head_width] + my_query_bias) * 0.125).astype(BF16)
    query256 = jnp.pad(plane_query, ((0, 0), (0, 256 - head_width)))
    content_part = projected[: 4 * tok_rows, head_width:]
    kv_bias = jnp.concatenate([jnp.zeros_like(my_value_bias), my_value_bias])
    plane_kv = (content_part + kv_bias).astype(BF16)
    gathered = plane_kv.reshape(8, 1, half_rows, 2 * head_width)
    bit = members // 2
    while bit >= 1:
        flag = (member & bit) != 0
        other = swap(gathered, bit)
        gathered = jnp.stack(
            [jnp.where(flag, other, gathered), jnp.where(flag, gathered, other)], axis=2
        ).reshape(8, -1, half_rows, 2 * head_width)
        bit //= 2
    keys_values = gathered.reshape(seq_length, 2 * head_width)

    exps, bucket_ids, bucket_lows, maxima, mixed_plane, mixed_t, totals = attention_forward(
        query256, keys_values, key_anchor_wide, row_info, tables, my_heads, seq_length
    )

    other_output = swap_side_shared(output_weight)
    full_output = order_two(side_flag, output_weight, other_output, 1)
    hidden_half = outer_weight.shape[0] // 2
    outer_sent = lax.dynamic_slice_in_dim(outer_weight, (1 - side) * hidden_half, hidden_half, 0)
    outer_kept = lax.dynamic_slice_in_dim(outer_weight, side * hidden_half, hidden_half, 0)
    outer_rows = order_two(side_flag, outer_kept, swap_side_shared(outer_sent), 1)
    full_qkv = [
        order_two(
            side_flag,
            own_qkv[:, i * half_width : (i + 1) * half_width],
            other_qkv[:, i * half_width : (i + 1) * half_width],
            1,
        )
        for i in range(3)
    ]

    mixed_blocks = exchange_planes([pack_rows(block) for block in split_rows(mixed_plane)])
    mixed = jnp.concatenate([unpack_rows(block) for block in mixed_blocks], axis=1)
    branch = dot(mixed, full_output) + full_output_bias
    first_norm, first_back = jax.vjp(
        norm_of_sum, stacked.astype(F32), branch, full_first_gain, full_first_shift
    )
    first_low = first_norm.astype(BF16)
    both_first = jnp.concatenate([first_low, swap_side(first_low)], axis=0)
    inner_value = dot(both_first, inner_weight) + inner_bias.astype(F32)
    hidden_value, gelu_back = jax.vjp(gelu_exact, inner_value)
    hidden_low = hidden_value.astype(BF16)
    outer_part = dot(hidden_low, outer_rows)
    outer_arrived = swap_side(outer_part[rows_dev:].astype(BF16))
    outer_value = outer_part[:rows_dev] + outer_arrived.astype(F32) + full_outer_bias
    final_norm, second_back = jax.vjp(
        norm_of_sum, first_norm, outer_value, full_second_gain, full_second_shift
    )
    content_result = final_norm[:tok_rows].reshape(1, 2, half_rows, width).astype(BF16)
    query_result = final_norm[tok_rows:].reshape(1, query_rows, width).astype(BF16)
    cotangent = jnp.concatenate(
        [content_cotangent[0].reshape(tok_rows, width), query_cotangent[0]], axis=0
    )
    rest_grad, outer_grad, second_gain_grad, second_shift_grad = second_back(cotangent.astype(F32))
    outer_low = outer_grad.astype(BF16)
    both_outer = jnp.concatenate([outer_low, swap_side(outer_low)], axis=0)
    (inner_grad,) = gelu_back(times_transpose(both_outer, outer_rows))
    inner_low = inner_grad.astype(BF16)
    first_part = times_transpose(inner_low, inner_weight)
    first_arrived = swap_side(first_part[rows_dev:].astype(BF16))
    first_grad = rest_grad + (first_part[:rows_dev] + first_arrived.astype(F32))
    row_grad, branch_grad, first_gain_grad, first_shift_grad = first_back(first_grad)
    branch_low = branch_grad.astype(BF16)
    mixed_low = times_transpose(branch_low, full_output).astype(BF16)

    def scatter_sum(partial):
        current = partial
        bit = 1
        while bit < ctx:
            rows = current.shape[0] // 2
            flag = (index & bit) != 0
            low, high = current[:rows], current[rows:]
            sent = jnp.where(flag, low, high).astype(BF16)
            kept = jnp.where(flag, high, low)
            current = kept + swap(sent, bit).astype(F32)
            bit *= 2
        return current

    def gather_rows(piece, axis):
        current = piece
        bit = ctx // 2
        while bit >= 1:
            flag = (index & bit) != 0
            current = order_two(flag, current, swap(current, bit), axis)
            bit //= 2
        return current

    outer_piece = scatter_sum(contract_rows(hidden_low, both_outer)).astype(BF16)
    piece_left, piece_right = outer_piece[:, :half_width], outer_piece[:, half_width:]
    piece_sent = jnp.where(side_flag, piece_left, piece_right)
    piece_kept = jnp.where(side_flag, piece_right, piece_left)
    piece_both = order_two(side_flag, piece_kept[None], swap_side(piece_sent)[None], 0)
    outer_weight_grad = gather_rows(piece_both, 1).reshape(2 * hidden_half, half_width)

    other_mixed = swap_side(mixed)
    branch_left, branch_right = branch_low[:, :half_width], branch_low[:, half_width:]
    branch_kept = jnp.where(side_flag, branch_right, branch_left)
    branch_arrived = swap_side(jnp.where(side_flag, branch_left, branch_right))
    output_part = contract_rows(mixed, branch_kept) + contract_rows(other_mixed, branch_arrived)
    inner_part = contract_rows(both_first, inner_low)
    joined = jnp.concatenate([inner_part, output_part], axis=1)
    joined_grad = gather_rows(scatter_sum(joined).astype(BF16), 0)
    inner_columns = inner_part.shape[1]
    inner_weight_grad = joined_grad[:, :inner_columns]
    output_weight_grad = joined_grad[:, inner_columns:]

    grad_blocks = exchange_planes(
        [
            pack_rows(mixed_low[:, d * head_width : (d + 1) * head_width])
            for d in range(4)
        ]
    )
    plane_grad = plane_rows([unpack_rows(block) for block in grad_blocks])
    grad256 = jnp.pad(plane_grad, ((0, 0), (256 - head_width, 0)))
    dkv, query_low, table_part = attention_backward(
        exps,
        bucket_ids,
        bucket_lows,
        maxima,
        totals,
        query256,
        grad256,
        mixed_t,
        keys_values,
        my_heads,
    )
    remaining = dkv.reshape(8, members, half_rows, 2 * head_width)
    bit = 1
    while bit < members:
        flag = (member & bit) != 0
        pairs = remaining.reshape(8, -1, 2, half_rows, 2 * head_width)
        sent = jnp.where(flag, pairs[:, :, 0], pairs[:, :, 1]).astype(BF16)
        kept = jnp.where(flag, pairs[:, :, 1], pairs[:, :, 0])
        remaining = kept + swap(sent, bit).astype(F32)
        bit *= 2
    kv_low = remaining.reshape(4 * tok_rows, 2 * head_width).astype(BF16)
    query_scaled = query_low * 0.125

    sent_blocks = [
        jnp.concatenate([pack_rows(query_block), kv_block], axis=0)
        for query_block, kv_block in zip(split_rows(query_scaled), split_rows(kv_low))
    ]
    got_blocks = exchange_planes(sent_blocks)
    packed_rows = half_rows + query_rows
    own_query = jnp.concatenate([unpack_rows(b[:packed_rows]) for b in got_blocks], axis=1)
    own_key = jnp.concatenate([b[packed_rows:, :head_width] for b in got_blocks], axis=1)
    own_value = jnp.concatenate([b[packed_rows:, head_width:] for b in got_blocks], axis=1)
    full_query, full_key, full_value = full_qkv
    input_grad = row_grad + times_transpose(own_query, full_query)
    content_extra = times_transpose(own_key, full_key) + times_transpose(own_value, full_value)
    content_gradient = (input_grad[:tok_rows] + content_extra).reshape(1, 2, half_rows, width)
    query_gradient = input_grad[tok_rows:].reshape(1, query_rows, width)

    qkv_part = jnp.concatenate(
        [
            contract_rows(plane_x, query_scaled),
            contract_rows(plane_x[: 4 * tok_rows], kv_low),
        ],
        axis=1,
    )
    current = qkv_part
    bit = 1
    while bit < members:
        rows = current.shape[0] // 2
        flag = (member & bit) != 0
        low, high = current[:rows], current[rows:]
        sent = jnp.where(flag, low, high).astype(BF16)
        current = jnp.where(flag, high, low) + swap(sent, bit).astype(F32)
        bit *= 2
    current = current + swap_side(current.astype(BF16)).astype(F32)
    current = current.astype(BF16)
    far = swap(current, 2 * members)
    current = jnp.where(owner == side, current, far)
    near = swap(current, members)
    current = order_two(odd_plane, current[None], near[None], 0)
    bit = members // 2
    while bit >= 1:
        flag = (member & bit) != 0
        current = order_two(flag, current, swap(current, bit), 1)
        bit //= 2
    qkv_grads = [
        jnp.concatenate(
            [current[d][:, i * head_width : (i + 1) * head_width] for d in range(2)], axis=1
        ).astype(F32)
        for i in range(3)
    ]

    blocks = table_part.reshape(8, GROUP, 4, my_heads, GROUP)
    same = jnp.eye(GROUP, dtype=F32)[None, :, None, None, :]
    table_cumulative = jnp.sum(blocks * same, axis=(1, 4))
    table_grad = table_cumulative - jnp.concatenate(
        [table_cumulative[1:], jnp.zeros_like(table_cumulative[:1])], axis=0
    )
    table_grad = table_grad.reshape(buckets, my_heads)
    table_wide = lax.dynamic_update_slice_in_dim(
        jnp.zeros((buckets, heads), F32), table_grad, head_start, 1
    )

    def at_plane(values):
        return lax.dynamic_update_slice_in_dim(
            jnp.zeros((width,), F32), values, plane * head_width, 0
        )

    inner_bias_wide = lax.dynamic_update_slice_in_dim(
        jnp.zeros((2 * hidden_half,), F32),
        jnp.sum(inner_low.astype(F32), axis=0),
        side * hidden_half,
        0,
    )
    small = jnp.concatenate(
        [
            at_plane(jnp.sum(query_scaled.astype(F32), axis=0)),
            at_plane(jnp.sum(kv_low[:, head_width:].astype(F32), axis=0)),
            jnp.sum(branch_low.astype(F32), axis=0),
            first_gain_grad,
            first_shift_grad,
            jnp.sum(outer_low.astype(F32), axis=0),
            second_gain_grad,
            second_shift_grad,
            inner_bias_wide,
            table_wide.reshape(-1),
        ]
    )
    small_length = small.shape[0]
    small = jnp.pad(small, (0, -small_length % 1024)).reshape(-1, 128)
    bit = 1
    while bit < ctx:
        small = small + swap(small, bit)
        bit *= 2
    small = (small + swap_side(small)).reshape(-1)[:small_length]
    halves = small[: 8 * width].reshape(8, 2, half_width)
    mine = lax.dynamic_index_in_dim(halves, side, 1, keepdims=False)
    inner_bias_grad = lax.dynamic_slice_in_dim(
        small, 8 * width + side * hidden_half, hidden_half, 0
    )
    table_all = small[8 * width + 2 * hidden_half :].reshape(2, buckets // 2, heads)
    bias_table_grad = lax.dynamic_index_in_dim(table_all, side, 0, keepdims=False)

    return (
        content_result,
        query_result,
        content_gradient,
        query_gradient,
        qkv_grads[0],
        qkv_grads[1],
        qkv_grads[2],
        output_weight_grad.astype(F32),
        mine[0],
        mine[1],
        mine[2],
        bias_table_grad,
        mine[3],
        mine[4],
        inner_weight_grad.astype(F32),
        inner_bias_grad,
        outer_weight_grad.astype(F32),
        mine[5],
        mine[6],
        mine[7],
    )


def solution(mesh):
    return jax.shard_map(
        body,
        mesh=mesh,
        in_specs=(
            P("wt", None, "ctx", None),
            P("wt", "ctx", None),
            P("wt", None),
            P("wt", None),
            P(None, "wt"),
            P(None, "wt"),
            P(None, "wt"),
            P(None, "wt"),
            P("wt"),
            P("wt"),
            P("wt"),
            P("wt", None),
            P("wt"),
            P("wt"),
            P(None, "wt"),
            P("wt"),
            P(None, "wt"),
            P("wt"),
            P("wt"),
            P("wt"),
            P("wt", None, "ctx", None),
            P("wt", "ctx", None),
        ),
        out_specs=(
            P("wt", None, "ctx", None),
            P("wt", "ctx", None),
            P("wt", None, "ctx", None),
            P("wt", "ctx", None),
            P(None, "wt"),
            P(None, "wt"),
            P(None, "wt"),
            P(None, "wt"),
            P("wt"),
            P("wt"),
            P("wt"),
            P("wt", None),
            P("wt"),
            P("wt"),
            P(None, "wt"),
            P("wt"),
            P(None, "wt"),
            P("wt"),
            P("wt"),
            P("wt"),
        ),
        check_vma=False,
    )
```

```python
import functools

import jax
import jax.numpy as jnp
from jax import lax
from jax.experimental import pallas as pl
from jax.experimental.layout import Layout, with_layout_constraint
from jax.experimental.pallas import tpu as pltpu
from jax.sharding import PartitionSpec as P

BF16 = jnp.bfloat16
F32 = jnp.float32
FAR_EDGES = (12, 16, 23, 32, 46, 64, 91)
NEGATIVE = -1e30
TILE = 256
ROWS = 640
GROUP = 16


def layer_norm(hidden_rows, gain_row, shift_row):
    average = jnp.mean(hidden_rows, axis=-1, keepdims=True)
    centered = hidden_rows - average
    variance = jnp.mean(centered * centered, axis=-1, keepdims=True)
    return centered * lax.rsqrt(variance + 1e-05) * gain_row + shift_row


def norm_of_sum(residual, branch_value, gain_row, shift_row):
    return layer_norm(residual + branch_value, gain_row, shift_row)


def gelu_exact(values):
    return jax.nn.gelu(values, approximate=False)


def dot(left, right):
    return jnp.dot(left, right, preferred_element_type=F32)


def contract_rows(left, right):
    return lax.dot_general(left, right, (((0,), (0,)), ((), ())), preferred_element_type=F32)


def times_transpose(left, right):
    return lax.dot_general(left, right, (((1,), (1,)), ((), ())), preferred_element_type=F32)


def transpose_low(block):
    return block.astype(F32).T.astype(BF16)


def tile_branches(branch_index, process):
    for branch in range(4):
        pl.when(branch_index == branch)(functools.partial(process, 128 * branch))


def forward_kernel(call, count, heads, *refs):
    place_ref, query_ref, kv_ref, anchor_ref, row_ref, table_ref = refs[:6]
    refs = refs[6:]
    if call == 1:
        max_in, sum_in, mixed_in = refs[4:7]
        refs = refs[7:]
    exp_ref, bucket_ref, low_ref, max_ref, run_max, run_sum, mixed_t_ref = refs[:7]
    refs = refs[7:]
    if call == 1:
        mixed_ref, total_ref = refs[:2]
        refs = refs[2:]
    query_z, prob_ref, scale_ref = refs
    step = pl.program_id(0)
    branch_index = step // count
    tile_index = branch_index * (2 * count) + call * count + step % count

    @pl.when(step == 0)
    def _():
        query_t = transpose_low(query_ref[...])
        part = lax.broadcasted_iota(jnp.int32, (256, ROWS), 0) // 64
        for head in range(heads):
            query_z[head] = jnp.where(part == head, query_t.astype(F32), 0.0).astype(BF16)
        if call == 0:
            run_max[...] = jnp.full(run_max.shape, NEGATIVE, F32)
            run_sum[...] = jnp.zeros(run_sum.shape, F32)
            mixed_t_ref[...] = jnp.zeros(mixed_t_ref.shape, F32)
        else:
            run_max[...] = max_in[...]
            run_sum[...] = sum_in[...]
            mixed_t_ref[...] = mixed_in[...]

    place_sign = jnp.where(branch_index < 2, 1, -1)
    keys_values = kv_ref[...].reshape(TILE, 384)
    value_t = transpose_low(keys_values[:, 128:384])

    def process(offset):
        chunks = (ROWS - offset) // 128
        for head in range(heads):
            exp_ref[head, :, offset:] = dot(keys_values[:, 0:256], query_z[head, :, offset:])

        def bias_group(group, tops):
            start = pl.multiple_of(group * GROUP, GROUP)
            keys = anchor_ref[pl.ds(start, GROUP), :]
            row = start % 64 + lax.broadcasted_iota(jnp.int32, (GROUP, 128), 0)
            place = place_ref[tile_index * (TILE // 64) + start // 64] + place_sign * row
            new_tops = []
            for chunk in range(chunks):
                lanes = slice(offset + chunk * 128, offset + chunk * 128 + 128)
                relative = keys - row_ref[0:1, lanes]
                magnitude = jnp.abs(relative)
                bucket = jnp.minimum(magnitude, 8)
                for edge in FAR_EDGES:
                    bucket = bucket + jnp.where(magnitude >= edge, 1, 0)
                bucket = bucket + jnp.where(relative > 0, 16, 0)
                bucket_ref[pl.ds(start, GROUP), lanes] = bucket.astype(F32).astype(BF16)
                low_ref[pl.ds(start, GROUP), lanes] = (bucket & 3).astype(F32).astype(BF16)
                allowed = place < row_ref[1:2, lanes]
                for head in range(heads):
                    table = jnp.broadcast_to(table_ref[head : head + 1, :], (8, 128))
                    bias = jnp.concatenate(
                        [
                            jnp.take_along_axis(table, bucket[0:8], axis=1),
                            jnp.take_along_axis(table, bucket[8:16], axis=1),
                        ],
                        axis=0,
                    )
                    scores = exp_ref[head, pl.ds(start, GROUP), lanes] + bias
                    scores = jnp.where(allowed, scores, NEGATIVE)
                    exp_ref[head, pl.ds(start, GROUP), lanes] = scores
                    top = tops[chunk * heads + head]
                    new_tops.append(jnp.maximum(top, jnp.maximum(scores[0:8], scores[8:16])))
            return tuple(new_tops)

        tops = lax.fori_loop(
            0,
            TILE // GROUP,
            bias_group,
            tuple(jnp.full((8, 128), NEGATIVE, F32) for _ in range(chunks * heads)),
        )
        for chunk in range(chunks):
            lanes = slice(offset + chunk * 128, offset + chunk * 128 + 128)
            for head in range(heads):
                top = jnp.max(tops[chunk * heads + head], axis=0, keepdims=True)
                old = run_max[head : head + 1, lanes]
                new = jnp.maximum(old, top)
                scale_ref[head : head + 1, lanes] = jnp.exp(old - new)
                run_max[head : head + 1, lanes] = new
        max_ref[0] = run_max[...]

        def exp_group(group, sums):
            start = pl.multiple_of(group * GROUP, GROUP)
            new_sums = []
            for chunk in range(chunks):
                lanes = slice(offset + chunk * 128, offset + chunk * 128 + 128)
                for head in range(heads):
                    terms = jnp.exp(
                        exp_ref[head, pl.ds(start, GROUP), lanes] - run_max[head : head + 1, lanes]
                    )
                    exp_ref[head, pl.ds(start, GROUP), lanes] = terms
                    prob_ref[head, pl.ds(start, GROUP), lanes] = terms.astype(BF16)
                    new_sums.append(sums[chunk * heads + head] + (terms[0:8] + terms[8:16]))
            return tuple(new_sums)

        sums = lax.fori_loop(
            0,
            TILE // GROUP,
            exp_group,
            tuple(jnp.zeros((8, 128), F32) for _ in range(chunks * heads)),
        )
        for chunk in range(chunks):
            lanes = slice(offset + chunk * 128, offset + chunk * 128 + 128)
            for head in range(heads):
                run_sum[head : head + 1, lanes] = run_sum[head : head + 1, lanes] * scale_ref[
                    head : head + 1, lanes
                ] + jnp.sum(sums[chunk * heads + head], axis=0, keepdims=True)
        for head in range(heads):
            rows = slice(64 * head, 64 * head + 64)
            mixed_t_ref[rows, offset:] = mixed_t_ref[rows, offset:] * scale_ref[
                head : head + 1, offset:
            ] + dot(value_t[64 + 64 * head : 128 + 64 * head], prob_ref[head, :, offset:])

    tile_branches(branch_index, process)

    if call == 1:

        @pl.when(step == 4 * count - 1)
        def _():
            for head in range(heads):
                rows = slice(64 * head, 64 * head + 64)
                mixed_t_ref[rows, :] = mixed_t_ref[rows, :] / run_sum[head : head + 1, :]
                total_ref[head : head + 1, :] = run_max[head : head + 1, :] + jnp.log(
                    run_sum[head : head + 1, :]
                )
            mixed_ref[...] = mixed_t_ref[...].T.astype(BF16)


def attention_forward(
    call, query256, keys_values, key_anchor, block_places, row_info, tables, previous, heads
):
    count = keys_values.shape[0] // 2
    tiles = 8 * count
    total_keys = tiles * TILE

    def tile_of(s):
        return (s // count) * (2 * count) + call * count + s % count

    def whole(shape):
        return pl.BlockSpec(shape, lambda s, p: (0,) * len(shape))

    in_specs = [
        whole((ROWS, 256)),
        pl.BlockSpec((2, 2, 64, 384), lambda s, p: (s % count, s // count, 0, 0)),
        pl.BlockSpec((TILE, 128), lambda s, p: (tile_of(s), 0)),
        whole((8, ROWS)),
        whole((8, 128)),
    ]
    out_specs = [
        pl.BlockSpec((heads, TILE, ROWS), lambda s, p: (0, tile_of(s), 0)),
        pl.BlockSpec((TILE, ROWS), lambda s, p: (tile_of(s), 0)),
        pl.BlockSpec((TILE, ROWS), lambda s, p: (tile_of(s), 0)),
        pl.BlockSpec((1, 8, ROWS), lambda s, p: (tile_of(s), 0, 0)),
        whole((8, ROWS)),
        whole((8, ROWS)),
        whole((192, ROWS)),
    ]
    out_shape = [
        jax.ShapeDtypeStruct((heads, total_keys, ROWS), F32),
        jax.ShapeDtypeStruct((total_keys, ROWS), BF16),
        jax.ShapeDtypeStruct((total_keys, ROWS), BF16),
        jax.ShapeDtypeStruct((tiles, 8, ROWS), F32),
        jax.ShapeDtypeStruct((8, ROWS), F32),
        jax.ShapeDtypeStruct((8, ROWS), F32),
        jax.ShapeDtypeStruct((192, ROWS), F32),
    ]
    aliases = {}
    if call == 1:
        in_specs += [pl.BlockSpec(memory_space=pl.ANY)] * 4
        in_specs += [whole((8, ROWS)), whole((8, ROWS)), whole((192, ROWS))]
        out_specs += [whole((ROWS, 192)), whole((8, ROWS))]
        out_shape += [
            jax.ShapeDtypeStruct((ROWS, 192), BF16),
            jax.ShapeDtypeStruct((8, ROWS), F32),
        ]
        aliases = {6: 0, 7: 1, 8: 2, 9: 3}
    return pl.pallas_call(
        functools.partial(forward_kernel, call, count, heads),
        grid_spec=pltpu.PrefetchScalarGridSpec(
            num_scalar_prefetch=1,
            grid=(4 * count,),
            in_specs=in_specs,
            out_specs=out_specs,
            scratch_shapes=[
                pltpu.VMEM((heads, 256, ROWS), BF16),
                pltpu.VMEM((heads, TILE, ROWS), BF16),
                pltpu.VMEM((8, ROWS), F32),
            ],
        ),
        out_shape=out_shape,
        input_output_aliases=aliases,
        compiler_params=pltpu.CompilerParams(
            dimension_semantics=("arbitrary",), vmem_limit_bytes=32 << 20
        ),
        cost_estimate=pl.CostEstimate(
            flops=14 << 30, bytes_accessed=12 << 20, transcendentals=2 << 20
        ),
        name="attention_forward",
    )(block_places, query256, keys_values, key_anchor, row_info, tables, *previous)


def backward_kernel(branch, heads, *refs):
    refs = list(refs)
    if branch > 0:
        del refs[11]
    backward_tile(branch, heads, *refs)


def backward_tile(
    branch,
    heads,
    exp_ref,
    bucket_ref,
    low_ref,
    max_ref,
    total_ref,
    query_ref,
    grad_ref,
    mixed_t_ref,
    kv_ref,
    dquery_in,
    dtable_in,
    dquery_ref,
    dtable_ref,
    dkv_ref,
    grad_z,
    query_n,
    grad_n,
    dprob_ref,
    dscore_ref,
    prob_ref,
    high_hot,
    low_parts,
    delta_ref,
    scale_ref,
):
    tile_index = pl.program_id(0)
    offset = 128 * branch
    chunks = (ROWS - offset) // 128

    @pl.when(tile_index == 0)
    def _():
        grad_t = grad_ref[offset:, :].astype(F32).T
        part = lax.broadcasted_iota(jnp.int32, (256, ROWS - offset), 0) // 64
        lane_part = lax.broadcasted_iota(jnp.int32, (ROWS - offset, 256), 1) // 64
        for head in range(heads):
            grad_z[head, :, offset:] = jnp.where(part == head + 1, grad_t, 0.0).astype(BF16)
            query_n[head, offset:, :] = jnp.where(
                lane_part == head, query_ref[offset:, :].astype(F32), 0.0
            ).astype(BF16)
            grad_n[head, offset:, :] = jnp.where(
                lane_part == head + 1, grad_ref[offset:, :].astype(F32), 0.0
            ).astype(BF16)
            delta_ref[head : head + 1, offset:] = jnp.sum(
                grad_t[64 + 64 * head : 128 + 64 * head]
                * mixed_t_ref[64 * head : 64 * head + 64, offset:],
                axis=0,
                keepdims=True,
            )
        if branch == 0:
            dquery_ref[...] = jnp.zeros(dquery_ref.shape, F32)
            dtable_ref[...] = jnp.zeros(dtable_ref.shape, F32)
        else:
            dquery_ref[...] = dquery_in[...]
            dtable_ref[...] = dtable_in[...]

    keys_values = kv_ref[...].reshape(TILE, 384)
    key_t = transpose_low(keys_values[:, 0:256])
    for head in range(heads):
        dprob_ref[head, :, offset:] = dot(keys_values[:, 128:384], grad_z[head, :, offset:])
        scale_ref[head : head + 1, offset:] = jnp.exp(
            max_ref[0, head : head + 1, offset:] - total_ref[head : head + 1, offset:]
        )

    def score_group(group, carry):
        start = pl.multiple_of(group * GROUP, GROUP)
        for chunk in range(chunks):
            lanes = slice(offset + chunk * 128, offset + chunk * 128 + 128)
            bucket = bucket_ref[pl.ds(start, GROUP), lanes]
            low = low_ref[pl.ds(start, GROUP), lanes]
            one = jnp.ones((GROUP, 128), BF16)
            zero = jnp.zeros((GROUP, 128), BF16)
            for high in range(8):
                hot = jnp.where(bucket >= jnp.asarray(4 * high, BF16), one, zero)
                high_hot[group, GROUP * high : GROUP * high + GROUP, lanes] = hot
            matches = [low == jnp.asarray(value, BF16) for value in range(4)]
            for head in range(heads):
                prob = (
                    exp_ref[head, pl.ds(start, GROUP), lanes] * scale_ref[head : head + 1, lanes]
                )
                dscore = prob * (
                    dprob_ref[head, pl.ds(start, GROUP), lanes]
                    - delta_ref[head : head + 1, lanes]
                )
                dscore_low = dscore.astype(BF16)
                prob_ref[head, pl.ds(start, GROUP), lanes] = prob.astype(BF16)
                dscore_ref[head, pl.ds(start, GROUP), lanes] = dscore_low
                for value in range(4):
                    row = GROUP * (value * heads + head)
                    low_parts[group, row : row + GROUP, lanes] = jnp.where(
                        matches[value], dscore_low, zero
                    )
        return carry

    lax.fori_loop(0, TILE // GROUP, score_group, 0)
    table_sum = dtable_ref[...]
    for group in range(TILE // GROUP):
        table_sum = table_sum + times_transpose(
            high_hot[group, :, offset:], low_parts[group, :, offset:]
        )
    dtable_ref[...] = table_sum
    dkey = jnp.zeros((TILE, 256), F32)
    dvalue = jnp.zeros((TILE, 256), F32)
    for head in range(heads):
        dkey = dkey + dot(dscore_ref[head, :, offset:], query_n[head, offset:, :])
        dvalue = dvalue + dot(prob_ref[head, :, offset:], grad_n[head, offset:, :])
        rows = slice(64 * head, 64 * head + 64)
        dquery_ref[rows, offset:] = dquery_ref[rows, offset:] + dot(
            key_t[rows], dscore_ref[head, :, offset:]
        )
    dkv_ref[:, :, :, 0:128] = dkey[:, 0:128].reshape(2, 2, 64, 128)
    dkv_ref[:, :, :, 128:256] = (dkey[:, 128:256] + dvalue[:, 0:128]).reshape(2, 2, 64, 128)
    dkv_ref[:, :, :, 256:384] = dvalue[:, 128:256].reshape(2, 2, 64, 128)


def attention_backward(branch, saved, query256, grad256, mixed_t, keys_values, carried, heads):
    exps, buckets, lows, maxima, totals = saved
    members = keys_values.shape[0]
    tiles = members // 2
    first = branch * tiles
    groups = TILE // GROUP

    def whole(shape):
        return pl.BlockSpec(shape, lambda t: (0,) * len(shape))

    in_specs = [
        pl.BlockSpec((heads, TILE, ROWS), lambda t: (0, first + t, 0)),
        pl.BlockSpec((TILE, ROWS), lambda t: (first + t, 0)),
        pl.BlockSpec((TILE, ROWS), lambda t: (first + t, 0)),
        pl.BlockSpec((1, 8, ROWS), lambda t: (first + t, 0, 0)),
        whole((8, ROWS)),
        whole((ROWS, 256)),
        whole((ROWS, 256)),
        whole((192, ROWS)),
        pl.BlockSpec((2, 2, 64, 384), lambda t: (t, branch, 0, 0)),
    ]
    if branch == 0:
        carried = (totals, totals)
        in_specs += [whole((8, ROWS)), whole((8, ROWS))]
        aliases = {}
    else:
        in_specs += [
            whole((192, ROWS)),
            whole((128, 64 * heads)),
            pl.BlockSpec(memory_space=pl.ANY),
        ]
        aliases = {11: 2}
    return pl.pallas_call(
        functools.partial(backward_kernel, branch, heads),
        grid=(tiles,),
        in_specs=in_specs,
        out_specs=[
            whole((192, ROWS)),
            whole((128, 64 * heads)),
            pl.BlockSpec((2, 2, 64, 384), lambda t: (t, branch, 0, 0)),
        ],
        out_shape=[
            jax.ShapeDtypeStruct((192, ROWS), F32),
            jax.ShapeDtypeStruct((128, 64 * heads), F32),
            jax.ShapeDtypeStruct((members, 8, 64, 384), F32),
        ],
        input_output_aliases=aliases,
        scratch_shapes=[
            pltpu.VMEM((heads, 256, ROWS), BF16),
            pltpu.VMEM((heads, ROWS, 256), BF16),
            pltpu.VMEM((heads, ROWS, 256), BF16),
            pltpu.VMEM((heads, TILE, ROWS), F32),
            pltpu.VMEM((heads, TILE, ROWS), BF16),
            pltpu.VMEM((heads, TILE, ROWS), BF16),
            pltpu.VMEM((groups, 128, ROWS), BF16),
            pltpu.VMEM((groups, 64 * heads, ROWS), BF16),
            pltpu.VMEM((8, ROWS), F32),
            pltpu.VMEM((8, ROWS), F32),
        ],
        compiler_params=pltpu.CompilerParams(
            dimension_semantics=("arbitrary",), vmem_limit_bytes=58 << 20
        ),
        cost_estimate=pl.CostEstimate(
            flops=8 << 30, bytes_accessed=6 << 20, transcendentals=1 << 18
        ),
        name="attention_backward",
    )(exps, buckets, lows, maxima, totals, query256, grad256, mixed_t, keys_values, *carried)


def arrange_kernel(half_rows, query_rows, plane_ref, *refs):
    block_refs, out_ref, rows_ref = refs[:4], refs[4], refs[5]
    rows_ref[...] = jnp.zeros(rows_ref.shape, F32)
    for distance in range(4):
        plane = plane_ref[0] ^ distance
        block = block_refs[distance][...].astype(F32)
        start = pl.multiple_of(plane * half_rows, half_rows)
        rows_ref[pl.ds(start, half_rows), 64:256] = block[:half_rows, 0:192]
        start = pl.multiple_of((7 - plane) * half_rows, half_rows)
        rows_ref[pl.ds(start, half_rows), 64:256] = block[:half_rows, 192:384]
        start = pl.multiple_of(8 * half_rows + plane * query_rows, 8)
        rows_ref[pl.ds(start, query_rows), 64:256] = block[half_rows:, 0:192]
    out_ref[...] = rows_ref[...].astype(BF16)


def arrange_rows(blocks, plane, half_rows, query_rows):
    return pl.pallas_call(
        functools.partial(arrange_kernel, half_rows, query_rows),
        in_specs=[pl.BlockSpec(memory_space=pltpu.SMEM)]
        + [pl.BlockSpec(memory_space=pltpu.VMEM)] * 4,
        out_specs=pl.BlockSpec(memory_space=pltpu.VMEM),
        out_shape=jax.ShapeDtypeStruct((ROWS, 256), BF16),
        scratch_shapes=[pltpu.VMEM((ROWS, 256), F32)],
        name="arrange_rows",
    )(plane[None], *blocks)


def widen_kernel(group, order_ref, near_ref, far_ref, *out_refs):
    step = pl.program_id(0) ^ (order_ref[0] // group)
    half_steps = pl.num_programs(0) // 2
    inner = order_ref[0] % group

    def from_pieces(pieces_ref):
        rows = pieces_ref.shape[-2]
        for k in range(group):
            start = 0
            for out_ref in out_refs:
                columns = out_ref.shape[-1]
                lanes = slice(start, start + columns)
                if len(pieces_ref.shape) == 4:
                    for s in range(2):
                        block = pieces_ref[k ^ inner, s ^ order_ref[1], :, lanes]
                        out_ref[s, k * rows : (k + 1) * rows, :] = block.astype(F32)
                else:
                    block = pieces_ref[k ^ inner, :, lanes]
                    out_ref[k * rows : (k + 1) * rows, :] = block.astype(F32)
                start += columns

    pl.when(step < half_steps)(lambda: from_pieces(near_ref))
    pl.when(step >= half_steps)(lambda: from_pieces(far_ref))


def widen_rows(near, far, order, columns):
    half, rows, width = near.shape[0], near.shape[-2], near.shape[-1]
    sides = near.shape[1:-2]
    group = min(4, half)
    if rows % 16 != 0:
        pieces = jnp.concatenate([near, far], axis=0)
        position = jnp.arange(2 * half, dtype=jnp.int32) ^ order[0]
        whole = jnp.take(pieces, position, axis=0).astype(F32)
        if sides:
            whole = jnp.swapaxes(jnp.where(order[1] == 1, whole[:, ::-1], whole), 0, 1)
        whole = whole.reshape(sides + (2 * half * rows, width))
        ends = [sum(columns[: i + 1]) for i in range(len(columns))]
        return [whole[..., end - c : end] for end, c in zip(ends, columns)]
    zeros = (0,) * (len(sides) + 2)
    half_steps = half // group

    def piece_map(part):
        def index(r, o):
            order_step = o[0] // group
            first = jnp.where(order_step >= half_steps, 1 - part, part) * half_steps
            inside = jnp.clip(r, first, first + half_steps - 1)
            return ((inside ^ order_step) % half_steps,) + zeros

        return index

    def out_map(r, o):
        return (0,) * len(sides) + (r, 0)

    return pl.pallas_call(
        functools.partial(widen_kernel, group),
        grid_spec=pltpu.PrefetchScalarGridSpec(
            num_scalar_prefetch=1,
            grid=(2 * half_steps,),
            in_specs=[pl.BlockSpec((group,) + near.shape[1:], piece_map(part)) for part in range(2)],
            out_specs=[pl.BlockSpec(sides + (group * rows, c), out_map) for c in columns],
        ),
        out_shape=[jax.ShapeDtypeStruct(sides + (2 * half * rows, c), F32) for c in columns],
        compiler_params=pltpu.CompilerParams(
            dimension_semantics=("arbitrary",), vmem_limit_bytes=24 << 20
        ),
        cost_estimate=pl.CostEstimate(
            flops=0, bytes_accessed=6 * near.size * 2, transcendentals=0
        ),
        name="widen_rows",
    )(order, near, far)


def widen_heads_kernel(order_ref, pieces_ref, *out_refs):
    odd = order_ref[1] == 1
    first, second = pieces_ref[0, 0], pieces_ref[0, 1]
    low = jnp.where(odd, second.astype(F32), first.astype(F32))
    high = jnp.where(odd, first.astype(F32), second.astype(F32))
    size = low.shape[1] // 3
    for i, out_ref in enumerate(out_refs):
        lanes = slice(i * size, (i + 1) * size)
        out_ref[...] = jnp.concatenate([low[:, lanes], high[:, lanes]], axis=1)


def widen_heads(pieces, order, odd):
    count, _, rows, width = pieces.shape
    columns = 2 * width // 3
    return pl.pallas_call(
        widen_heads_kernel,
        grid_spec=pltpu.PrefetchScalarGridSpec(
            num_scalar_prefetch=1,
            grid=(count,),
            in_specs=[pl.BlockSpec((1, 2, rows, width), lambda r, o: (r ^ o[0], 0, 0, 0))],
            out_specs=[pl.BlockSpec((rows, columns), lambda r, o: (r, 0))] * 3,
        ),
        out_shape=[jax.ShapeDtypeStruct((count * rows, columns), F32)] * 3,
        compiler_params=pltpu.CompilerParams(dimension_semantics=("arbitrary",)),
        cost_estimate=pl.CostEstimate(
            flops=0, bytes_accessed=12 * count * rows * width, transcendentals=0
        ),
        name="widen_heads",
    )(jnp.stack([order, odd]), pieces)


def after(value, *earlier):
    return lax.optimization_barrier((value,) + earlier)[0]


def row_major(value):
    return with_layout_constraint(value, Layout(major_to_minor=tuple(range(value.ndim))))


class Chain:
    def __init__(self, state, stages):
        self.state, self.stages = state, stages
        self.leave()

    def leave(self):
        if self.stages:
            self.sent, self.kept = self.stages[0][0](self.state)
            self.arrived = self.stages[0][1](self.sent)

    def advance(self, token):
        kept = jax.tree.map(lambda leaf: after(leaf, token), self.kept)
        self.state = self.stages[0][2](kept, self.arrived)
        self.stages = self.stages[1:]
        self.leave()
        return self.sent if self.stages else jax.tree.leaves(self.state)[0]

    def drain(self, token):
        while self.stages:
            token = self.advance(token)
        return token


def reverse_bits(value, count):
    result = jnp.zeros_like(value)
    bit, mirrored = 1, count // 2
    while bit < count:
        result = result + jnp.where((value & bit) != 0, mirrored, 0)
        bit, mirrored = bit * 2, mirrored // 2
    return result


def body(
    content,
    query_stream,
    token_order,
    targets,
    query_weight,
    key_weight,
    value_weight,
    output_weight,
    query_bias,
    value_bias,
    output_bias,
    bias_table,
    first_gain,
    first_shift,
    inner_weight,
    inner_bias,
    outer_weight,
    outer_bias,
    second_gain,
    second_shift,
    content_cotangent,
    query_cotangent,
):
    ctx = lax.axis_size("ctx")
    index = lax.axis_index("ctx")
    side = lax.axis_index("wt")
    members = ctx // 4
    plane = index // members
    member = index % members
    half_rows = content.shape[2]
    tok_rows = 2 * half_rows
    query_rows = query_stream.shape[1]
    rows_dev = tok_rows + query_rows
    width = content.shape[3]
    heads = bias_table.shape[1]
    my_heads = heads // 4
    head_width = my_heads * (width // heads)
    half_width = width // 2
    seq_length = tok_rows * ctx
    half_length = seq_length // 2
    order_row = token_order[0]
    target_row = targets[0]
    core_bit = (index & 1) == 1

    def swap(value, bit):
        return lax.ppermute(value, "ctx", [(i, i ^ bit) for i in range(ctx)])

    def swap_side(value):
        return lax.ppermute(value, "wt", [(0, 1), (1, 0)])

    def order_two(flag, mine, other, axis):
        low = jnp.where(flag, other, mine)
        high = jnp.where(flag, mine, other)
        return jnp.concatenate([low, high], axis=axis)

    def half_of_core(value):
        rows = value.shape[0] // 2
        return lax.dynamic_slice_in_dim(value, (index & 1) * rows, rows, 0)

    def both_cores(arrived):
        return order_two(core_bit, arrived, swap(arrived, 1), 0)

    def by_distance(blocks):
        flag = (plane & 1) == 1
        blocks = [jnp.where(flag, blocks[d ^ 1], blocks[d]) for d in range(4)]
        flag = (plane & 2) == 2
        return [jnp.where(flag, blocks[d ^ 2], blocks[d]) for d in range(4)]

    def exchange_planes(blocks):
        sent = by_distance(blocks)
        arrived = [sent[0]] + [swap(sent[d], d * members) for d in range(1, 4)]
        return by_distance(arrived)

    def pack_rows(rows):
        top = jnp.concatenate([rows[:half_rows], rows[half_rows:tok_rows]], axis=1)
        bottom = jnp.concatenate([rows[tok_rows:], jnp.zeros_like(rows[tok_rows:])], axis=1)
        return jnp.concatenate([top, bottom], axis=0)

    def unpack_rows(packed):
        return jnp.concatenate(
            [
                packed[:half_rows, :head_width],
                packed[:half_rows, head_width:],
                packed[half_rows:, :head_width],
            ],
            axis=0,
        )

    def plane_rows(blocks):
        pad = ROWS - 4 * rows_dev
        return jnp.concatenate(
            [blocks[d][:half_rows] for d in range(4)]
            + [blocks[3 - d][half_rows:tok_rows] for d in range(4)]
            + [blocks[d][tok_rows:] for d in range(4)]
            + [jnp.zeros((pad, blocks[0].shape[1]), blocks[0].dtype)],
            axis=0,
        )

    def split_rows(rows):
        blocks = []
        for d in range(4):
            parts = [
                rows[d * half_rows : (d + 1) * half_rows],
                rows[(7 - d) * half_rows : (8 - d) * half_rows],
            ]
            if rows.shape[0] > 4 * tok_rows:
                start = 4 * tok_rows + d * query_rows
                parts.append(rows[start : start + query_rows])
            blocks.append(jnp.concatenate(parts, axis=0))
        return blocks

    local_content = content[0].reshape(tok_rows, width)
    stacked = jnp.concatenate([local_content, query_stream[0]], axis=0)
    arrived_rows = [stacked] + [swap(stacked, d * members) for d in range(1, 4)]
    owner = plane // 2
    odd_plane = (plane & 1) == 1
    side_flag = side == 1
    shards = [query_weight, key_weight, value_weight]
    near_own = jnp.concatenate(
        [jnp.where(odd_plane, s[:, head_width:], s[:, :head_width]) for s in shards], axis=1
    )
    near_sent = half_of_core(near_own)
    near_other = both_cores(swap_side(near_sent))
    vectors = [
        query_bias,
        value_bias,
        output_bias,
        first_gain,
        first_shift,
        outer_bias,
        second_gain,
        second_shift,
    ]
    own_vectors = jnp.concatenate(
        [after(vectors[0], near_sent)] + vectors[1:] + [bias_table.reshape(-1)]
    )
    other_vectors = swap_side(own_vectors)
    (
        full_query_bias,
        full_value_bias,
        full_output_bias,
        full_first_gain,
        full_first_shift,
        full_outer_bias,
        full_second_gain,
        full_second_shift,
    ) = [
        order_two(
            side_flag,
            own_vectors[i * half_width : (i + 1) * half_width],
            other_vectors[i * half_width : (i + 1) * half_width],
            0,
        ).astype(F32)
        for i in range(8)
    ]
    full_table = (
        order_two(side_flag, own_vectors[8 * half_width :], other_vectors[8 * half_width :], 0)
        .astype(F32)
        .reshape(-1, heads)
    )
    buckets = full_table.shape[0]

    places = jnp.arange(half_length, dtype=jnp.int32)
    key_place = jnp.concatenate(
        [places, (seq_length - 1 - places).reshape(4, -1)[::-1].reshape(-1)]
    )
    key_anchor = jnp.concatenate(
        [
            order_row[:half_length],
            order_row[half_length:][::-1].reshape(4, -1)[::-1].reshape(-1),
        ]
    )

    def of_member(array, count):
        return lax.dynamic_index_in_dim(
            array.reshape(-1, members, count), member, 1, keepdims=False
        ).reshape(-1)

    def by_member_distance(array):
        pieces = [array.reshape(8, members, -1)]
        bit = members // 2
        while bit >= 1:
            flag = (member & bit) != 0
            split = []
            for piece in pieces:
                size = piece.shape[1] // 2
                low, high = piece[:, :size], piece[:, size:]
                split.append(jnp.where(flag, high, low))
                split.append(jnp.where(flag, low, high))
            pieces = split
            bit //= 2
        return jnp.concatenate(pieces, axis=1)

    plane_targets = of_member(target_row, query_rows)
    target_anchor = jnp.sum(
        jnp.where(
            jnp.arange(seq_length, dtype=jnp.int32)[:, None] == plane_targets[None],
            order_row[:, None],
            0,
        ),
        axis=0,
    )
    pad_rows = ROWS - 4 * rows_dev
    row_anchor = jnp.concatenate(
        [of_member(key_anchor, half_rows), target_anchor, jnp.zeros((pad_rows,), jnp.int32)]
    )
    row_limit = jnp.concatenate(
        [
            of_member(key_place, half_rows) + 1,
            plane_targets,
            jnp.ones((pad_rows,), jnp.int32),
        ]
    )
    row_info = jnp.concatenate(
        [row_anchor[None], row_limit[None], jnp.zeros((6, ROWS), jnp.int32)], axis=0
    )

    def by_tile(array):
        parts = by_member_distance(array).reshape(4, 2, members // 2, 2, -1)
        return jnp.transpose(parts, (0, 2, 3, 1, 4)).reshape(-1)

    near_anchor = by_tile(key_anchor)
    key_anchor_wide = jnp.broadcast_to(near_anchor[:, None], (seq_length, 128))
    block_places = by_tile(key_place.reshape(-1, half_rows)[:, 0])
    head_start = plane * my_heads
    my_table = lax.dynamic_slice_in_dim(full_table, head_start, my_heads, 1)
    tables = jnp.pad(my_table.T, ((0, 8 - my_heads), (0, 128 - buckets)))

    head_weights = jnp.where(side == owner, near_own, near_other)
    plane_x = plane_rows(by_distance(arrived_rows))
    my_query_bias = lax.dynamic_slice_in_dim(full_query_bias, plane * head_width, head_width, 0)
    my_value_bias = lax.dynamic_slice_in_dim(full_value_bias, plane * head_width, head_width, 0)
    kv_bias = jnp.concatenate([jnp.zeros_like(my_value_bias), my_value_bias])
    plane_kv = (dot(plane_x[: 4 * tok_rows], head_weights[:, head_width:]) + kv_bias).astype(BF16)
    first_kv = plane_kv.reshape(1, 8, half_rows, 2 * head_width)
    far_kv = swap(first_kv, members // 2)
    bit = 1
    near_members = first_kv
    while bit < members // 2:
        near_members = jnp.concatenate([near_members, swap(near_members, bit)], axis=0)
        bit *= 2
    query_weights = jnp.pad(head_weights[:, :head_width], ((0, 0), (0, 256 - head_width)))
    query_shift = jnp.pad(my_query_bias, (0, 256 - head_width))
    query256 = ((dot(plane_x, query_weights) + query_shift) * 0.125).astype(BF16)

    output_early, outer_early, rest_own = lax.optimization_barrier(
        (
            output_weight,
            outer_weight,
            jnp.concatenate(
                [jnp.where(odd_plane, s[:, :head_width], s[:, head_width:]) for s in shards],
                axis=1,
            ),
            query256,
        )
    )[:3]
    hidden_half = outer_weight.shape[0] // 2

    outer_sent = lax.dynamic_slice_in_dim(outer_early, (1 - side) * hidden_half, hidden_half, 0)
    output_arrived = swap_side(half_of_core(output_early))
    outer_arrived_half = swap_side(half_of_core(outer_sent))
    rest_arrived = swap_side(half_of_core(rest_own))

    forward_info = (key_anchor_wide, block_places, row_info, tables)
    first_half = attention_forward(0, query256, near_members, *forward_info, (), my_heads)
    far_members = far_kv
    bit = 1
    while bit < members // 2:
        far_members = jnp.concatenate([far_members, swap(far_members, bit)], axis=0)
        bit *= 2
    exps, bucket_ids, bucket_lows, maxima, _, _, mixed_t, mixed_plane, totals = attention_forward(
        1, query256, far_members, *forward_info, first_half, my_heads
    )
    keys_values = jnp.concatenate([near_members, far_members], axis=0)

    full_output = order_two(side_flag, output_weight, both_cores(after(output_arrived, mixed_plane)), 1)
    outer_kept = lax.dynamic_slice_in_dim(outer_weight, side * hidden_half, hidden_half, 0)
    outer_rows = order_two(side_flag, outer_kept, both_cores(after(outer_arrived_half, mixed_plane)), 1)
    rest_other = both_cores(after(rest_arrived, mixed_plane))
    full_qkv = []
    for i in range(3):
        lanes = slice(i * head_width, (i + 1) * head_width)
        other = order_two(odd_plane, near_other[:, lanes], rest_other[:, lanes], 1)
        full_qkv.append(order_two(side_flag, shards[i], other, 1))

    mixed_blocks = exchange_planes([pack_rows(block) for block in split_rows(mixed_plane)])
    mixed = jnp.concatenate([unpack_rows(block) for block in mixed_blocks], axis=1)
    branch = dot(mixed, full_output) + full_output_bias
    first_norm, first_back = jax.vjp(
        norm_of_sum, stacked.astype(F32), branch, full_first_gain, full_first_shift
    )
    first_low = first_norm.astype(BF16)
    both_first = jnp.concatenate([first_low, swap_side(first_low)], axis=0)
    inner_value = dot(both_first, inner_weight) + inner_bias.astype(F32)
    hidden_value, gelu_back = jax.vjp(gelu_exact, inner_value)
    hidden_low = hidden_value.astype(BF16)
    outer_part = dot(hidden_low, outer_rows)
    outer_arrived = swap_side(outer_part[rows_dev:].astype(BF16))
    outer_value = outer_part[:rows_dev] + outer_arrived.astype(F32) + full_outer_bias
    final_norm, second_back = jax.vjp(
        norm_of_sum, first_norm, outer_value, full_second_gain, full_second_shift
    )
    content_result = final_norm[:tok_rows].reshape(1, 2, half_rows, width).astype(BF16)
    query_result = final_norm[tok_rows:].reshape(1, query_rows, width).astype(BF16)
    cotangent = jnp.concatenate(
        [content_cotangent[0].reshape(tok_rows, width), query_cotangent[0]], axis=0
    )
    rest_grad, outer_grad, second_gain_grad, second_shift_grad = second_back(cotangent.astype(F32))
    outer_low = outer_grad.astype(BF16)
    both_outer = jnp.concatenate([outer_low, swap_side(outer_low)], axis=0)
    (inner_grad,) = gelu_back(times_transpose(both_outer, outer_rows))
    inner_low = inner_grad.astype(BF16)
    first_part = times_transpose(inner_low, inner_weight)
    first_arrived = swap_side(first_part[rows_dev:].astype(BF16))
    first_grad = rest_grad + (first_part[:rows_dev] + first_arrived.astype(F32))
    row_grad, branch_grad, first_gain_grad, first_shift_grad = first_back(first_grad)
    branch_low = branch_grad.astype(BF16)
    mixed_low = times_transpose(branch_low, full_output).astype(BF16)

    def to(bit):
        return lambda value: swap(value, bit)

    def leave_half(bit):
        def leave(parts):
            rows = parts[0].shape[0] // 2
            upper = jnp.where((index & bit) != 0, 1, 0)
            sent = [
                lax.dynamic_slice_in_dim(part, (1 - upper) * rows, rows, 0).astype(BF16)
                for part in parts
            ]
            return jnp.concatenate(sent, axis=1), parts

        return leave

    def add_half(bit):
        def add(parts, arrived):
            rows = parts[0].shape[0] // 2
            upper = jnp.where((index & bit) != 0, 1, 0)
            kept = [lax.dynamic_slice_in_dim(part, upper * rows, rows, 0) for part in parts]
            return [jnp.concatenate(kept, axis=1) + arrived.astype(F32)]

        return add

    def keep_all(state):
        return state, state

    def append(kept, arrived):
        return jnp.concatenate([kept, arrived], axis=0)

    bits = []
    bit = 1
    while bit < ctx:
        bits.append(bit)
        bit *= 2
    sum_stages = [(leave_half(bit), to(bit), add_half(bit)) for bit in bits]
    gather_stages = [(keep_all, to(bit), append) for bit in bits[::-1]]

    def leave_columns(parts):
        piece = parts[0].astype(BF16)
        left, right = piece[:, :half_width], piece[:, half_width:]
        return jnp.where(side_flag, left, right), jnp.where(side_flag, right, left)

    def pair_sides(kept, arrived):
        return jnp.stack([kept, arrived], axis=0)[None]

    def start_gather(parts):
        state = parts[0].astype(BF16)[None]
        return state, state

    outer_chain = Chain(
        [contract_rows(hidden_low, both_outer)],
        sum_stages + [(leave_columns, swap_side, pair_sides)] + gather_stages[:-1],
    )

    other_mixed = swap_side(mixed)
    branch_left, branch_right = branch_low[:, :half_width], branch_low[:, half_width:]
    branch_kept = jnp.where(side_flag, branch_right, branch_left)
    inner_part = contract_rows(both_first, inner_low)
    branch_arrived = swap_side(jnp.where(side_flag, branch_left, branch_right))
    output_part = contract_rows(mixed, branch_kept) + contract_rows(other_mixed, branch_arrived)
    joined_chain = Chain(
        [inner_part, output_part],
        sum_stages + [(start_gather, to(bits[-1]), append)] + gather_stages[1:-1],
    )

    token = outer_chain.advance(branch_low)
    grad_sent = by_distance(
        [
            pack_rows(mixed_low[:, d * head_width : (d + 1) * head_width])
            for d in range(4)
        ]
    )
    grad_sent = lax.optimization_barrier(tuple(grad_sent) + (token,))[:4]
    grad_blocks = [grad_sent[0]] + [swap(grad_sent[d], d * members) for d in range(1, 4)]
    grad256 = arrange_rows(grad_blocks, plane, half_rows, query_rows)
    saved = (exps, bucket_ids, bucket_lows, maxima, totals)
    carried = None
    for call in range(4):
        if call == 0:
            token = outer_chain.advance(grad256)
            token = joined_chain.advance(token)
            grad256 = after(grad256, token)
        else:
            token = outer_chain.advance(carried[0])
            if call > 1:
                token = joined_chain.advance(token)
            carried = (after(carried[0], token),) + carried[1:]
        carried = tuple(
            attention_backward(
                call, saved, query256, grad256, mixed_t, keys_values, carried, my_heads
            )
        )
    dquery_t, table_part, dkv = carried
    query_scaled = dquery_t.T.astype(BF16) * 0.125

    member_bits = [bit for bit in bits if bit < members]

    def leave_members(state):
        pairs = state.reshape((-1, 2) + state.shape[1:])
        return row_major(pairs[:, 1].astype(BF16)), state

    def add_members(state, arrived):
        pairs = state.reshape((-1, 2) + state.shape[1:])
        return row_major(pairs[:, 0] + arrived.astype(F32))

    kv_chain = Chain(
        dkv,
        [(leave_members, to(bit), add_members) for bit in member_bits],
    )
    token = joined_chain.advance(kv_chain.sent)
    token = kv_chain.advance(token)
    token = outer_chain.advance(token)
    token = joined_chain.advance(token)
    token = kv_chain.drain(token)
    kv_low = kv_chain.state.reshape(4 * tok_rows, 2 * head_width).astype(BF16)

    low_parts = jnp.concatenate(
        [query_scaled, jnp.pad(kv_low, ((0, ROWS - 4 * tok_rows), (0, 0)))], axis=1
    )

    def leave_same(parts):
        return parts[0].astype(BF16), parts

    def add_side(kept, arrived):
        return (kept[0] + arrived.astype(F32)).astype(BF16)

    def choose_owner(kept, arrived):
        return jnp.where(owner == side, kept, arrived)[None]

    def append_plane(kept, arrived):
        return jnp.concatenate([kept, arrived], axis=0)[None]

    heads_chain = Chain(
        [contract_rows(plane_x, low_parts)],
        sum_stages[: len(member_bits)]
        + [
            (leave_same, swap_side, add_side),
            (keep_all, to(2 * members), choose_owner),
            (keep_all, to(members), append_plane),
        ]
        + [(keep_all, to(bit), append) for bit in member_bits[::-1]],
    )

    sent_blocks = [
        jnp.concatenate([pack_rows(query_block), kv_block], axis=0)
        for query_block, kv_block in zip(split_rows(query_scaled), split_rows(kv_low))
    ]
    sent_distance = by_distance(sent_blocks)
    sent_distance = lax.optimization_barrier(tuple(sent_distance) + (heads_chain.sent,))[:4]
    got_distance = [sent_distance[0]] + [
        swap(sent_distance[d], d * members) for d in range(1, 4)
    ]
    full_query, full_key, full_value = full_qkv

    blocks = table_part.reshape(8, GROUP, 4, my_heads, GROUP)
    same = jnp.eye(GROUP, dtype=F32)[None, :, None, None, :]
    table_cumulative = jnp.sum(blocks * same, axis=(1, 4))
    table_grad = table_cumulative - jnp.concatenate(
        [table_cumulative[1:], jnp.zeros_like(table_cumulative[:1])], axis=0
    )
    table_grad = table_grad.reshape(buckets, my_heads)

    def at_plane(values, axis):
        return jnp.concatenate(
            [jnp.where(plane == d, values, jnp.zeros_like(values)) for d in range(4)], axis=axis
        )

    inner_bias_part = jnp.sum(inner_low.astype(F32), axis=0)
    inner_bias_zero = jnp.zeros_like(inner_bias_part)
    late_small = jnp.concatenate(
        [
            at_plane(jnp.sum(query_scaled.astype(F32), axis=0), 0),
            at_plane(jnp.sum(kv_low[:, head_width:].astype(F32), axis=0), 0),
            jnp.sum(branch_low.astype(F32), axis=0),
            first_gain_grad,
            first_shift_grad,
            jnp.sum(outer_low.astype(F32), axis=0),
            second_gain_grad,
            second_shift_grad,
            jnp.where(side_flag, inner_bias_zero, inner_bias_part),
            jnp.where(side_flag, inner_bias_part, inner_bias_zero),
            at_plane(table_grad, 1).reshape(-1),
        ]
    )
    late_length = late_small.shape[0]
    late_small = jnp.pad(late_small, (0, -late_length % 1024)).reshape(-1, 128)

    def add_plain(kept, arrived):
        return kept + arrived

    late_chain = Chain(
        after(late_small, heads_chain.sent),
        [(keep_all, to(bit), add_plain) for bit in bits] + [(keep_all, swap_side, add_plain)],
    )

    token = heads_chain.advance(late_chain.sent)
    token = late_chain.advance(token)
    token = joined_chain.advance(token)
    token = heads_chain.advance(token)
    token = outer_chain.advance(token)
    token = late_chain.advance(token)
    token = heads_chain.advance(token)
    got_distance = lax.optimization_barrier(tuple(got_distance) + (token,))[:4]
    got_blocks = by_distance(got_distance)
    packed_rows = half_rows + query_rows
    own_query = jnp.concatenate([unpack_rows(b[:packed_rows]) for b in got_blocks], axis=1)
    own_key = jnp.concatenate([b[packed_rows:, :head_width] for b in got_blocks], axis=1)
    own_value = jnp.concatenate([b[packed_rows:, head_width:] for b in got_blocks], axis=1)
    input_grad = row_grad + times_transpose(own_query, full_query)
    content_extra = times_transpose(own_key, full_key) + times_transpose(own_value, full_value)
    content_gradient = (input_grad[:tok_rows] + content_extra).reshape(1, 2, half_rows, width)
    query_gradient = input_grad[tok_rows:].reshape(1, query_rows, width)
    token = joined_chain.advance(content_gradient)
    token = late_chain.advance(token)
    token = heads_chain.advance(token)
    token = outer_chain.advance(token)
    token = late_chain.advance(token)
    token = heads_chain.advance(token)
    token = late_chain.drain(token)
    token = outer_chain.drain(token)
    outer_near, outer_far = outer_chain.state, swap(outer_chain.state, 1)
    token = joined_chain.drain(token)
    token = heads_chain.drain(token)
    row_order = jnp.stack([reverse_bits(index, ctx), side])
    joined_pieces = joined_chain.state
    outer_weight_grad = widen_rows(
        outer_near, outer_far, row_order, (half_width,)
    )[0].reshape(2 * hidden_half, half_width)
    inner_weight_grad, output_weight_grad = widen_rows(
        joined_pieces, swap(joined_pieces, 1), row_order, (hidden_half, half_width)
    )
    qkv_grads = widen_heads(heads_chain.state, reverse_bits(member, members), plane & 1)

    late_small = late_chain.state.reshape(-1)[:late_length]
    table_start = 8 * width + 2 * hidden_half
    table_all = late_small[table_start:].reshape(2, buckets // 2, heads)
    bias_table_grad = jnp.where(side_flag, table_all[1], table_all[0])

    def my_half(start, size):
        low = late_small[start : start + size]
        return jnp.where(side_flag, late_small[start + size : start + 2 * size], low)

    mine = [my_half(i * width, half_width) for i in range(8)]
    inner_bias_grad = my_half(8 * width, hidden_half)

    return (
        content_result,
        query_result,
        content_gradient,
        query_gradient,
        qkv_grads[0],
        qkv_grads[1],
        qkv_grads[2],
        output_weight_grad,
        mine[0],
        mine[1],
        mine[2],
        bias_table_grad,
        mine[3],
        mine[4],
        inner_weight_grad,
        inner_bias_grad,
        outer_weight_grad,
        mine[5],
        mine[6],
        mine[7],
    )


def solution(mesh):
    return jax.shard_map(
        body,
        mesh=mesh,
        in_specs=(
            P("wt", None, "ctx", None),
            P("wt", "ctx", None),
            P("wt", None),
            P("wt", None),
            P(None, "wt"),
            P(None, "wt"),
            P(None, "wt"),
            P(None, "wt"),
            P("wt"),
            P("wt"),
            P("wt"),
            P("wt", None),
            P("wt"),
            P("wt"),
            P(None, "wt"),
            P("wt"),
            P(None, "wt"),
            P("wt"),
            P("wt"),
            P("wt"),
            P("wt", None, "ctx", None),
            P("wt", "ctx", None),
        ),
        out_specs=(
            P("wt", None, "ctx", None),
            P("wt", "ctx", None),
            P("wt", None, "ctx", None),
            P("wt", "ctx", None),
            P(None, "wt"),
            P(None, "wt"),
            P(None, "wt"),
            P(None, "wt"),
            P("wt"),
            P("wt"),
            P("wt"),
            P("wt", None),
            P("wt"),
            P("wt"),
            P(None, "wt"),
            P("wt"),
            P(None, "wt"),
            P("wt"),
            P("wt"),
            P("wt"),
        ),
        check_vma=False,
    )
```

```python
import functools

import jax
import jax.numpy as jnp
from jax import lax
from jax.experimental import pallas as pl
from jax.experimental.layout import Layout, with_layout_constraint
from jax.experimental.pallas import tpu as pltpu
from jax.sharding import PartitionSpec as P

BF16 = jnp.bfloat16
F32 = jnp.float32
FAR_EDGES = (12, 16, 23, 32, 46, 64, 91)
NEGATIVE = -1e30
TILE = 256
ROWS = 640
GROUP = 16


def layer_norm(hidden_rows, gain_row, shift_row):
    average = jnp.mean(hidden_rows, axis=-1, keepdims=True)
    centered = hidden_rows - average
    variance = jnp.mean(centered * centered, axis=-1, keepdims=True)
    return centered * lax.rsqrt(variance + 1e-05) * gain_row + shift_row


def norm_of_sum(residual, branch_value, gain_row, shift_row):
    return layer_norm(residual + branch_value, gain_row, shift_row)


def gelu_exact(values):
    return jax.nn.gelu(values, approximate=False)


def dot(left, right):
    return jnp.dot(left, right, preferred_element_type=F32)


def contract_rows(left, right):
    return lax.dot_general(left, right, (((0,), (0,)), ((), ())), preferred_element_type=F32)


def times_transpose(left, right):
    return lax.dot_general(left, right, (((1,), (1,)), ((), ())), preferred_element_type=F32)


def transpose_low(block):
    return block.astype(F32).T.astype(BF16)


def tile_branches(branch_index, process):
    for branch in range(4):
        pl.when(branch_index == branch)(functools.partial(process, 128 * branch))


def forward_kernel(call, count, heads, *refs):
    place_ref, query_ref, kv_ref, anchor_ref, row_ref, table_ref = refs[:6]
    refs = refs[6:]
    if call == 1:
        max_in, sum_in, mixed_in = refs[4:7]
        refs = refs[7:]
    exp_ref, bucket_ref, low_ref, max_ref, run_max, run_sum, mixed_t_ref = refs[:7]
    refs = refs[7:]
    if call == 1:
        mixed_ref, total_ref = refs[:2]
        refs = refs[2:]
    query_z, prob_ref, scale_ref = refs
    step = pl.program_id(0)
    branch_index = step // count
    tile_index = branch_index * (2 * count) + call * count + step % count

    @pl.when(step == 0)
    def _():
        query_t = transpose_low(query_ref[...])
        part = lax.broadcasted_iota(jnp.int32, (256, ROWS), 0) // 64
        for head in range(heads):
            query_z[head] = jnp.where(part == head, query_t.astype(F32), 0.0).astype(BF16)
        if call == 0:
            run_max[...] = jnp.full(run_max.shape, NEGATIVE, F32)
            run_sum[...] = jnp.zeros(run_sum.shape, F32)
            mixed_t_ref[...] = jnp.zeros(mixed_t_ref.shape, F32)
        else:
            run_max[...] = max_in[...]
            run_sum[...] = sum_in[...]
            mixed_t_ref[...] = mixed_in[...]

    place_sign = jnp.where(branch_index < 2, 1, -1)
    keys_values = kv_ref[...].reshape(TILE, 384)
    value_t = transpose_low(keys_values[:, 128:384])

    def process(offset):
        chunks = (ROWS - offset) // 128
        for head in range(heads):
            exp_ref[head, :, offset:] = dot(keys_values[:, 0:256], query_z[head, :, offset:])

        def bias_group(group, tops):
            start = pl.multiple_of(group * GROUP, GROUP)
            keys = anchor_ref[pl.ds(start, GROUP), :]
            row = start % 64 + lax.broadcasted_iota(jnp.int32, (GROUP, 128), 0)
            place = place_ref[tile_index * (TILE // 64) + start // 64] + place_sign * row
            new_tops = []
            for chunk in range(chunks):
                lanes = slice(offset + chunk * 128, offset + chunk * 128 + 128)
                relative = keys - row_ref[0:1, lanes]
                magnitude = jnp.abs(relative)
                bucket = jnp.minimum(magnitude, 8)
                for edge in FAR_EDGES:
                    bucket = bucket + jnp.where(magnitude >= edge, 1, 0)
                bucket = bucket + jnp.where(relative > 0, 16, 0)
                bucket_ref[pl.ds(start, GROUP), lanes] = bucket.astype(F32).astype(BF16)
                low_ref[pl.ds(start, GROUP), lanes] = (bucket & 3).astype(F32).astype(BF16)
                allowed = place < row_ref[1:2, lanes]
                for head in range(heads):
                    table = jnp.broadcast_to(table_ref[head : head + 1, :], (8, 128))
                    bias = jnp.concatenate(
                        [
                            jnp.take_along_axis(table, bucket[0:8], axis=1),
                            jnp.take_along_axis(table, bucket[8:16], axis=1),
                        ],
                        axis=0,
                    )
                    scores = exp_ref[head, pl.ds(start, GROUP), lanes] + bias
                    scores = jnp.where(allowed, scores, NEGATIVE)
                    exp_ref[head, pl.ds(start, GROUP), lanes] = scores
                    top = tops[chunk * heads + head]
                    new_tops.append(jnp.maximum(top, jnp.maximum(scores[0:8], scores[8:16])))
            return tuple(new_tops)

        tops = lax.fori_loop(
            0,
            TILE // GROUP,
            bias_group,
            tuple(jnp.full((8, 128), NEGATIVE, F32) for _ in range(chunks * heads)),
            unroll=2,
        )
        for chunk in range(chunks):
            lanes = slice(offset + chunk * 128, offset + chunk * 128 + 128)
            for head in range(heads):
                top = jnp.max(tops[chunk * heads + head], axis=0, keepdims=True)
                old = run_max[head : head + 1, lanes]
                new = jnp.maximum(old, top)
                scale_ref[head : head + 1, lanes] = jnp.exp(old - new)
                run_max[head : head + 1, lanes] = new
        max_ref[0] = run_max[...]

        def exp_group(group, sums):
            start = pl.multiple_of(group * GROUP, GROUP)
            new_sums = []
            for chunk in range(chunks):
                lanes = slice(offset + chunk * 128, offset + chunk * 128 + 128)
                for head in range(heads):
                    terms = jnp.exp(
                        exp_ref[head, pl.ds(start, GROUP), lanes] - run_max[head : head + 1, lanes]
                    )
                    exp_ref[head, pl.ds(start, GROUP), lanes] = terms
                    prob_ref[head, pl.ds(start, GROUP), lanes] = terms.astype(BF16)
                    new_sums.append(sums[chunk * heads + head] + (terms[0:8] + terms[8:16]))
            return tuple(new_sums)

        sums = lax.fori_loop(
            0,
            TILE // GROUP,
            exp_group,
            tuple(jnp.zeros((8, 128), F32) for _ in range(chunks * heads)),
        )
        for chunk in range(chunks):
            lanes = slice(offset + chunk * 128, offset + chunk * 128 + 128)
            for head in range(heads):
                run_sum[head : head + 1, lanes] = run_sum[head : head + 1, lanes] * scale_ref[
                    head : head + 1, lanes
                ] + jnp.sum(sums[chunk * heads + head], axis=0, keepdims=True)
        for head in range(heads):
            rows = slice(64 * head, 64 * head + 64)
            mixed_t_ref[rows, offset:] = mixed_t_ref[rows, offset:] * scale_ref[
                head : head + 1, offset:
            ] + dot(value_t[64 + 64 * head : 128 + 64 * head], prob_ref[head, :, offset:])

    tile_branches(branch_index, process)

    if call == 1:

        @pl.when(step == 4 * count - 1)
        def _():
            for head in range(heads):
                rows = slice(64 * head, 64 * head + 64)
                mixed_t_ref[rows, :] = mixed_t_ref[rows, :] / run_sum[head : head + 1, :]
                total_ref[head : head + 1, :] = run_max[head : head + 1, :] + jnp.log(
                    run_sum[head : head + 1, :]
                )
            mixed_ref[...] = mixed_t_ref[...].T.astype(BF16)


def attention_forward(
    call, query256, keys_values, key_anchor, block_places, row_info, tables, previous, heads
):
    count = keys_values.shape[0] // 2
    tiles = 8 * count
    total_keys = tiles * TILE

    def tile_of(s):
        return (s // count) * (2 * count) + call * count + s % count

    def whole(shape):
        return pl.BlockSpec(shape, lambda s, p: (0,) * len(shape))

    in_specs = [
        whole((ROWS, 256)),
        pl.BlockSpec((2, 2, 64, 384), lambda s, p: (s % count, s // count, 0, 0)),
        pl.BlockSpec((TILE, 128), lambda s, p: (tile_of(s), 0)),
        whole((8, ROWS)),
        whole((8, 128)),
    ]
    out_specs = [
        pl.BlockSpec((heads, TILE, ROWS), lambda s, p: (0, tile_of(s), 0)),
        pl.BlockSpec((TILE, ROWS), lambda s, p: (tile_of(s), 0)),
        pl.BlockSpec((TILE, ROWS), lambda s, p: (tile_of(s), 0)),
        pl.BlockSpec((1, 8, ROWS), lambda s, p: (tile_of(s), 0, 0)),
        whole((8, ROWS)),
        whole((8, ROWS)),
        whole((192, ROWS)),
    ]
    out_shape = [
        jax.ShapeDtypeStruct((heads, total_keys, ROWS), F32),
        jax.ShapeDtypeStruct((total_keys, ROWS), BF16),
        jax.ShapeDtypeStruct((total_keys, ROWS), BF16),
        jax.ShapeDtypeStruct((tiles, 8, ROWS), F32),
        jax.ShapeDtypeStruct((8, ROWS), F32),
        jax.ShapeDtypeStruct((8, ROWS), F32),
        jax.ShapeDtypeStruct((192, ROWS), F32),
    ]
    aliases = {}
    if call == 1:
        in_specs += [pl.BlockSpec(memory_space=pl.ANY)] * 4
        in_specs += [whole((8, ROWS)), whole((8, ROWS)), whole((192, ROWS))]
        out_specs += [whole((ROWS, 192)), whole((8, ROWS))]
        out_shape += [
            jax.ShapeDtypeStruct((ROWS, 192), BF16),
            jax.ShapeDtypeStruct((8, ROWS), F32),
        ]
        aliases = {6: 0, 7: 1, 8: 2, 9: 3}
    return pl.pallas_call(
        functools.partial(forward_kernel, call, count, heads),
        grid_spec=pltpu.PrefetchScalarGridSpec(
            num_scalar_prefetch=1,
            grid=(4 * count,),
            in_specs=in_specs,
            out_specs=out_specs,
            scratch_shapes=[
                pltpu.VMEM((heads, 256, ROWS), BF16),
                pltpu.VMEM((heads, TILE, ROWS), BF16),
                pltpu.VMEM((8, ROWS), F32),
            ],
        ),
        out_shape=out_shape,
        input_output_aliases=aliases,
        compiler_params=pltpu.CompilerParams(
            dimension_semantics=("arbitrary",), vmem_limit_bytes=32 << 20
        ),
        cost_estimate=pl.CostEstimate(
            flops=14 << 30, bytes_accessed=12 << 20, transcendentals=2 << 20
        ),
        name="attention_forward",
    )(block_places, query256, keys_values, key_anchor, row_info, tables, *previous)


def backward_kernel(branch, heads, *refs):
    refs = list(refs)
    if branch > 0:
        del refs[11]
    backward_tile(branch, heads, *refs)


def backward_tile(
    branch,
    heads,
    exp_ref,
    bucket_ref,
    low_ref,
    max_ref,
    total_ref,
    query_ref,
    grad_ref,
    mixed_t_ref,
    kv_ref,
    dquery_in,
    dtable_in,
    dquery_ref,
    dtable_ref,
    dkv_ref,
    grad_z,
    query_n,
    grad_n,
    dprob_ref,
    dscore_ref,
    prob_ref,
    high_hot,
    low_parts,
    delta_ref,
    scale_ref,
):
    tile_index = pl.program_id(0)
    offset = 128 * branch
    chunks = (ROWS - offset) // 128

    @pl.when(tile_index == 0)
    def _():
        grad_t = grad_ref[offset:, :].astype(F32).T
        part = lax.broadcasted_iota(jnp.int32, (256, ROWS - offset), 0) // 64
        lane_part = lax.broadcasted_iota(jnp.int32, (ROWS - offset, 256), 1) // 64
        for head in range(heads):
            grad_z[head, :, offset:] = jnp.where(part == head + 1, grad_t, 0.0).astype(BF16)
            query_n[head, offset:, :] = jnp.where(
                lane_part == head, query_ref[offset:, :].astype(F32), 0.0
            ).astype(BF16)
            grad_n[head, offset:, :] = jnp.where(
                lane_part == head + 1, grad_ref[offset:, :].astype(F32), 0.0
            ).astype(BF16)
            delta_ref[head : head + 1, offset:] = jnp.sum(
                grad_t[64 + 64 * head : 128 + 64 * head]
                * mixed_t_ref[64 * head : 64 * head + 64, offset:],
                axis=0,
                keepdims=True,
            )
        if branch == 0:
            dquery_ref[...] = jnp.zeros(dquery_ref.shape, F32)
            dtable_ref[...] = jnp.zeros(dtable_ref.shape, F32)
        else:
            dquery_ref[...] = dquery_in[...]
            dtable_ref[...] = dtable_in[...]

    keys_values = kv_ref[...].reshape(TILE, 384)
    key_t = transpose_low(keys_values[:, 0:256])
    for head in range(heads):
        dprob_ref[head, :, offset:] = dot(keys_values[:, 128:384], grad_z[head, :, offset:])
        scale_ref[head : head + 1, offset:] = jnp.exp(
            max_ref[0, head : head + 1, offset:] - total_ref[head : head + 1, offset:]
        )

    def build(group, slot):
        start = pl.multiple_of(group * GROUP, GROUP)
        one = jnp.ones((GROUP, 128), BF16)
        zero = jnp.zeros((GROUP, 128), BF16)
        for chunk in range(chunks):
            lanes = slice(offset + chunk * 128, offset + chunk * 128 + 128)
            bucket = bucket_ref[pl.ds(start, GROUP), lanes]
            low = low_ref[pl.ds(start, GROUP), lanes]
            for high in range(8):
                hot = jnp.where(bucket >= jnp.asarray(4 * high, BF16), one, zero)
                high_hot[slot, GROUP * high : GROUP * high + GROUP, lanes] = hot
            matches = [low == jnp.asarray(value, BF16) for value in range(4)]
            for head in range(heads):
                prob = (
                    exp_ref[head, pl.ds(start, GROUP), lanes] * scale_ref[head : head + 1, lanes]
                )
                dscore = prob * (
                    dprob_ref[head, pl.ds(start, GROUP), lanes]
                    - delta_ref[head : head + 1, lanes]
                )
                dscore_low = dscore.astype(BF16)
                prob_ref[head, pl.ds(start, GROUP), lanes] = prob.astype(BF16)
                dscore_ref[head, pl.ds(start, GROUP), lanes] = dscore_low
                for value in range(4):
                    row = GROUP * (value * heads + head)
                    low_parts[slot, row : row + GROUP, lanes] = jnp.where(
                        matches[value], dscore_low, zero
                    )

    def product(slot):
        return times_transpose(high_hot[slot, :, offset:], low_parts[slot, :, offset:])

    groups = TILE // GROUP
    build(0, 0)
    build(1, 1)

    def step(index, carry):
        even = product(0) + product(1)
        build(4 * index + 2, 2)
        build(4 * index + 3, 3)
        odd = product(2) + product(3)
        following = jnp.minimum(4 * index + 4, groups - 2)
        build(following, 0)
        build(following + 1, 1)
        dtable_ref[...] = dtable_ref[...] + (even + odd)
        return carry

    lax.fori_loop(0, groups // 4, step, 0)
    dkey = jnp.zeros((TILE, 256), F32)
    dvalue = jnp.zeros((TILE, 256), F32)
    for head in range(heads):
        dkey = dkey + dot(dscore_ref[head, :, offset:], query_n[head, offset:, :])
        dvalue = dvalue + dot(prob_ref[head, :, offset:], grad_n[head, offset:, :])
        rows = slice(64 * head, 64 * head + 64)
        dquery_ref[rows, offset:] = dquery_ref[rows, offset:] + dot(
            key_t[rows], dscore_ref[head, :, offset:]
        )
    dkv_ref[:, :, :, 0:128] = dkey[:, 0:128].reshape(2, 2, 64, 128)
    dkv_ref[:, :, :, 128:256] = (dkey[:, 128:256] + dvalue[:, 0:128]).reshape(2, 2, 64, 128)
    dkv_ref[:, :, :, 256:384] = dvalue[:, 128:256].reshape(2, 2, 64, 128)


def attention_backward(branch, saved, query256, grad256, mixed_t, keys_values, carried, heads):
    exps, buckets, lows, maxima, totals = saved
    members = keys_values.shape[0]
    tiles = members // 2
    first = branch * tiles
    def whole(shape):
        return pl.BlockSpec(shape, lambda t: (0,) * len(shape))

    in_specs = [
        pl.BlockSpec((heads, TILE, ROWS), lambda t: (0, first + t, 0)),
        pl.BlockSpec((TILE, ROWS), lambda t: (first + t, 0)),
        pl.BlockSpec((TILE, ROWS), lambda t: (first + t, 0)),
        pl.BlockSpec((1, 8, ROWS), lambda t: (first + t, 0, 0)),
        whole((8, ROWS)),
        whole((ROWS, 256)),
        whole((ROWS, 256)),
        whole((192, ROWS)),
        pl.BlockSpec((2, 2, 64, 384), lambda t: (t, branch, 0, 0)),
    ]
    if branch == 0:
        carried = (totals, totals)
        in_specs += [whole((8, ROWS)), whole((8, ROWS))]
        aliases = {}
    else:
        in_specs += [
            whole((192, ROWS)),
            whole((128, 64 * heads)),
            pl.BlockSpec(memory_space=pl.ANY),
        ]
        aliases = {11: 2}
    return pl.pallas_call(
        functools.partial(backward_kernel, branch, heads),
        grid=(tiles,),
        in_specs=in_specs,
        out_specs=[
            whole((192, ROWS)),
            whole((128, 64 * heads)),
            pl.BlockSpec((2, 2, 64, 384), lambda t: (t, branch, 0, 0)),
        ],
        out_shape=[
            jax.ShapeDtypeStruct((192, ROWS), F32),
            jax.ShapeDtypeStruct((128, 64 * heads), F32),
            jax.ShapeDtypeStruct((members, 8, 64, 384), F32),
        ],
        input_output_aliases=aliases,
        scratch_shapes=[
            pltpu.VMEM((heads, 256, ROWS), BF16),
            pltpu.VMEM((heads, ROWS, 256), BF16),
            pltpu.VMEM((heads, ROWS, 256), BF16),
            pltpu.VMEM((heads, TILE, ROWS), F32),
            pltpu.VMEM((heads, TILE, ROWS), BF16),
            pltpu.VMEM((heads, TILE, ROWS), BF16),
            pltpu.VMEM((4, 128, ROWS), BF16),
            pltpu.VMEM((4, 64 * heads, ROWS), BF16),
            pltpu.VMEM((8, ROWS), F32),
            pltpu.VMEM((8, ROWS), F32),
        ],
        compiler_params=pltpu.CompilerParams(
            dimension_semantics=("arbitrary",), vmem_limit_bytes=58 << 20
        ),
        cost_estimate=pl.CostEstimate(
            flops=8 << 30, bytes_accessed=6 << 20, transcendentals=1 << 18
        ),
        name="attention_backward",
    )(exps, buckets, lows, maxima, totals, query256, grad256, mixed_t, keys_values, *carried)


def arrange_kernel(half_rows, query_rows, plane_ref, *refs):
    block_refs, out_ref, rows_ref = refs[:4], refs[4], refs[5]
    rows_ref[...] = jnp.zeros(rows_ref.shape, F32)
    for distance in range(4):
        plane = plane_ref[0] ^ distance
        block = block_refs[distance][...].astype(F32)
        start = pl.multiple_of(plane * half_rows, half_rows)
        rows_ref[pl.ds(start, half_rows), 64:256] = block[:half_rows, 0:192]
        start = pl.multiple_of((7 - plane) * half_rows, half_rows)
        rows_ref[pl.ds(start, half_rows), 64:256] = block[:half_rows, 192:384]
        start = pl.multiple_of(8 * half_rows + plane * query_rows, 8)
        rows_ref[pl.ds(start, query_rows), 64:256] = block[half_rows:, 0:192]
    out_ref[...] = rows_ref[...].astype(BF16)


def arrange_rows(blocks, plane, half_rows, query_rows):
    return pl.pallas_call(
        functools.partial(arrange_kernel, half_rows, query_rows),
        in_specs=[pl.BlockSpec(memory_space=pltpu.SMEM)]
        + [pl.BlockSpec(memory_space=pltpu.VMEM)] * 4,
        out_specs=pl.BlockSpec(memory_space=pltpu.VMEM),
        out_shape=jax.ShapeDtypeStruct((ROWS, 256), BF16),
        scratch_shapes=[pltpu.VMEM((ROWS, 256), F32)],
        name="arrange_rows",
    )(plane[None], *blocks)


def widen_kernel(group, order_ref, near_ref, far_ref, *out_refs):
    step = pl.program_id(0) ^ (order_ref[0] // group)
    half_steps = pl.num_programs(0) // 2
    inner = order_ref[0] % group

    def from_pieces(pieces_ref):
        rows = pieces_ref.shape[-2]
        for k in range(group):
            start = 0
            for out_ref in out_refs:
                columns = out_ref.shape[-1]
                lanes = slice(start, start + columns)
                if len(pieces_ref.shape) == 4:
                    for s in range(2):
                        block = pieces_ref[k ^ inner, s ^ order_ref[1], :, lanes]
                        out_ref[s, k * rows : (k + 1) * rows, :] = block.astype(F32)
                else:
                    block = pieces_ref[k ^ inner, :, lanes]
                    out_ref[k * rows : (k + 1) * rows, :] = block.astype(F32)
                start += columns

    pl.when(step < half_steps)(lambda: from_pieces(near_ref))
    pl.when(step >= half_steps)(lambda: from_pieces(far_ref))


def widen_rows(near, far, order, columns):
    half, rows, width = near.shape[0], near.shape[-2], near.shape[-1]
    sides = near.shape[1:-2]
    group = min(4, half)
    if rows % 16 != 0:
        pieces = jnp.concatenate([near, far], axis=0)
        position = jnp.arange(2 * half, dtype=jnp.int32) ^ order[0]
        whole = jnp.take(pieces, position, axis=0).astype(F32)
        if sides:
            whole = jnp.swapaxes(jnp.where(order[1] == 1, whole[:, ::-1], whole), 0, 1)
        whole = whole.reshape(sides + (2 * half * rows, width))
        ends = [sum(columns[: i + 1]) for i in range(len(columns))]
        return [whole[..., end - c : end] for end, c in zip(ends, columns)]
    zeros = (0,) * (len(sides) + 2)
    half_steps = half // group

    def piece_map(part):
        def index(r, o):
            order_step = o[0] // group
            first = jnp.where(order_step >= half_steps, 1 - part, part) * half_steps
            inside = jnp.clip(r, first, first + half_steps - 1)
            return ((inside ^ order_step) % half_steps,) + zeros

        return index

    def out_map(r, o):
        return (0,) * len(sides) + (r, 0)

    return pl.pallas_call(
        functools.partial(widen_kernel, group),
        grid_spec=pltpu.PrefetchScalarGridSpec(
            num_scalar_prefetch=1,
            grid=(2 * half_steps,),
            in_specs=[pl.BlockSpec((group,) + near.shape[1:], piece_map(part)) for part in range(2)],
            out_specs=[pl.BlockSpec(sides + (group * rows, c), out_map) for c in columns],
        ),
        out_shape=[jax.ShapeDtypeStruct(sides + (2 * half * rows, c), F32) for c in columns],
        compiler_params=pltpu.CompilerParams(
            dimension_semantics=("arbitrary",), vmem_limit_bytes=24 << 20
        ),
        cost_estimate=pl.CostEstimate(
            flops=0, bytes_accessed=6 * near.size * 2, transcendentals=0
        ),
        name="widen_rows",
    )(order, near, far)


def widen_heads_kernel(order_ref, pieces_ref, *out_refs):
    odd = order_ref[1] == 1
    first, second = pieces_ref[0, 0], pieces_ref[0, 1]
    low = jnp.where(odd, second.astype(F32), first.astype(F32))
    high = jnp.where(odd, first.astype(F32), second.astype(F32))
    size = low.shape[1] // 3
    for i, out_ref in enumerate(out_refs):
        lanes = slice(i * size, (i + 1) * size)
        out_ref[...] = jnp.concatenate([low[:, lanes], high[:, lanes]], axis=1)


def widen_heads(pieces, order, odd):
    count, _, rows, width = pieces.shape
    columns = 2 * width // 3
    return pl.pallas_call(
        widen_heads_kernel,
        grid_spec=pltpu.PrefetchScalarGridSpec(
            num_scalar_prefetch=1,
            grid=(count,),
            in_specs=[pl.BlockSpec((1, 2, rows, width), lambda r, o: (r ^ o[0], 0, 0, 0))],
            out_specs=[pl.BlockSpec((rows, columns), lambda r, o: (r, 0))] * 3,
        ),
        out_shape=[jax.ShapeDtypeStruct((count * rows, columns), F32)] * 3,
        compiler_params=pltpu.CompilerParams(dimension_semantics=("arbitrary",)),
        cost_estimate=pl.CostEstimate(
            flops=0, bytes_accessed=12 * count * rows * width, transcendentals=0
        ),
        name="widen_heads",
    )(jnp.stack([order, odd]), pieces)


def pack_kernel(*refs):
    out_ref = refs[-1]
    rows = [ref[...].reshape(1, -1).astype(F32) for ref in refs[:8]]
    out_ref[...] = jnp.zeros(out_ref.shape, BF16)
    out_ref[0:8, :] = jnp.concatenate(rows, axis=0).astype(BF16)
    table = refs[8][...].astype(F32)
    lanes = jnp.zeros((table.shape[0], 128 - table.shape[1]), F32)
    out_ref[16:32, 0:128] = jnp.concatenate([table, lanes], axis=1).astype(BF16)


def pack_vectors(vectors, table):
    vmem = pl.BlockSpec(memory_space=pltpu.VMEM)
    return pl.pallas_call(
        pack_kernel,
        in_specs=[vmem] * 9,
        out_specs=vmem,
        out_shape=jax.ShapeDtypeStruct((32, vectors[0].shape[0]), BF16),
        name="pack_vectors",
    )(*vectors, table)


def unpack_kernel(heads, where_ref, own_ref, other_ref, full_ref, bias_ref, table_ref, turned_ref):
    side = where_ref[0] == 1
    own, other = own_ref[...].astype(F32), other_ref[...].astype(F32)
    low, high = jnp.where(side, other, own), jnp.where(side, own, other)
    full = jnp.concatenate([low[0:8], high[0:8]], axis=1)
    full_ref[...] = full
    both = jnp.concatenate([low[16:32, 0:128], high[16:32, 0:128]], axis=0)
    square = jnp.concatenate([both, jnp.zeros((96, 128), F32)], axis=0)
    turned_ref[...] = square.T
    bias_ref[...] = jnp.zeros(bias_ref.shape, F32)
    table_ref[...] = jnp.zeros(table_ref.shape, F32)
    for plane in range(4):

        @pl.when(where_ref[1] == plane)
        def _(plane=plane):
            lanes = slice(192 * plane, 192 * plane + 192)
            bias_ref[0:1, 0:192] = full[0:1, lanes]
            bias_ref[1:2, 192:384] = full[1:2, lanes]
            table_ref[0:heads, :] = turned_ref[heads * plane : heads * plane + heads, :]


def unpack_vectors(own, other, side, plane, heads):
    vmem = pl.BlockSpec(memory_space=pltpu.VMEM)
    half = own.shape[1]
    return pl.pallas_call(
        functools.partial(unpack_kernel, heads),
        in_specs=[pl.BlockSpec(memory_space=pltpu.SMEM)] + [vmem] * 2,
        out_specs=[vmem] * 3,
        out_shape=[
            jax.ShapeDtypeStruct((8, 2 * half), F32),
            jax.ShapeDtypeStruct((8, half), F32),
            jax.ShapeDtypeStruct((8, 128), F32),
        ],
        scratch_shapes=[pltpu.VMEM((128, 128), F32)],
        name="unpack_vectors",
    )(jnp.stack([side, plane]), own, other)


def after(value, *earlier):
    return lax.optimization_barrier((value,) + earlier)[0]


def row_major(value):
    return with_layout_constraint(value, Layout(major_to_minor=tuple(range(value.ndim))))


class Chain:
    def __init__(self, state, stages):
        self.state, self.stages = state, stages
        self.leave()

    def leave(self):
        if self.stages:
            self.sent, self.kept = self.stages[0][0](self.state)
            self.arrived = self.stages[0][1](self.sent)

    def advance(self, token):
        kept = jax.tree.map(lambda leaf: after(leaf, token), self.kept)
        self.state = self.stages[0][2](kept, self.arrived)
        self.stages = self.stages[1:]
        self.leave()
        return self.sent if self.stages else jax.tree.leaves(self.state)[0]

    def drain(self, token):
        while self.stages:
            token = self.advance(token)
        return token


def reverse_bits(value, count):
    result = jnp.zeros_like(value)
    bit, mirrored = 1, count // 2
    while bit < count:
        result = result + jnp.where((value & bit) != 0, mirrored, 0)
        bit, mirrored = bit * 2, mirrored // 2
    return result


def body(
    content,
    query_stream,
    token_order,
    targets,
    query_weight,
    key_weight,
    value_weight,
    output_weight,
    query_bias,
    value_bias,
    output_bias,
    bias_table,
    first_gain,
    first_shift,
    inner_weight,
    inner_bias,
    outer_weight,
    outer_bias,
    second_gain,
    second_shift,
    content_cotangent,
    query_cotangent,
):
    ctx = lax.axis_size("ctx")
    index = lax.axis_index("ctx")
    side = lax.axis_index("wt")
    members = ctx // 4
    plane = index // members
    member = index % members
    half_rows = content.shape[2]
    tok_rows = 2 * half_rows
    query_rows = query_stream.shape[1]
    rows_dev = tok_rows + query_rows
    width = content.shape[3]
    heads = bias_table.shape[1]
    my_heads = heads // 4
    head_width = my_heads * (width // heads)
    half_width = width // 2
    seq_length = tok_rows * ctx
    half_length = seq_length // 2
    order_row = token_order[0]
    target_row = targets[0]
    core_bit = (index & 1) == 1

    def swap(value, bit):
        return lax.ppermute(value, "ctx", [(i, i ^ bit) for i in range(ctx)])

    def swap_side(value):
        return lax.ppermute(value, "wt", [(0, 1), (1, 0)])

    def order_two(flag, mine, other, axis):
        low = jnp.where(flag, other, mine)
        high = jnp.where(flag, mine, other)
        return jnp.concatenate([low, high], axis=axis)

    def half_of_core(value):
        rows = value.shape[0] // 2
        return lax.dynamic_slice_in_dim(value, (index & 1) * rows, rows, 0)

    def both_cores(arrived):
        return order_two(core_bit, arrived, swap(arrived, 1), 0)

    def by_distance(blocks):
        flag = (plane & 1) == 1
        blocks = [jnp.where(flag, blocks[d ^ 1], blocks[d]) for d in range(4)]
        flag = (plane & 2) == 2
        return [jnp.where(flag, blocks[d ^ 2], blocks[d]) for d in range(4)]

    def exchange_planes(blocks):
        sent = by_distance(blocks)
        arrived = [sent[0]] + [swap(sent[d], d * members) for d in range(1, 4)]
        return by_distance(arrived)

    def pack_rows(rows):
        top = jnp.concatenate([rows[:half_rows], rows[half_rows:tok_rows]], axis=1)
        bottom = jnp.concatenate([rows[tok_rows:], jnp.zeros_like(rows[tok_rows:])], axis=1)
        return jnp.concatenate([top, bottom], axis=0)

    def unpack_rows(packed):
        return jnp.concatenate(
            [
                packed[:half_rows, :head_width],
                packed[:half_rows, head_width:],
                packed[half_rows:, :head_width],
            ],
            axis=0,
        )

    def plane_rows(blocks):
        pad = ROWS - 4 * rows_dev
        return jnp.concatenate(
            [blocks[d][:half_rows] for d in range(4)]
            + [blocks[3 - d][half_rows:tok_rows] for d in range(4)]
            + [blocks[d][tok_rows:] for d in range(4)]
            + [jnp.zeros((pad, blocks[0].shape[1]), blocks[0].dtype)],
            axis=0,
        )

    def split_rows(rows):
        blocks = []
        for d in range(4):
            parts = [
                rows[d * half_rows : (d + 1) * half_rows],
                rows[(7 - d) * half_rows : (8 - d) * half_rows],
            ]
            if rows.shape[0] > 4 * tok_rows:
                start = 4 * tok_rows + d * query_rows
                parts.append(rows[start : start + query_rows])
            blocks.append(jnp.concatenate(parts, axis=0))
        return blocks

    local_content = content[0].reshape(tok_rows, width)
    stacked = jnp.concatenate([local_content, query_stream[0]], axis=0)
    arrived_rows = [stacked] + [swap(stacked, d * members) for d in range(1, 4)]
    owner = plane // 2
    odd_plane = (plane & 1) == 1
    side_flag = side == 1
    shards = [query_weight, key_weight, value_weight]
    near_own = jnp.concatenate(
        [jnp.where(odd_plane, s[:, head_width:], s[:, :head_width]) for s in shards], axis=1
    )
    near_sent = half_of_core(near_own)
    near_other = both_cores(swap_side(near_sent))
    vectors = [
        query_bias,
        value_bias,
        output_bias,
        first_gain,
        first_shift,
        outer_bias,
        second_gain,
        second_shift,
    ]
    own_vectors = pack_vectors(vectors, bias_table)
    other_vectors = swap_side(own_vectors)
    full_vectors, head_bias, tables = unpack_vectors(
        own_vectors, other_vectors, side, plane, my_heads
    )
    (
        full_output_bias,
        full_first_gain,
        full_first_shift,
        full_outer_bias,
        full_second_gain,
        full_second_shift,
    ) = [full_vectors[i : i + 1] for i in range(2, 8)]
    buckets = 2 * bias_table.shape[0]

    places = jnp.arange(half_length, dtype=jnp.int32)
    key_place = jnp.concatenate(
        [places, (seq_length - 1 - places).reshape(4, -1)[::-1].reshape(-1)]
    )
    key_anchor = jnp.concatenate(
        [
            order_row[:half_length],
            order_row[half_length:][::-1].reshape(4, -1)[::-1].reshape(-1),
        ]
    )

    def of_member(array, count):
        return lax.dynamic_index_in_dim(
            array.reshape(-1, members, count), member, 1, keepdims=False
        ).reshape(-1)

    def by_member_distance(array):
        pieces = [array.reshape(8, members, -1)]
        bit = members // 2
        while bit >= 1:
            flag = (member & bit) != 0
            split = []
            for piece in pieces:
                size = piece.shape[1] // 2
                low, high = piece[:, :size], piece[:, size:]
                split.append(jnp.where(flag, high, low))
                split.append(jnp.where(flag, low, high))
            pieces = split
            bit //= 2
        return jnp.concatenate(pieces, axis=1)

    plane_targets = of_member(target_row, query_rows)
    target_anchor = jnp.sum(
        jnp.where(
            jnp.arange(seq_length, dtype=jnp.int32)[:, None] == plane_targets[None],
            order_row[:, None],
            0,
        ),
        axis=0,
    )
    pad_rows = ROWS - 4 * rows_dev
    row_anchor = jnp.concatenate(
        [of_member(key_anchor, half_rows), target_anchor, jnp.zeros((pad_rows,), jnp.int32)]
    )
    row_limit = jnp.concatenate(
        [
            of_member(key_place, half_rows) + 1,
            plane_targets,
            jnp.ones((pad_rows,), jnp.int32),
        ]
    )
    row_info = jnp.concatenate(
        [row_anchor[None], row_limit[None], jnp.zeros((6, ROWS), jnp.int32)], axis=0
    )

    def by_tile(array):
        parts = by_member_distance(array).reshape(4, 2, members // 2, 2, -1)
        return jnp.transpose(parts, (0, 2, 3, 1, 4)).reshape(-1)

    near_anchor = by_tile(key_anchor)
    key_anchor_wide = jnp.broadcast_to(near_anchor[:, None], (seq_length, 128))
    block_places = by_tile(key_place.reshape(-1, half_rows)[:, 0])
    head_weights = jnp.where(side == owner, near_own, near_other)
    plane_x = plane_rows(by_distance(arrived_rows))
    plane_kv = (
        dot(plane_x[: 4 * tok_rows], head_weights[:, head_width:]) + head_bias[1:2]
    ).astype(BF16)
    first_kv = plane_kv.reshape(1, 8, half_rows, 2 * head_width)
    far_kv = swap(first_kv, members // 2)
    bit = 1
    near_members = first_kv
    while bit < members // 2:
        near_members = jnp.concatenate([near_members, swap(near_members, bit)], axis=0)
        bit *= 2
    query_weights = jnp.pad(head_weights[:, :head_width], ((0, 0), (0, 256 - head_width)))
    query256 = ((dot(plane_x, query_weights) + head_bias[0:1, :256]) * 0.125).astype(BF16)

    output_early, outer_early, rest_own = lax.optimization_barrier(
        (
            output_weight,
            outer_weight,
            jnp.concatenate(
                [
                    jnp.where(odd_plane, s[:, :head_width], s[:, head_width:])
                    for s in lax.optimization_barrier(tuple(shards) + (plane_kv,))[:3]
                ],
                axis=1,
            ),
            query256,
        )
    )[:3]
    hidden_half = outer_weight.shape[0] // 2

    outer_sent = lax.dynamic_slice_in_dim(outer_early, (1 - side) * hidden_half, hidden_half, 0)
    output_arrived = swap_side(half_of_core(output_early))
    outer_arrived_half = swap_side(half_of_core(outer_sent))
    rest_arrived = swap_side(half_of_core(rest_own))

    forward_info = (key_anchor_wide, block_places, row_info, tables)
    first_half = attention_forward(0, query256, near_members, *forward_info, (), my_heads)
    far_members = far_kv
    bit = 1
    while bit < members // 2:
        far_members = jnp.concatenate([far_members, swap(far_members, bit)], axis=0)
        bit *= 2
    exps, bucket_ids, bucket_lows, maxima, _, _, mixed_t, mixed_plane, totals = attention_forward(
        1, query256, far_members, *forward_info, first_half, my_heads
    )
    keys_values = jnp.concatenate([near_members, far_members], axis=0)

    full_output = order_two(side_flag, output_weight, both_cores(after(output_arrived, mixed_plane)), 1)
    outer_kept = lax.dynamic_slice_in_dim(outer_weight, side * hidden_half, hidden_half, 0)
    outer_rows = order_two(side_flag, outer_kept, both_cores(after(outer_arrived_half, mixed_plane)), 1)
    rest_other = both_cores(after(rest_arrived, mixed_plane))
    full_qkv = []
    for i in range(3):
        lanes = slice(i * head_width, (i + 1) * head_width)
        other = order_two(odd_plane, near_other[:, lanes], rest_other[:, lanes], 1)
        full_qkv.append(order_two(side_flag, shards[i], other, 1))

    mixed_blocks = exchange_planes([pack_rows(block) for block in split_rows(mixed_plane)])
    mixed = jnp.concatenate([unpack_rows(block) for block in mixed_blocks], axis=1)
    branch = dot(mixed, full_output) + full_output_bias
    first_norm, first_back = jax.vjp(
        norm_of_sum, stacked.astype(F32), branch, full_first_gain, full_first_shift
    )
    first_low = first_norm.astype(BF16)
    both_first = jnp.concatenate([first_low, swap_side(first_low)], axis=0)
    inner_value = dot(both_first, inner_weight) + inner_bias.astype(F32)
    hidden_value, gelu_back = jax.vjp(gelu_exact, inner_value)
    hidden_low = hidden_value.astype(BF16)
    outer_part = dot(hidden_low, outer_rows)
    outer_arrived = swap_side(outer_part[rows_dev:].astype(BF16))
    outer_value = outer_part[:rows_dev] + outer_arrived.astype(F32) + full_outer_bias
    final_norm, second_back = jax.vjp(
        norm_of_sum, first_norm, outer_value, full_second_gain, full_second_shift
    )
    content_result = final_norm[:tok_rows].reshape(1, 2, half_rows, width).astype(BF16)
    query_result = final_norm[tok_rows:].reshape(1, query_rows, width).astype(BF16)
    cotangent = jnp.concatenate(
        [content_cotangent[0].reshape(tok_rows, width), query_cotangent[0]], axis=0
    )
    rest_grad, outer_grad, second_gain_grad, second_shift_grad = second_back(cotangent.astype(F32))
    outer_low = outer_grad.astype(BF16)
    both_outer = jnp.concatenate([outer_low, swap_side(outer_low)], axis=0)
    (inner_grad,) = gelu_back(times_transpose(both_outer, outer_rows))
    inner_low = inner_grad.astype(BF16)
    first_part = times_transpose(inner_low, inner_weight)
    first_arrived = swap_side(first_part[rows_dev:].astype(BF16))
    first_grad = rest_grad + (first_part[:rows_dev] + first_arrived.astype(F32))
    row_grad, branch_grad, first_gain_grad, first_shift_grad = first_back(first_grad)
    branch_low = branch_grad.astype(BF16)
    mixed_low = times_transpose(branch_low, full_output).astype(BF16)

    def to(bit):
        return lambda value: swap(value, bit)

    def leave_half(bit):
        def leave(parts):
            rows = parts[0].shape[0] // 2
            upper = jnp.where((index & bit) != 0, 1, 0)
            sent = [
                lax.dynamic_slice_in_dim(part, (1 - upper) * rows, rows, 0).astype(BF16)
                for part in parts
            ]
            return jnp.concatenate(sent, axis=1), parts

        return leave

    def add_half(bit):
        def add(parts, arrived):
            rows = parts[0].shape[0] // 2
            upper = jnp.where((index & bit) != 0, 1, 0)
            kept = [lax.dynamic_slice_in_dim(part, upper * rows, rows, 0) for part in parts]
            return [jnp.concatenate(kept, axis=1) + arrived.astype(F32)]

        return add

    def keep_all(state):
        return state, state

    def append(kept, arrived):
        return jnp.concatenate([kept, arrived], axis=0)

    bits = []
    bit = 1
    while bit < ctx:
        bits.append(bit)
        bit *= 2
    sum_stages = [(leave_half(bit), to(bit), add_half(bit)) for bit in bits]
    gather_stages = [(keep_all, to(bit), append) for bit in bits[::-1]]

    def leave_columns(parts):
        piece = parts[0].astype(BF16)
        left, right = piece[:, :half_width], piece[:, half_width:]
        return jnp.where(side_flag, left, right), jnp.where(side_flag, right, left)

    def pair_sides(kept, arrived):
        return jnp.stack([kept, arrived], axis=0)[None]

    def start_gather(parts):
        state = parts[0].astype(BF16)[None]
        return state, state

    outer_chain = Chain(
        [contract_rows(hidden_low, both_outer)],
        sum_stages + [(leave_columns, swap_side, pair_sides)] + gather_stages[:-1],
    )

    other_mixed = swap_side(mixed)
    branch_left, branch_right = branch_low[:, :half_width], branch_low[:, half_width:]
    branch_kept = jnp.where(side_flag, branch_right, branch_left)
    inner_part = contract_rows(both_first, inner_low)
    branch_arrived = swap_side(jnp.where(side_flag, branch_left, branch_right))
    output_part = contract_rows(mixed, branch_kept) + contract_rows(other_mixed, branch_arrived)
    joined_chain = Chain(
        [inner_part, output_part],
        sum_stages + [(start_gather, to(bits[-1]), append)] + gather_stages[1:-1],
    )

    token = outer_chain.advance(branch_low)
    grad_sent = by_distance(
        [
            pack_rows(mixed_low[:, d * head_width : (d + 1) * head_width])
            for d in range(4)
        ]
    )
    grad_sent = lax.optimization_barrier(tuple(grad_sent) + (token,))[:4]
    grad_blocks = [grad_sent[0]] + [swap(grad_sent[d], d * members) for d in range(1, 4)]
    grad256 = arrange_rows(grad_blocks, plane, half_rows, query_rows)
    saved = (exps, bucket_ids, bucket_lows, maxima, totals)
    carried = None
    for call in range(4):
        if call == 0:
            token = outer_chain.advance(grad256)
            token = joined_chain.advance(token)
            grad256 = after(grad256, token)
        else:
            token = outer_chain.advance(carried[0])
            if call > 1:
                token = joined_chain.advance(token)
            carried = (after(carried[0], token),) + carried[1:]
        carried = tuple(
            attention_backward(
                call, saved, query256, grad256, mixed_t, keys_values, carried, my_heads
            )
        )
    dquery_t, table_part, dkv = carried
    query_scaled = dquery_t.T.astype(BF16) * 0.125

    member_bits = [bit for bit in bits if bit < members]

    def leave_members(state):
        pairs = state.reshape((-1, 2) + state.shape[1:])
        return row_major(pairs[:, 1].astype(BF16)), state

    def add_members(state, arrived):
        pairs = state.reshape((-1, 2) + state.shape[1:])
        return row_major(pairs[:, 0] + arrived.astype(F32))

    kv_chain = Chain(
        dkv,
        [(leave_members, to(bit), add_members) for bit in member_bits],
    )
    token = joined_chain.advance(kv_chain.sent)
    token = kv_chain.advance(token)
    token = outer_chain.advance(token)
    token = joined_chain.advance(token)
    token = kv_chain.drain(token)
    kv_low = kv_chain.state.reshape(4 * tok_rows, 2 * head_width).astype(BF16)

    low_parts = jnp.concatenate(
        [query_scaled, jnp.pad(kv_low, ((0, ROWS - 4 * tok_rows), (0, 0)))], axis=1
    )

    def leave_same(parts):
        return parts[0].astype(BF16), parts

    def add_side(kept, arrived):
        return (kept[0] + arrived.astype(F32)).astype(BF16)

    def choose_owner(kept, arrived):
        return jnp.where(owner == side, kept, arrived)[None]

    def append_plane(kept, arrived):
        return jnp.concatenate([kept, arrived], axis=0)[None]

    heads_chain = Chain(
        [contract_rows(plane_x, low_parts)],
        sum_stages[: len(member_bits)]
        + [
            (leave_same, swap_side, add_side),
            (keep_all, to(2 * members), choose_owner),
            (keep_all, to(members), append_plane),
        ]
        + [(keep_all, to(bit), append) for bit in member_bits[::-1]],
    )

    sent_blocks = [
        jnp.concatenate([pack_rows(query_block), kv_block], axis=0)
        for query_block, kv_block in zip(split_rows(query_scaled), split_rows(kv_low))
    ]
    sent_distance = by_distance(sent_blocks)
    sent_distance = lax.optimization_barrier(tuple(sent_distance) + (heads_chain.sent,))[:4]
    got_distance = [sent_distance[0]] + [
        swap(sent_distance[d], d * members) for d in range(1, 4)
    ]
    full_query, full_key, full_value = full_qkv

    blocks = table_part.reshape(8, GROUP, 4, my_heads, GROUP)
    same = jnp.eye(GROUP, dtype=F32)[None, :, None, None, :]
    table_cumulative = jnp.sum(blocks * same, axis=(1, 4))
    table_grad = table_cumulative - jnp.concatenate(
        [table_cumulative[1:], jnp.zeros_like(table_cumulative[:1])], axis=0
    )
    table_grad = table_grad.reshape(buckets, my_heads)

    def at_plane(values, axis):
        return jnp.concatenate(
            [jnp.where(plane == d, values, jnp.zeros_like(values)) for d in range(4)], axis=axis
        )

    inner_bias_part = jnp.sum(inner_low.astype(F32), axis=0)
    inner_bias_zero = jnp.zeros_like(inner_bias_part)
    late_small = jnp.concatenate(
        [
            at_plane(jnp.sum(query_scaled.astype(F32), axis=0), 0),
            at_plane(jnp.sum(kv_low[:, head_width:].astype(F32), axis=0), 0),
            jnp.sum(branch_low.astype(F32), axis=0),
            first_gain_grad.reshape(-1),
            first_shift_grad.reshape(-1),
            jnp.sum(outer_low.astype(F32), axis=0),
            second_gain_grad.reshape(-1),
            second_shift_grad.reshape(-1),
            jnp.where(side_flag, inner_bias_zero, inner_bias_part),
            jnp.where(side_flag, inner_bias_part, inner_bias_zero),
            at_plane(table_grad, 1).reshape(-1),
        ]
    )
    late_length = late_small.shape[0]
    late_small = jnp.pad(late_small, (0, -late_length % 1024)).reshape(-1, 128)

    def add_plain(kept, arrived):
        return kept + arrived

    late_chain = Chain(
        after(late_small, heads_chain.sent),
        [(keep_all, to(bit), add_plain) for bit in bits] + [(keep_all, swap_side, add_plain)],
    )

    token = heads_chain.advance(late_chain.sent)
    token = late_chain.advance(token)
    token = joined_chain.advance(token)
    token = heads_chain.advance(token)
    token = outer_chain.advance(token)
    token = late_chain.advance(token)
    token = heads_chain.advance(token)
    got_distance = lax.optimization_barrier(tuple(got_distance) + (token,))[:4]
    got_blocks = by_distance(got_distance)
    packed_rows = half_rows + query_rows
    own_query = jnp.concatenate([unpack_rows(b[:packed_rows]) for b in got_blocks], axis=1)
    own_key = jnp.concatenate([b[packed_rows:, :head_width] for b in got_blocks], axis=1)
    own_value = jnp.concatenate([b[packed_rows:, head_width:] for b in got_blocks], axis=1)
    input_grad = row_grad + times_transpose(own_query, full_query)
    content_extra = times_transpose(own_key, full_key) + times_transpose(own_value, full_value)
    content_gradient = (input_grad[:tok_rows] + content_extra).reshape(1, 2, half_rows, width)
    query_gradient = input_grad[tok_rows:].reshape(1, query_rows, width)
    token = joined_chain.advance(content_gradient)
    token = late_chain.advance(token)
    token = heads_chain.advance(token)
    token = outer_chain.advance(token)
    token = late_chain.advance(token)
    token = heads_chain.advance(token)
    token = late_chain.drain(token)
    token = outer_chain.drain(token)
    outer_near, outer_far = outer_chain.state, swap(outer_chain.state, 1)
    token = joined_chain.drain(token)
    token = heads_chain.drain(token)
    row_order = jnp.stack([reverse_bits(index, ctx), side])
    joined_pieces = joined_chain.state
    outer_weight_grad = widen_rows(
        outer_near, outer_far, row_order, (half_width,)
    )[0].reshape(2 * hidden_half, half_width)
    inner_weight_grad, output_weight_grad = widen_rows(
        joined_pieces, swap(joined_pieces, 1), row_order, (hidden_half, half_width)
    )
    qkv_grads = widen_heads(heads_chain.state, reverse_bits(member, members), plane & 1)

    late_small = late_chain.state.reshape(-1)[:late_length]
    table_start = 8 * width + 2 * hidden_half
    table_all = late_small[table_start:].reshape(2, buckets // 2, heads)
    bias_table_grad = jnp.where(side_flag, table_all[1], table_all[0])

    def my_half(start, size):
        low = late_small[start : start + size]
        return jnp.where(side_flag, late_small[start + size : start + 2 * size], low)

    mine = [my_half(i * width, half_width) for i in range(8)]
    inner_bias_grad = my_half(8 * width, hidden_half)

    return (
        content_result,
        query_result,
        content_gradient,
        query_gradient,
        qkv_grads[0],
        qkv_grads[1],
        qkv_grads[2],
        output_weight_grad,
        mine[0],
        mine[1],
        mine[2],
        bias_table_grad,
        mine[3],
        mine[4],
        inner_weight_grad,
        inner_bias_grad,
        outer_weight_grad,
        mine[5],
        mine[6],
        mine[7],
    )


def solution(mesh):
    return jax.shard_map(
        body,
        mesh=mesh,
        in_specs=(
            P("wt", None, "ctx", None),
            P("wt", "ctx", None),
            P("wt", None),
            P("wt", None),
            P(None, "wt"),
            P(None, "wt"),
            P(None, "wt"),
            P(None, "wt"),
            P("wt"),
            P("wt"),
            P("wt"),
            P("wt", None),
            P("wt"),
            P("wt"),
            P(None, "wt"),
            P("wt"),
            P(None, "wt"),
            P("wt"),
            P("wt"),
            P("wt"),
            P("wt", None, "ctx", None),
            P("wt", "ctx", None),
        ),
        out_specs=(
            P("wt", None, "ctx", None),
            P("wt", "ctx", None),
            P("wt", None, "ctx", None),
            P("wt", "ctx", None),
            P(None, "wt"),
            P(None, "wt"),
            P(None, "wt"),
            P(None, "wt"),
            P("wt"),
            P("wt"),
            P("wt"),
            P("wt", None),
            P("wt"),
            P("wt"),
            P(None, "wt"),
            P("wt"),
            P(None, "wt"),
            P("wt"),
            P("wt"),
            P("wt"),
        ),
        check_vma=False,
    )
```

```python
import functools

import jax
import jax.numpy as jnp
from jax import lax
from jax.experimental import pallas as pl
from jax.experimental.layout import Layout, with_layout_constraint
from jax.experimental.pallas import tpu as pltpu
from jax.sharding import PartitionSpec as P

BF16 = jnp.bfloat16
F32 = jnp.float32
FAR_EDGES = (12, 16, 23, 32, 46, 64, 91)
NEGATIVE = -1e30
TILE = 256
ROWS = 640
GROUP = 16
GAPS = ['O', 'OJ', 'O', 'OJ', 'OJ']
TAIL = 'KJOK|HLHJOHXLJHLOHLBLHAC'


def layer_norm(hidden_rows, gain_row, shift_row):
    average = jnp.mean(hidden_rows, axis=-1, keepdims=True)
    centered = hidden_rows - average
    variance = jnp.mean(centered * centered, axis=-1, keepdims=True)
    return centered * lax.rsqrt(variance + 1e-05) * gain_row + shift_row


def norm_of_sum(residual, branch_value, gain_row, shift_row):
    return layer_norm(residual + branch_value, gain_row, shift_row)


def gelu_exact(values):
    return jax.nn.gelu(values, approximate=False)


def dot(left, right):
    return jnp.dot(left, right, preferred_element_type=F32)


def contract_rows(left, right):
    return lax.dot_general(left, right, (((0,), (0,)), ((), ())), preferred_element_type=F32)


def times_transpose(left, right):
    return lax.dot_general(left, right, (((1,), (1,)), ((), ())), preferred_element_type=F32)


def transpose_low(block):
    return block.astype(F32).T.astype(BF16)


def tile_branches(branch_index, process):
    for branch in range(4):
        pl.when(branch_index == branch)(functools.partial(process, 128 * branch))


def forward_kernel(call, count, heads, *refs):
    place_ref, query_ref, kv_ref, anchor_ref, row_ref, table_ref = refs[:6]
    refs = refs[6:]
    if call == 1:
        max_in, sum_in, mixed_in = refs[4:7]
        refs = refs[7:]
    exp_ref, bucket_ref, low_ref, max_ref, run_max, run_sum, mixed_t_ref = refs[:7]
    refs = refs[7:]
    if call == 1:
        mixed_ref, total_ref = refs[:2]
        refs = refs[2:]
    query_z, prob_ref, scale_ref = refs
    step = pl.program_id(0)
    branch_index = step // count
    tile_index = branch_index * (2 * count) + call * count + step % count

    @pl.when(step == 0)
    def _():
        query_t = transpose_low(query_ref[...])
        part = lax.broadcasted_iota(jnp.int32, (256, ROWS), 0) // 64
        for head in range(heads):
            query_z[head] = jnp.where(part == head, query_t.astype(F32), 0.0).astype(BF16)
        if call == 0:
            run_max[...] = jnp.full(run_max.shape, NEGATIVE, F32)
            run_sum[...] = jnp.zeros(run_sum.shape, F32)
            mixed_t_ref[...] = jnp.zeros(mixed_t_ref.shape, F32)
        else:
            run_max[...] = max_in[...]
            run_sum[...] = sum_in[...]
            mixed_t_ref[...] = mixed_in[...]

    place_sign = jnp.where(branch_index < 2, 1, -1)
    keys_values = kv_ref[...].reshape(TILE, 384)
    value_t = transpose_low(keys_values[:, 128:384])

    def process(offset):
        chunks = (ROWS - offset) // 128
        for head in range(heads):
            exp_ref[head, :, offset:] = dot(keys_values[:, 0:256], query_z[head, :, offset:])

        def bias_group(group, tops):
            start = pl.multiple_of(group * GROUP, GROUP)
            keys = anchor_ref[pl.ds(start, GROUP), :]
            row = start % 64 + lax.broadcasted_iota(jnp.int32, (GROUP, 128), 0)
            place = place_ref[tile_index * (TILE // 64) + start // 64] + place_sign * row
            new_tops = []
            for chunk in range(chunks):
                lanes = slice(offset + chunk * 128, offset + chunk * 128 + 128)
                relative = keys - row_ref[0:1, lanes]
                magnitude = jnp.abs(relative)
                bucket = jnp.minimum(magnitude, 8)
                for edge in FAR_EDGES:
                    bucket = bucket + jnp.where(magnitude >= edge, 1, 0)
                bucket = bucket + jnp.where(relative > 0, 16, 0)
                bucket_ref[pl.ds(start, GROUP), lanes] = bucket.astype(F32).astype(BF16)
                low_ref[pl.ds(start, GROUP), lanes] = (bucket & 3).astype(F32).astype(BF16)
                allowed = place < row_ref[1:2, lanes]
                for head in range(heads):
                    table = jnp.broadcast_to(table_ref[head : head + 1, :], (8, 128))
                    bias = jnp.concatenate(
                        [
                            jnp.take_along_axis(table, bucket[0:8], axis=1),
                            jnp.take_along_axis(table, bucket[8:16], axis=1),
                        ],
                        axis=0,
                    )
                    scores = exp_ref[head, pl.ds(start, GROUP), lanes] + bias
                    scores = jnp.where(allowed, scores, NEGATIVE)
                    exp_ref[head, pl.ds(start, GROUP), lanes] = scores
                    top = tops[chunk * heads + head]
                    new_tops.append(jnp.maximum(top, jnp.maximum(scores[0:8], scores[8:16])))
            return tuple(new_tops)

        tops = lax.fori_loop(
            0,
            TILE // GROUP,
            bias_group,
            tuple(jnp.full((8, 128), NEGATIVE, F32) for _ in range(chunks * heads)),
            unroll=2,
        )
        for chunk in range(chunks):
            lanes = slice(offset + chunk * 128, offset + chunk * 128 + 128)
            for head in range(heads):
                top = jnp.max(tops[chunk * heads + head], axis=0, keepdims=True)
                old = run_max[head : head + 1, lanes]
                new = jnp.maximum(old, top)
                scale_ref[head : head + 1, lanes] = jnp.exp(old - new)
                run_max[head : head + 1, lanes] = new
        max_ref[0] = run_max[...]

        def exp_group(group, sums):
            start = pl.multiple_of(group * GROUP, GROUP)
            new_sums = []
            for chunk in range(chunks):
                lanes = slice(offset + chunk * 128, offset + chunk * 128 + 128)
                for head in range(heads):
                    terms = jnp.exp(
                        exp_ref[head, pl.ds(start, GROUP), lanes] - run_max[head : head + 1, lanes]
                    )
                    exp_ref[head, pl.ds(start, GROUP), lanes] = terms
                    prob_ref[head, pl.ds(start, GROUP), lanes] = terms.astype(BF16)
                    new_sums.append(sums[chunk * heads + head] + (terms[0:8] + terms[8:16]))
            return tuple(new_sums)

        sums = lax.fori_loop(
            0,
            TILE // GROUP,
            exp_group,
            tuple(jnp.zeros((8, 128), F32) for _ in range(chunks * heads)),
        )
        for chunk in range(chunks):
            lanes = slice(offset + chunk * 128, offset + chunk * 128 + 128)
            for head in range(heads):
                run_sum[head : head + 1, lanes] = run_sum[head : head + 1, lanes] * scale_ref[
                    head : head + 1, lanes
                ] + jnp.sum(sums[chunk * heads + head], axis=0, keepdims=True)
        for head in range(heads):
            rows = slice(64 * head, 64 * head + 64)
            mixed_t_ref[rows, offset:] = mixed_t_ref[rows, offset:] * scale_ref[
                head : head + 1, offset:
            ] + dot(value_t[64 + 64 * head : 128 + 64 * head], prob_ref[head, :, offset:])

    tile_branches(branch_index, process)

    if call == 1:

        @pl.when(step == 4 * count - 1)
        def _():
            for head in range(heads):
                rows = slice(64 * head, 64 * head + 64)
                mixed_t_ref[rows, :] = mixed_t_ref[rows, :] / run_sum[head : head + 1, :]
                total_ref[head : head + 1, :] = run_max[head : head + 1, :] + jnp.log(
                    run_sum[head : head + 1, :]
                )
            mixed_ref[...] = mixed_t_ref[...].T.astype(BF16)


def attention_forward(
    call, query256, keys_values, key_anchor, block_places, row_info, tables, previous, heads
):
    count = keys_values.shape[0] // 2
    tiles = 8 * count
    total_keys = tiles * TILE

    def tile_of(s):
        return (s // count) * (2 * count) + call * count + s % count

    def whole(shape):
        return pl.BlockSpec(shape, lambda s, p: (0,) * len(shape))

    in_specs = [
        whole((ROWS, 256)),
        pl.BlockSpec((2, 2, 64, 384), lambda s, p: (s % count, s // count, 0, 0)),
        pl.BlockSpec((TILE, 128), lambda s, p: (tile_of(s), 0)),
        whole((8, ROWS)),
        whole((8, 128)),
    ]
    out_specs = [
        pl.BlockSpec((heads, TILE, ROWS), lambda s, p: (0, tile_of(s), 0)),
        pl.BlockSpec((TILE, ROWS), lambda s, p: (tile_of(s), 0)),
        pl.BlockSpec((TILE, ROWS), lambda s, p: (tile_of(s), 0)),
        pl.BlockSpec((1, 8, ROWS), lambda s, p: (tile_of(s), 0, 0)),
        whole((8, ROWS)),
        whole((8, ROWS)),
        whole((192, ROWS)),
    ]
    out_shape = [
        jax.ShapeDtypeStruct((heads, total_keys, ROWS), F32),
        jax.ShapeDtypeStruct((total_keys, ROWS), BF16),
        jax.ShapeDtypeStruct((total_keys, ROWS), BF16),
        jax.ShapeDtypeStruct((tiles, 8, ROWS), F32),
        jax.ShapeDtypeStruct((8, ROWS), F32),
        jax.ShapeDtypeStruct((8, ROWS), F32),
        jax.ShapeDtypeStruct((192, ROWS), F32),
    ]
    aliases = {}
    if call == 1:
        in_specs += [pl.BlockSpec(memory_space=pl.ANY)] * 4
        in_specs += [whole((8, ROWS)), whole((8, ROWS)), whole((192, ROWS))]
        out_specs += [whole((ROWS, 192)), whole((8, ROWS))]
        out_shape += [
            jax.ShapeDtypeStruct((ROWS, 192), BF16),
            jax.ShapeDtypeStruct((8, ROWS), F32),
        ]
        aliases = {6: 0, 7: 1, 8: 2, 9: 3}
    return pl.pallas_call(
        functools.partial(forward_kernel, call, count, heads),
        grid_spec=pltpu.PrefetchScalarGridSpec(
            num_scalar_prefetch=1,
            grid=(4 * count,),
            in_specs=in_specs,
            out_specs=out_specs,
            scratch_shapes=[
                pltpu.VMEM((heads, 256, ROWS), BF16),
                pltpu.VMEM((heads, TILE, ROWS), BF16),
                pltpu.VMEM((8, ROWS), F32),
            ],
        ),
        out_shape=out_shape,
        input_output_aliases=aliases,
        compiler_params=pltpu.CompilerParams(
            dimension_semantics=("arbitrary",), vmem_limit_bytes=32 << 20
        ),
        cost_estimate=pl.CostEstimate(
            flops=14 << 30, bytes_accessed=12 << 20, transcendentals=2 << 20
        ),
        name="attention_forward",
    )(block_places, query256, keys_values, key_anchor, row_info, tables, *previous)


def backward_kernel(branch, heads, *refs):
    refs = list(refs)
    if branch > 0:
        del refs[11:13]
    backward_tile(branch, heads, *refs)


def backward_tile(
    branch,
    heads,
    exp_ref,
    bucket_ref,
    low_ref,
    max_ref,
    total_ref,
    query_ref,
    grad_ref,
    mixed_t_ref,
    kv_ref,
    dquery_in,
    dtable_in,
    dquery_ref,
    dtable_ref,
    kept_ref,
    sent_ref,
    grad_z,
    query_n,
    grad_n,
    dprob_ref,
    dscore_ref,
    prob_ref,
    high_hot,
    low_parts,
    delta_ref,
    scale_ref,
):
    tile_index = pl.program_id(0)
    offset = 128 * branch
    chunks = (ROWS - offset) // 128

    @pl.when(tile_index == 0)
    def _():
        grad_t = grad_ref[offset:, :].astype(F32).T
        part = lax.broadcasted_iota(jnp.int32, (256, ROWS - offset), 0) // 64
        lane_part = lax.broadcasted_iota(jnp.int32, (ROWS - offset, 256), 1) // 64
        for head in range(heads):
            grad_z[head, :, offset:] = jnp.where(part == head + 1, grad_t, 0.0).astype(BF16)
            query_n[head, offset:, :] = jnp.where(
                lane_part == head, query_ref[offset:, :].astype(F32), 0.0
            ).astype(BF16)
            grad_n[head, offset:, :] = jnp.where(
                lane_part == head + 1, grad_ref[offset:, :].astype(F32), 0.0
            ).astype(BF16)
            delta_ref[head : head + 1, offset:] = jnp.sum(
                grad_t[64 + 64 * head : 128 + 64 * head]
                * mixed_t_ref[64 * head : 64 * head + 64, offset:],
                axis=0,
                keepdims=True,
            )
        if branch == 0:
            dquery_ref[...] = jnp.zeros(dquery_ref.shape, F32)
            dtable_ref[...] = jnp.zeros(dtable_ref.shape, F32)
        else:
            dquery_ref[...] = dquery_in[...]
            dtable_ref[...] = dtable_in[...]

    keys_values = kv_ref[...].reshape(TILE, 384)
    key_t = transpose_low(keys_values[:, 0:256])
    for head in range(heads):
        dprob_ref[head, :, offset:] = dot(keys_values[:, 128:384], grad_z[head, :, offset:])
        scale_ref[head : head + 1, offset:] = jnp.exp(
            max_ref[0, head : head + 1, offset:] - total_ref[head : head + 1, offset:]
        )

    def build(group, slot):
        start = pl.multiple_of(group * GROUP, GROUP)
        one = jnp.ones((GROUP, 128), BF16)
        zero = jnp.zeros((GROUP, 128), BF16)
        for chunk in range(chunks):
            lanes = slice(offset + chunk * 128, offset + chunk * 128 + 128)
            bucket = bucket_ref[pl.ds(start, GROUP), lanes]
            low = low_ref[pl.ds(start, GROUP), lanes]
            for high in range(8):
                hot = jnp.where(bucket >= jnp.asarray(4 * high, BF16), one, zero)
                high_hot[slot, GROUP * high : GROUP * high + GROUP, lanes] = hot
            matches = [low == jnp.asarray(value, BF16) for value in range(4)]
            for head in range(heads):
                prob = (
                    exp_ref[head, pl.ds(start, GROUP), lanes] * scale_ref[head : head + 1, lanes]
                )
                dscore = prob * (
                    dprob_ref[head, pl.ds(start, GROUP), lanes]
                    - delta_ref[head : head + 1, lanes]
                )
                dscore_low = dscore.astype(BF16)
                prob_ref[head, pl.ds(start, GROUP), lanes] = prob.astype(BF16)
                dscore_ref[head, pl.ds(start, GROUP), lanes] = dscore_low
                for value in range(4):
                    row = GROUP * (value * heads + head)
                    low_parts[slot, row : row + GROUP, lanes] = jnp.where(
                        matches[value], dscore_low, zero
                    )

    def product(slot):
        return times_transpose(high_hot[slot, :, offset:], low_parts[slot, :, offset:])

    groups = TILE // GROUP
    build(0, 0)
    build(1, 1)

    def step(index, carry):
        even = product(0) + product(1)
        build(4 * index + 2, 2)
        build(4 * index + 3, 3)
        odd = product(2) + product(3)
        following = jnp.minimum(4 * index + 4, groups - 2)
        build(following, 0)
        build(following + 1, 1)
        dtable_ref[...] = dtable_ref[...] + (even + odd)
        return carry

    lax.fori_loop(0, groups // 4, step, 0)
    dkey = jnp.zeros((TILE, 256), F32)
    dvalue = jnp.zeros((TILE, 256), F32)
    for head in range(heads):
        dkey = dkey + dot(dscore_ref[head, :, offset:], query_n[head, offset:, :])
        dvalue = dvalue + dot(prob_ref[head, :, offset:], grad_n[head, offset:, :])
        rows = slice(64 * head, 64 * head + 64)
        dquery_ref[rows, offset:] = dquery_ref[rows, offset:] + dot(
            key_t[rows], dscore_ref[head, :, offset:]
        )
    shape = (1, 2, 64, 128)
    parts = (dkey[:, 0:128], dkey[:, 128:256] + dvalue[:, 0:128], dvalue[:, 128:256])
    for i, value in enumerate(parts):
        lanes = slice(128 * i, 128 * i + 128)
        kept_ref[:, :, :, lanes] = value[:128].reshape(shape)
        sent_ref[:, :, :, lanes] = value[128:].astype(BF16).reshape(shape)


def attention_backward(branch, saved, query256, grad256, mixed_t, keys_values, carried, heads):
    exps, buckets, lows, maxima, totals = saved
    members = keys_values.shape[0]
    tiles = members // 2
    first = branch * tiles
    def whole(shape):
        return pl.BlockSpec(shape, lambda t: (0,) * len(shape))

    in_specs = [
        pl.BlockSpec((heads, TILE, ROWS), lambda t: (0, first + t, 0)),
        pl.BlockSpec((TILE, ROWS), lambda t: (first + t, 0)),
        pl.BlockSpec((TILE, ROWS), lambda t: (first + t, 0)),
        pl.BlockSpec((1, 8, ROWS), lambda t: (first + t, 0, 0)),
        whole((8, ROWS)),
        whole((ROWS, 256)),
        whole((ROWS, 256)),
        whole((192, ROWS)),
        pl.BlockSpec((2, 2, 64, 384), lambda t: (t, branch, 0, 0)),
    ]
    if branch == 0:
        carried = (totals, totals)
        in_specs += [whole((8, ROWS)), whole((8, ROWS))]
        aliases = {}
    else:
        in_specs += [
            whole((192, ROWS)),
            whole((128, 64 * heads)),
            pl.BlockSpec(memory_space=pl.ANY),
            pl.BlockSpec(memory_space=pl.ANY),
        ]
        aliases = {11: 2, 12: 3}
    return pl.pallas_call(
        functools.partial(backward_kernel, branch, heads),
        grid=(tiles,),
        in_specs=in_specs,
        out_specs=[
            whole((192, ROWS)),
            whole((128, 64 * heads)),
            pl.BlockSpec((1, 2, 64, 384), lambda t: (t, branch, 0, 0)),
            pl.BlockSpec((1, 2, 64, 384), lambda t: (t, branch, 0, 0)),
        ],
        out_shape=[
            jax.ShapeDtypeStruct((192, ROWS), F32),
            jax.ShapeDtypeStruct((128, 64 * heads), F32),
            jax.ShapeDtypeStruct((tiles, 8, 64, 384), F32),
            jax.ShapeDtypeStruct((tiles, 8, 64, 384), BF16),
        ],
        input_output_aliases=aliases,
        scratch_shapes=[
            pltpu.VMEM((heads, 256, ROWS), BF16),
            pltpu.VMEM((heads, ROWS, 256), BF16),
            pltpu.VMEM((heads, ROWS, 256), BF16),
            pltpu.VMEM((heads, TILE, ROWS), F32),
            pltpu.VMEM((heads, TILE, ROWS), BF16),
            pltpu.VMEM((heads, TILE, ROWS), BF16),
            pltpu.VMEM((4, 128, ROWS), BF16),
            pltpu.VMEM((4, 64 * heads, ROWS), BF16),
            pltpu.VMEM((8, ROWS), F32),
            pltpu.VMEM((8, ROWS), F32),
        ],
        compiler_params=pltpu.CompilerParams(
            dimension_semantics=("arbitrary",), vmem_limit_bytes=58 << 20
        ),
        cost_estimate=pl.CostEstimate(
            flops=8 << 30, bytes_accessed=6 << 20, transcendentals=1 << 18
        ),
        name="attention_backward",
    )(exps, buckets, lows, maxima, totals, query256, grad256, mixed_t, keys_values, *carried)


def arrange_kernel(half_rows, query_rows, plane_ref, *refs):
    block_refs, out_ref, rows_ref = refs[:4], refs[4], refs[5]
    rows_ref[...] = jnp.zeros(rows_ref.shape, F32)
    for distance in range(4):
        plane = plane_ref[0] ^ distance
        block = block_refs[distance][...].astype(F32)
        start = pl.multiple_of(plane * half_rows, half_rows)
        rows_ref[pl.ds(start, half_rows), 64:256] = block[:half_rows, 0:192]
        start = pl.multiple_of((7 - plane) * half_rows, half_rows)
        rows_ref[pl.ds(start, half_rows), 64:256] = block[:half_rows, 192:384]
        start = pl.multiple_of(8 * half_rows + plane * query_rows, 8)
        rows_ref[pl.ds(start, query_rows), 64:256] = block[half_rows:, 0:192]
    out_ref[...] = rows_ref[...].astype(BF16)


def arrange_rows(blocks, plane, half_rows, query_rows):
    return pl.pallas_call(
        functools.partial(arrange_kernel, half_rows, query_rows),
        in_specs=[pl.BlockSpec(memory_space=pltpu.SMEM)]
        + [pl.BlockSpec(memory_space=pltpu.VMEM)] * 4,
        out_specs=pl.BlockSpec(memory_space=pltpu.VMEM),
        out_shape=jax.ShapeDtypeStruct((ROWS, 256), BF16),
        scratch_shapes=[pltpu.VMEM((ROWS, 256), F32)],
        name="arrange_rows",
    )(plane[None], *blocks)


def widen_kernel(group, order_ref, near_ref, far_ref, *out_refs):
    step = pl.program_id(0) ^ (order_ref[0] // group)
    half_steps = pl.num_programs(0) // 2
    inner = order_ref[0] % group

    def from_pieces(pieces_ref):
        rows = pieces_ref.shape[-2]
        for k in range(group):
            start = 0
            for out_ref in out_refs:
                columns = out_ref.shape[-1]
                lanes = slice(start, start + columns)
                if len(pieces_ref.shape) == 4:
                    for s in range(2):
                        block = pieces_ref[k ^ inner, s ^ order_ref[1], :, lanes]
                        out_ref[s, k * rows : (k + 1) * rows, :] = block.astype(F32)
                else:
                    block = pieces_ref[k ^ inner, :, lanes]
                    out_ref[k * rows : (k + 1) * rows, :] = block.astype(F32)
                start += columns

    pl.when(step < half_steps)(lambda: from_pieces(near_ref))
    pl.when(step >= half_steps)(lambda: from_pieces(far_ref))


def widen_rows(near, far, order, columns):
    half, rows, width = near.shape[0], near.shape[-2], near.shape[-1]
    sides = near.shape[1:-2]
    group = min(4, half)
    if rows % 16 != 0:
        pieces = jnp.concatenate([near, far], axis=0)
        position = jnp.arange(2 * half, dtype=jnp.int32) ^ order[0]
        whole = jnp.take(pieces, position, axis=0).astype(F32)
        if sides:
            whole = jnp.swapaxes(jnp.where(order[1] == 1, whole[:, ::-1], whole), 0, 1)
        whole = whole.reshape(sides + (2 * half * rows, width))
        ends = [sum(columns[: i + 1]) for i in range(len(columns))]
        return [whole[..., end - c : end] for end, c in zip(ends, columns)]
    zeros = (0,) * (len(sides) + 2)
    half_steps = half // group

    def piece_map(part):
        def index(r, o):
            order_step = o[0] // group
            first = jnp.where(order_step >= half_steps, 1 - part, part) * half_steps
            inside = jnp.clip(r, first, first + half_steps - 1)
            return ((inside ^ order_step) % half_steps,) + zeros

        return index

    def out_map(r, o):
        return (0,) * len(sides) + (r, 0)

    return pl.pallas_call(
        functools.partial(widen_kernel, group),
        grid_spec=pltpu.PrefetchScalarGridSpec(
            num_scalar_prefetch=1,
            grid=(2 * half_steps,),
            in_specs=[pl.BlockSpec((group,) + near.shape[1:], piece_map(part)) for part in range(2)],
            out_specs=[pl.BlockSpec(sides + (group * rows, c), out_map) for c in columns],
        ),
        out_shape=[jax.ShapeDtypeStruct(sides + (2 * half * rows, c), F32) for c in columns],
        compiler_params=pltpu.CompilerParams(
            dimension_semantics=("arbitrary",), vmem_limit_bytes=24 << 20
        ),
        cost_estimate=pl.CostEstimate(
            flops=0, bytes_accessed=6 * near.size * 2, transcendentals=0
        ),
        name="widen_rows",
    )(order, near, far)


def widen_heads_kernel(count, order_ref, near_ref, far_ref, *out_refs):
    def from_pieces(pieces_ref):
        odd = order_ref[1] == 1
        first, second = pieces_ref[0, 0].astype(F32), pieces_ref[0, 1].astype(F32)
        low = jnp.where(odd, second, first)
        high = jnp.where(odd, first, second)
        size = low.shape[1] // 3
        for i, out_ref in enumerate(out_refs):
            lanes = slice(i * size, (i + 1) * size)
            out_ref[...] = jnp.concatenate([low[:, lanes], high[:, lanes]], axis=1)

    near = (pl.program_id(0) ^ order_ref[0]) < count // 2
    pl.when(near)(lambda: from_pieces(near_ref))
    pl.when(jnp.logical_not(near))(lambda: from_pieces(far_ref))


def widen_heads(near, far, order, odd):
    half, _, rows, width = near.shape
    count = 2 * half
    columns = 2 * width // 3

    def piece(part):
        def index(r, o):
            first = jnp.where(o[0] >= half, 1 - part, part) * half
            inside = jnp.clip(r, first, first + half - 1)
            return ((inside ^ o[0]) % half, 0, 0, 0)

        return index

    return pl.pallas_call(
        functools.partial(widen_heads_kernel, count),
        grid_spec=pltpu.PrefetchScalarGridSpec(
            num_scalar_prefetch=1,
            grid=(count,),
            in_specs=[pl.BlockSpec((1, 2, rows, width), piece(part)) for part in range(2)],
            out_specs=[pl.BlockSpec((rows, columns), lambda r, o: (r, 0))] * 3,
        ),
        out_shape=[jax.ShapeDtypeStruct((count * rows, columns), F32)] * 3,
        compiler_params=pltpu.CompilerParams(dimension_semantics=("arbitrary",)),
        cost_estimate=pl.CostEstimate(
            flops=0, bytes_accessed=12 * count * rows * width, transcendentals=0
        ),
        name="widen_heads",
    )(jnp.stack([order, odd]), near, far)


def pack_kernel(*refs):
    out_ref = refs[-1]
    rows = [ref[...].reshape(1, -1).astype(F32) for ref in refs[:8]]
    out_ref[...] = jnp.zeros(out_ref.shape, BF16)
    out_ref[0:8, :] = jnp.concatenate(rows, axis=0).astype(BF16)
    table = refs[8][...].astype(F32)
    lanes = jnp.zeros((table.shape[0], 128 - table.shape[1]), F32)
    out_ref[16:32, 0:128] = jnp.concatenate([table, lanes], axis=1).astype(BF16)


def pack_vectors(vectors, table):
    vmem = pl.BlockSpec(memory_space=pltpu.VMEM)
    return pl.pallas_call(
        pack_kernel,
        in_specs=[vmem] * 9,
        out_specs=vmem,
        out_shape=jax.ShapeDtypeStruct((32, vectors[0].shape[0]), BF16),
        name="pack_vectors",
    )(*vectors, table)


def unpack_kernel(heads, where_ref, own_ref, other_ref, full_ref, bias_ref, table_ref, turned_ref):
    side = where_ref[0] == 1
    own, other = own_ref[...].astype(F32), other_ref[...].astype(F32)
    low, high = jnp.where(side, other, own), jnp.where(side, own, other)
    full = jnp.concatenate([low[0:8], high[0:8]], axis=1)
    full_ref[...] = full
    both = jnp.concatenate([low[16:32, 0:128], high[16:32, 0:128]], axis=0)
    square = jnp.concatenate([both, jnp.zeros((96, 128), F32)], axis=0)
    turned_ref[...] = square.T
    bias_ref[...] = jnp.zeros(bias_ref.shape, F32)
    table_ref[...] = jnp.zeros(table_ref.shape, F32)
    for plane in range(4):

        @pl.when(where_ref[1] == plane)
        def _(plane=plane):
            lanes = slice(192 * plane, 192 * plane + 192)
            bias_ref[0:1, 0:192] = full[0:1, lanes]
            bias_ref[1:2, 192:384] = full[1:2, lanes]
            table_ref[0:heads, :] = turned_ref[heads * plane : heads * plane + heads, :]


def unpack_vectors(own, other, side, plane, heads):
    vmem = pl.BlockSpec(memory_space=pltpu.VMEM)
    half = own.shape[1]
    return pl.pallas_call(
        functools.partial(unpack_kernel, heads),
        in_specs=[pl.BlockSpec(memory_space=pltpu.SMEM)] + [vmem] * 2,
        out_specs=[vmem] * 3,
        out_shape=[
            jax.ShapeDtypeStruct((8, 2 * half), F32),
            jax.ShapeDtypeStruct((8, half), F32),
            jax.ShapeDtypeStruct((8, 128), F32),
        ],
        scratch_shapes=[pltpu.VMEM((128, 128), F32)],
        name="unpack_vectors",
    )(jnp.stack([side, plane]), own, other)


def finish_kernel(half_rows, query_rows, where_ref, dquery_ref, kv_ref, kv_far_ref, x_ref, *refs):
    block_refs, sent_ref, kept_ref, sums_ref, query_ref, value_ref, low_ref = (
        refs[:4],
        *refs[4:],
    )
    keys = 8 * half_rows
    value_ref[...] = kv_ref[...] + kv_far_ref[...].astype(F32)
    query = dquery_ref[...].T.astype(BF16).astype(F32) * 0.125
    query_ref[...] = query
    low_ref[...] = jnp.zeros(low_ref.shape, BF16)
    low_ref[:, 0:192] = query.astype(BF16)
    low_ref[0:keys, 192:576] = value_ref[...].astype(BF16)
    plane = where_ref[0]
    for distance in range(4):
        other = plane ^ distance
        block_ref = block_refs[distance]
        first = pl.multiple_of(other * half_rows, half_rows)
        second = pl.multiple_of((7 - other) * half_rows, half_rows)
        third = pl.multiple_of(keys + other * query_rows, 8)
        rows = half_rows + query_rows
        block_ref[0:half_rows, 0:192] = query_ref[pl.ds(first, half_rows), :].astype(BF16)
        block_ref[0:half_rows, 192:384] = query_ref[pl.ds(second, half_rows), :].astype(BF16)
        tail = query_ref[pl.ds(third, query_rows), :]
        tail = jnp.concatenate([tail, jnp.zeros_like(tail)], axis=1)
        content = jnp.concatenate(
            [value_ref[pl.ds(first, half_rows), :], value_ref[pl.ds(second, half_rows), :]], axis=0
        )
        block_ref[half_rows:, :] = jnp.concatenate([tail, content], axis=0).astype(BF16)
    width = x_ref.shape[1] // 2
    for target_ref, flip in ((sent_ref, 1), (kept_ref, 0)):
        start = pl.multiple_of((where_ref[1] ^ flip) * width, width)
        product = contract_rows(x_ref[:, pl.ds(start, width)], low_ref[...])
        target_ref[...] = product.astype(target_ref.dtype)
    rounded = low_ref[...].astype(F32)
    sums_ref[...] = jnp.zeros(sums_ref.shape, F32)
    sums_ref[0:1, :] = jnp.sum(rounded, axis=0, keepdims=True)


def finish_heads(dquery_t, kv, kv_far, plane_x, plane, core, half_rows, query_rows):
    keys = 8 * half_rows
    block_rows = half_rows + query_rows + 2 * half_rows
    width = plane_x.shape[1] // 2
    vmem = pl.BlockSpec(memory_space=pltpu.VMEM)
    return pl.pallas_call(
        functools.partial(finish_kernel, half_rows, query_rows),
        in_specs=[pl.BlockSpec(memory_space=pltpu.SMEM)] + [vmem] * 4,
        out_specs=[vmem] * 7,
        out_shape=[jax.ShapeDtypeStruct((block_rows, 384), BF16)] * 4
        + [
            jax.ShapeDtypeStruct((width, 576), BF16),
            jax.ShapeDtypeStruct((width, 576), F32),
            jax.ShapeDtypeStruct((8, 576), F32),
        ],
        scratch_shapes=[
            pltpu.VMEM((ROWS, 192), F32),
            pltpu.VMEM((keys, 384), F32),
            pltpu.VMEM((ROWS, 576), BF16),
        ],
        compiler_params=pltpu.CompilerParams(vmem_limit_bytes=32 << 20),
        cost_estimate=pl.CostEstimate(flops=1 << 30, bytes_accessed=6 << 20, transcendentals=0),
        name="finish_heads",
    )(jnp.stack([plane, core]), dquery_t, kv, kv_far, plane_x)


def after(value, *earlier):
    return lax.optimization_barrier((value,) + earlier)[0]


def row_major(value):
    return with_layout_constraint(value, Layout(major_to_minor=tuple(range(value.ndim))))


class Chain:
    def __init__(self, state, stages):
        self.state, self.stages = state, stages
        self.leave()

    def leave(self):
        if self.stages:
            self.sent, self.kept = self.stages[0][0](self.state)
            self.arrived = self.stages[0][1](self.sent)

    def advance(self, token):
        kept = jax.tree.map(lambda leaf: after(leaf, token), self.kept)
        self.state = self.stages[0][2](kept, self.arrived)
        self.stages = self.stages[1:]
        self.leave()
        return self.sent if self.stages else jax.tree.leaves(self.state)[0]

    def drain(self, token):
        while self.stages:
            token = self.advance(token)
        return token


def reverse_bits(value, count):
    result = jnp.zeros_like(value)
    bit, mirrored = 1, count // 2
    while bit < count:
        result = result + jnp.where((value & bit) != 0, mirrored, 0)
        bit, mirrored = bit * 2, mirrored // 2
    return result


def body(
    content,
    query_stream,
    token_order,
    targets,
    query_weight,
    key_weight,
    value_weight,
    output_weight,
    query_bias,
    value_bias,
    output_bias,
    bias_table,
    first_gain,
    first_shift,
    inner_weight,
    inner_bias,
    outer_weight,
    outer_bias,
    second_gain,
    second_shift,
    content_cotangent,
    query_cotangent,
):
    ctx = lax.axis_size("ctx")
    index = lax.axis_index("ctx")
    side = lax.axis_index("wt")
    members = ctx // 4
    plane = index // members
    member = index % members
    half_rows = content.shape[2]
    tok_rows = 2 * half_rows
    query_rows = query_stream.shape[1]
    rows_dev = tok_rows + query_rows
    width = content.shape[3]
    heads = bias_table.shape[1]
    my_heads = heads // 4
    head_width = my_heads * (width // heads)
    half_width = width // 2
    seq_length = tok_rows * ctx
    half_length = seq_length // 2
    order_row = token_order[0]
    target_row = targets[0]
    core_bit = (index & 1) == 1

    def swap(value, bit):
        return lax.ppermute(value, "ctx", [(i, i ^ bit) for i in range(ctx)])

    def swap_side(value):
        return lax.ppermute(value, "wt", [(0, 1), (1, 0)])

    def order_two(flag, mine, other, axis):
        low = jnp.where(flag, other, mine)
        high = jnp.where(flag, mine, other)
        return jnp.concatenate([low, high], axis=axis)

    def half_of_core(value):
        rows = value.shape[0] // 2
        return lax.dynamic_slice_in_dim(value, (index & 1) * rows, rows, 0)

    def both_cores(arrived):
        return order_two(core_bit, arrived, swap(arrived, 1), 0)

    def by_distance(blocks):
        flag = (plane & 1) == 1
        blocks = [jnp.where(flag, blocks[d ^ 1], blocks[d]) for d in range(4)]
        flag = (plane & 2) == 2
        return [jnp.where(flag, blocks[d ^ 2], blocks[d]) for d in range(4)]

    def exchange_planes(blocks):
        sent = by_distance(blocks)
        arrived = [sent[0]] + [swap(sent[d], d * members) for d in range(1, 4)]
        return by_distance(arrived)

    def pack_rows(rows):
        top = jnp.concatenate([rows[:half_rows], rows[half_rows:tok_rows]], axis=1)
        bottom = jnp.concatenate([rows[tok_rows:], jnp.zeros_like(rows[tok_rows:])], axis=1)
        return jnp.concatenate([top, bottom], axis=0)

    def unpack_rows(packed):
        return jnp.concatenate(
            [
                packed[:half_rows, :head_width],
                packed[:half_rows, head_width:],
                packed[half_rows:, :head_width],
            ],
            axis=0,
        )

    def plane_rows(blocks):
        pad = ROWS - 4 * rows_dev
        return jnp.concatenate(
            [blocks[d][:half_rows] for d in range(4)]
            + [blocks[3 - d][half_rows:tok_rows] for d in range(4)]
            + [blocks[d][tok_rows:] for d in range(4)]
            + [jnp.zeros((pad, blocks[0].shape[1]), blocks[0].dtype)],
            axis=0,
        )

    def split_rows(rows):
        blocks = []
        for d in range(4):
            parts = [
                rows[d * half_rows : (d + 1) * half_rows],
                rows[(7 - d) * half_rows : (8 - d) * half_rows],
            ]
            if rows.shape[0] > 4 * tok_rows:
                start = 4 * tok_rows + d * query_rows
                parts.append(rows[start : start + query_rows])
            blocks.append(jnp.concatenate(parts, axis=0))
        return blocks

    local_content = content[0].reshape(tok_rows, width)
    stacked = jnp.concatenate([local_content, query_stream[0]], axis=0)
    arrived_rows = [stacked] + [swap(stacked, d * members) for d in range(1, 4)]
    owner = plane // 2
    odd_plane = (plane & 1) == 1
    side_flag = side == 1
    shards = [query_weight, key_weight, value_weight]
    near_own = jnp.concatenate(
        [jnp.where(odd_plane, s[:, head_width:], s[:, :head_width]) for s in shards], axis=1
    )
    near_sent = half_of_core(near_own)
    near_other = both_cores(swap_side(near_sent))
    vectors = [
        query_bias,
        value_bias,
        output_bias,
        first_gain,
        first_shift,
        outer_bias,
        second_gain,
        second_shift,
    ]
    own_vectors = pack_vectors(vectors, bias_table)
    other_vectors = swap_side(own_vectors)
    full_vectors, head_bias, tables = unpack_vectors(
        own_vectors, other_vectors, side, plane, my_heads
    )
    (
        full_output_bias,
        full_first_gain,
        full_first_shift,
        full_outer_bias,
        full_second_gain,
        full_second_shift,
    ) = [full_vectors[i : i + 1] for i in range(2, 8)]
    buckets = 2 * bias_table.shape[0]

    places = jnp.arange(half_length, dtype=jnp.int32)
    key_place = jnp.concatenate(
        [places, (seq_length - 1 - places).reshape(4, -1)[::-1].reshape(-1)]
    )
    key_anchor = jnp.concatenate(
        [
            order_row[:half_length],
            order_row[half_length:][::-1].reshape(4, -1)[::-1].reshape(-1),
        ]
    )

    def of_member(array, count):
        return lax.dynamic_index_in_dim(
            array.reshape(-1, members, count), member, 1, keepdims=False
        ).reshape(-1)

    def by_member_distance(array):
        pieces = [array.reshape(8, members, -1)]
        bit = members // 2
        while bit >= 1:
            flag = (member & bit) != 0
            split = []
            for piece in pieces:
                size = piece.shape[1] // 2
                low, high = piece[:, :size], piece[:, size:]
                split.append(jnp.where(flag, high, low))
                split.append(jnp.where(flag, low, high))
            pieces = split
            bit //= 2
        return jnp.concatenate(pieces, axis=1)

    plane_targets = of_member(target_row, query_rows)
    target_anchor = jnp.sum(
        jnp.where(
            jnp.arange(seq_length, dtype=jnp.int32)[:, None] == plane_targets[None],
            order_row[:, None],
            0,
        ),
        axis=0,
    )
    pad_rows = ROWS - 4 * rows_dev
    row_anchor = jnp.concatenate(
        [of_member(key_anchor, half_rows), target_anchor, jnp.zeros((pad_rows,), jnp.int32)]
    )
    row_limit = jnp.concatenate(
        [
            of_member(key_place, half_rows) + 1,
            plane_targets,
            jnp.ones((pad_rows,), jnp.int32),
        ]
    )
    row_info = jnp.concatenate(
        [row_anchor[None], row_limit[None], jnp.zeros((6, ROWS), jnp.int32)], axis=0
    )

    def by_tile(array):
        parts = by_member_distance(array).reshape(4, 2, members // 2, 2, -1)
        return jnp.transpose(parts, (0, 2, 3, 1, 4)).reshape(-1)

    near_anchor = by_tile(key_anchor)
    key_anchor_wide = jnp.broadcast_to(near_anchor[:, None], (seq_length, 128))
    block_places = by_tile(key_place.reshape(-1, half_rows)[:, 0])
    head_weights = jnp.where(side == owner, near_own, near_other)
    plane_x = plane_rows(by_distance(arrived_rows))
    plane_kv = (
        dot(plane_x[: 4 * tok_rows], head_weights[:, head_width:]) + head_bias[1:2]
    ).astype(BF16)
    first_kv = plane_kv.reshape(1, 8, half_rows, 2 * head_width)
    far_kv = swap(first_kv, members // 2)
    bit = 1
    near_members = first_kv
    while bit < members // 2:
        near_members = jnp.concatenate([near_members, swap(near_members, bit)], axis=0)
        bit *= 2
    query_weights = jnp.pad(head_weights[:, :head_width], ((0, 0), (0, 256 - head_width)))
    query256 = ((dot(plane_x, query_weights) + head_bias[0:1, :256]) * 0.125).astype(BF16)

    output_early, outer_early, rest_own = lax.optimization_barrier(
        (
            output_weight,
            outer_weight,
            jnp.concatenate(
                [
                    jnp.where(odd_plane, s[:, :head_width], s[:, head_width:])
                    for s in lax.optimization_barrier(tuple(shards) + (plane_kv,))[:3]
                ],
                axis=1,
            ),
            query256,
        )
    )[:3]
    hidden_half = outer_weight.shape[0] // 2

    outer_sent = lax.dynamic_slice_in_dim(outer_early, (1 - side) * hidden_half, hidden_half, 0)
    output_arrived = swap_side(half_of_core(output_early))
    outer_arrived_half = swap_side(half_of_core(outer_sent))
    rest_arrived = swap_side(half_of_core(rest_own))

    forward_info = (key_anchor_wide, block_places, row_info, tables)
    first_half = attention_forward(0, query256, near_members, *forward_info, (), my_heads)
    far_members = far_kv
    bit = 1
    while bit < members // 2:
        far_members = jnp.concatenate([far_members, swap(far_members, bit)], axis=0)
        bit *= 2
    exps, bucket_ids, bucket_lows, maxima, _, _, mixed_t, mixed_plane, totals = attention_forward(
        1, query256, far_members, *forward_info, first_half, my_heads
    )
    keys_values = jnp.concatenate([near_members, far_members], axis=0)

    full_output = order_two(side_flag, output_weight, both_cores(after(output_arrived, mixed_plane)), 1)
    outer_kept = lax.dynamic_slice_in_dim(outer_weight, side * hidden_half, hidden_half, 0)
    outer_rows = order_two(side_flag, outer_kept, both_cores(after(outer_arrived_half, mixed_plane)), 1)
    rest_other = both_cores(after(rest_arrived, mixed_plane))
    full_qkv = []
    for i in range(3):
        lanes = slice(i * head_width, (i + 1) * head_width)
        other = order_two(odd_plane, near_other[:, lanes], rest_other[:, lanes], 1)
        full_qkv.append(order_two(side_flag, shards[i], other, 1))

    mixed_blocks = exchange_planes([pack_rows(block) for block in split_rows(mixed_plane)])
    mixed = jnp.concatenate([unpack_rows(block) for block in mixed_blocks], axis=1)
    branch = dot(mixed, full_output) + full_output_bias
    first_norm, first_back = jax.vjp(
        norm_of_sum, stacked.astype(F32), branch, full_first_gain, full_first_shift
    )
    first_low = first_norm.astype(BF16)
    both_first = jnp.concatenate([first_low, swap_side(first_low)], axis=0)
    inner_value = dot(both_first, inner_weight) + inner_bias.astype(F32)
    hidden_value, gelu_back = jax.vjp(gelu_exact, inner_value)
    hidden_low = hidden_value.astype(BF16)
    outer_part = dot(hidden_low, outer_rows)
    outer_arrived = swap_side(outer_part[rows_dev:].astype(BF16))
    outer_value = outer_part[:rows_dev] + outer_arrived.astype(F32) + full_outer_bias
    final_norm, second_back = jax.vjp(
        norm_of_sum, first_norm, outer_value, full_second_gain, full_second_shift
    )
    content_result = final_norm[:tok_rows].reshape(1, 2, half_rows, width).astype(BF16)
    query_result = final_norm[tok_rows:].reshape(1, query_rows, width).astype(BF16)
    cotangent = jnp.concatenate(
        [content_cotangent[0].reshape(tok_rows, width), query_cotangent[0]], axis=0
    )
    rest_grad, outer_grad, second_gain_grad, second_shift_grad = second_back(cotangent.astype(F32))
    outer_low = outer_grad.astype(BF16)
    both_outer = jnp.concatenate([outer_low, swap_side(outer_low)], axis=0)
    (inner_grad,) = gelu_back(times_transpose(both_outer, outer_rows))
    inner_low = inner_grad.astype(BF16)
    first_part = times_transpose(inner_low, inner_weight)
    first_arrived = swap_side(first_part[rows_dev:].astype(BF16))
    first_grad = rest_grad + (first_part[:rows_dev] + first_arrived.astype(F32))
    row_grad, branch_grad, first_gain_grad, first_shift_grad = first_back(first_grad)
    branch_low = branch_grad.astype(BF16)
    mixed_low = times_transpose(branch_low, full_output).astype(BF16)

    def to(bit):
        return lambda value: swap(value, bit)

    def leave_half(bit):
        def leave(parts):
            rows = parts[0].shape[0] // 2
            upper = jnp.where((index & bit) != 0, 1, 0)
            sent = [
                lax.dynamic_slice_in_dim(part, (1 - upper) * rows, rows, 0).astype(BF16)
                for part in parts
            ]
            return jnp.concatenate(sent, axis=1), parts

        return leave

    def add_half(bit):
        def add(parts, arrived):
            rows = parts[0].shape[0] // 2
            upper = jnp.where((index & bit) != 0, 1, 0)
            kept = [lax.dynamic_slice_in_dim(part, upper * rows, rows, 0) for part in parts]
            return [(kept[0].astype(F32) + arrived.astype(F32)).astype(kept[0].dtype)]

        return add

    def keep_all(state):
        return state, state

    def append(kept, arrived):
        return jnp.concatenate([kept, arrived], axis=0)

    bits = []
    bit = 1
    while bit < ctx:
        bits.append(bit)
        bit *= 2
    sum_stages = [(leave_half(bit), to(bit), add_half(bit)) for bit in bits]
    gather_stages = [(keep_all, to(bit), append) for bit in bits[::-1]]

    def leave_columns(parts):
        piece = parts[0].astype(BF16)
        left, right = piece[:, :half_width], piece[:, half_width:]
        return jnp.where(side_flag, left, right), jnp.where(side_flag, right, left)

    def pair_sides(kept, arrived):
        return jnp.stack([kept, arrived], axis=0)[None]

    def start_gather(parts):
        state = parts[0].astype(BF16)[None]
        return state, state

    core_half = index & 1

    def halves(left, right):
        size = left.shape[1] // 2
        parts = []
        for half in (1 - core_half, core_half):
            columns = lax.dynamic_slice_in_dim(left, half * size, size, 1)
            parts.append(contract_rows(columns, right).astype(BF16))
        return parts

    def add_pair(kept, arrived):
        return [(kept.astype(F32) + arrived.astype(F32)).astype(BF16)]

    first_stage = (lambda state: state, to(1), add_pair)
    outer_chain = Chain(
        halves(hidden_low, both_outer),
        [first_stage] + sum_stages[1:] + [(leave_columns, swap_side, pair_sides)] + gather_stages[:-1],
    )

    other_mixed = swap_side(after(mixed, inner_low))
    branch_left, branch_right = branch_low[:, :half_width], branch_low[:, half_width:]
    branch_kept = jnp.where(side_flag, branch_right, branch_left)
    inner_halves = halves(both_first, inner_low)
    branch_arrived = swap_side(after(jnp.where(side_flag, branch_left, branch_right), mixed_low))
    both_mixed = jnp.concatenate([mixed, other_mixed], axis=0)
    both_branch = jnp.concatenate([branch_kept, branch_arrived], axis=0)
    output_halves = halves(both_mixed, both_branch)
    joined_chain = Chain(
        [
            jnp.concatenate([inner, output], axis=1)
            for inner, output in zip(inner_halves, output_halves)
        ],
        [first_stage] + sum_stages[1:] + [(start_gather, to(bits[-1]), append)] + gather_stages[1:-1],
    )

    chains = {"O": outer_chain, "J": joined_chain}

    def run(order, token):
        for name in order:
            chain = chains.get(name)
            if chain is not None and chain.stages:
                token = chain.advance(token)
        return token

    grad_sent = by_distance(
        [
            pack_rows(mixed_low[:, d * head_width : (d + 1) * head_width])
            for d in range(4)
        ]
    )
    grad_blocks = [grad_sent[0]] + [swap(grad_sent[d], d * members) for d in range(1, 4)]
    token = run(GAPS[0], grad_sent[1])
    grad_blocks = lax.optimization_barrier(tuple(grad_blocks) + (token, joined_chain.sent))[:4]
    grad256 = arrange_rows(grad_blocks, plane, half_rows, query_rows)
    saved = (exps, bucket_ids, bucket_lows, maxima, totals)
    carried = None
    for call in range(4):
        if call == 0:
            token = run(GAPS[1], grad256)
            grad256 = after(grad256, token)
        else:
            token = run(GAPS[call + 1], carried[0])
            carried = (after(carried[0], token),) + carried[1:]
        carried = tuple(
            attention_backward(
                call, saved, query256, grad256, mixed_t, keys_values, carried, my_heads
            )
        )
    dquery_t, table_part, kv_kept, kv_sent = carried
    member_bits = [bit for bit in bits if bit < members]
    head_orders = TAIL.split("|")[0].split("K")
    token = run(head_orders[0], kv_sent)
    for bit in member_bits:
        kv_arrived = after(swap(kv_sent, bit), token)
        if bit < member_bits[-1]:
            pairs = (-1, 2, 8, half_rows, 2 * head_width)
            kept, arrived = kv_kept.reshape(pairs), kv_arrived.reshape(pairs)
            kv_sent = row_major((kept[:, 1] + arrived[:, 1].astype(F32)).astype(BF16))
            kv_kept = row_major(kept[:, 0] + arrived[:, 0].astype(F32))
        if bit == 1:
            token = run(head_orders[1], kv_sent)
    flat_kv = (8 * half_rows, 2 * head_width)
    *sent_distance, heads_sent, heads_kept, column_sums = finish_heads(
        dquery_t,
        kv_kept.reshape(flat_kv),
        after(kv_arrived, token).reshape(flat_kv),
        plane_x,
        plane,
        index & 1,
        half_rows,
        query_rows,
    )

    def add_first(kept, arrived):
        return [kept + arrived.astype(F32)]

    def leave_same(parts):
        return parts[0].astype(BF16), parts

    def add_side(kept, arrived):
        return (kept[0] + arrived.astype(F32)).astype(BF16)

    def choose_owner(kept, arrived):
        return jnp.where(owner == side, kept, arrived)[None]

    def append_plane(kept, arrived):
        return jnp.concatenate([kept, arrived], axis=0)[None]

    heads_chain = Chain(
        (heads_sent, heads_kept),
        [(lambda state: state, to(1), add_first)]
        + sum_stages[1 : len(member_bits)]
        + [
            (leave_same, swap_side, add_side),
            (keep_all, to(2 * members), choose_owner),
            (keep_all, to(members), append_plane),
        ]
        + [(keep_all, to(bit), append) for bit in member_bits[:0:-1]],
    )

    got_distance = [sent_distance[0]] + [
        swap(sent_distance[d], d * members) for d in range(1, 4)
    ]
    full_query, full_key, full_value = full_qkv

    blocks = table_part.reshape(8, GROUP, 4, my_heads, GROUP)
    same = jnp.eye(GROUP, dtype=F32)[None, :, None, None, :]
    table_cumulative = jnp.sum(blocks * same, axis=(1, 4))
    table_grad = table_cumulative - jnp.concatenate(
        [table_cumulative[1:], jnp.zeros_like(table_cumulative[:1])], axis=0
    )
    table_grad = table_grad.reshape(buckets, my_heads)

    def at_plane(values, axis):
        return jnp.concatenate(
            [jnp.where(plane == d, values, jnp.zeros_like(values)) for d in range(4)], axis=axis
        )

    inner_bias_part = jnp.sum(inner_low.astype(F32), axis=0)
    inner_bias_zero = jnp.zeros_like(inner_bias_part)
    late_small = jnp.concatenate(
        [
            at_plane(column_sums[0, :head_width], 0),
            at_plane(column_sums[0, 2 * head_width :], 0),
            jnp.sum(branch_low.astype(F32), axis=0),
            first_gain_grad.reshape(-1),
            first_shift_grad.reshape(-1),
            jnp.sum(outer_low.astype(F32), axis=0),
            second_gain_grad.reshape(-1),
            second_shift_grad.reshape(-1),
            jnp.where(side_flag, inner_bias_zero, inner_bias_part),
            jnp.where(side_flag, inner_bias_part, inner_bias_zero),
            at_plane(table_grad, 1).reshape(-1),
        ]
    )
    late_length = late_small.shape[0]
    late_small = jnp.pad(late_small, (0, -late_length % 1024)).reshape(-1, 128)

    def add_plain(kept, arrived):
        return kept + arrived

    late_chain = Chain(
        after(late_small, heads_chain.sent),
        [(keep_all, to(bit), add_plain) for bit in bits] + [(keep_all, swap_side, add_plain)],
    )

    chains["H"], chains["L"] = heads_chain, late_chain
    token = late_chain.sent
    row_order = jnp.stack([reverse_bits(index, ctx), side])
    for name in TAIL.split("|")[1]:
        if name == "X":
            arrived = lax.optimization_barrier(tuple(got_distance) + (token,))[:4]
            got_blocks = by_distance(arrived)
            packed_rows = half_rows + query_rows
            own_query = jnp.concatenate([unpack_rows(b[:packed_rows]) for b in got_blocks], axis=1)
            own_key = jnp.concatenate([b[packed_rows:, :head_width] for b in got_blocks], axis=1)
            own_value = jnp.concatenate([b[packed_rows:, head_width:] for b in got_blocks], axis=1)
            input_grad = row_grad + times_transpose(own_query, full_query)
            content_extra = times_transpose(own_key, full_key)
            content_extra = content_extra + times_transpose(own_value, full_value)
            content_gradient = input_grad[:tok_rows] + content_extra
            content_gradient = content_gradient.reshape(1, 2, half_rows, width)
            query_gradient = input_grad[tok_rows:].reshape(1, query_rows, width)
            token = content_gradient
        elif name in "ABC":
            chain = {"A": outer_chain, "B": joined_chain, "C": heads_chain}[name]
            token = chain.drain(token)
            near = chain.state
            if name == "A":
                far = after(swap(near, 1), token)
                outer_weight_grad = widen_rows(near, far, row_order, (half_width,))[0]
                outer_weight_grad = outer_weight_grad.reshape(2 * hidden_half, half_width)
                token = outer_weight_grad
            elif name == "B":
                far = after(swap(near, 1), token)
                inner_weight_grad, output_weight_grad = widen_rows(
                    near, far, row_order, (hidden_half, half_width)
                )
                token = inner_weight_grad
            else:
                far = after(swap(near, 1), token)
                qkv_grads = widen_heads(near, far, reverse_bits(member, members), plane & 1)
                token = qkv_grads[0]
        else:
            token = run(name, token)
    token = late_chain.drain(token)

    late_small = late_chain.state.reshape(-1)[:late_length]
    table_start = 8 * width + 2 * hidden_half
    table_all = late_small[table_start:].reshape(2, buckets // 2, heads)
    bias_table_grad = jnp.where(side_flag, table_all[1], table_all[0])

    def my_half(start, size):
        low = late_small[start : start + size]
        return jnp.where(side_flag, late_small[start + size : start + 2 * size], low)

    mine = [my_half(i * width, half_width) for i in range(8)]
    inner_bias_grad = my_half(8 * width, hidden_half)

    return (
        content_result,
        query_result,
        content_gradient,
        query_gradient,
        qkv_grads[0],
        qkv_grads[1],
        qkv_grads[2],
        output_weight_grad,
        mine[0],
        mine[1],
        mine[2],
        bias_table_grad,
        mine[3],
        mine[4],
        inner_weight_grad,
        inner_bias_grad,
        outer_weight_grad,
        mine[5],
        mine[6],
        mine[7],
    )


def solution(mesh):
    return jax.shard_map(
        body,
        mesh=mesh,
        in_specs=(
            P("wt", None, "ctx", None),
            P("wt", "ctx", None),
            P("wt", None),
            P("wt", None),
            P(None, "wt"),
            P(None, "wt"),
            P(None, "wt"),
            P(None, "wt"),
            P("wt"),
            P("wt"),
            P("wt"),
            P("wt", None),
            P("wt"),
            P("wt"),
            P(None, "wt"),
            P("wt"),
            P(None, "wt"),
            P("wt"),
            P("wt"),
            P("wt"),
            P("wt", None, "ctx", None),
            P("wt", "ctx", None),
        ),
        out_specs=(
            P("wt", None, "ctx", None),
            P("wt", "ctx", None),
            P("wt", None, "ctx", None),
            P("wt", "ctx", None),
            P(None, "wt"),
            P(None, "wt"),
            P(None, "wt"),
            P(None, "wt"),
            P("wt"),
            P("wt"),
            P("wt"),
            P("wt", None),
            P("wt"),
            P("wt"),
            P(None, "wt"),
            P("wt"),
            P(None, "wt"),
            P("wt"),
            P("wt"),
            P("wt"),
        ),
        check_vma=False,
    )
```

```python
import functools

import jax
import jax.numpy as jnp
from jax import lax
from jax.experimental import pallas as pl
from jax.experimental.layout import Layout, with_layout_constraint
from jax.experimental.pallas import tpu as pltpu
from jax.sharding import PartitionSpec as P

BF16 = jnp.bfloat16
F32 = jnp.float32
FAR_EDGES = (12, 16, 23, 32, 46, 64, 91)
NEGATIVE = -1e30
TILE = 256
ROWS = 640
GROUP = 16
GAPS = ['O', 'OJ', 'O', 'OJ', 'OJ']
TAIL = 'KJOK|HLHJOHXLJHLOHLBLHAC'


def layer_norm(hidden_rows, gain_row, shift_row):
    average = jnp.mean(hidden_rows, axis=-1, keepdims=True)
    centered = hidden_rows - average
    variance = jnp.mean(centered * centered, axis=-1, keepdims=True)
    return centered * lax.rsqrt(variance + 1e-05) * gain_row + shift_row


def norm_of_sum(residual, branch_value, gain_row, shift_row):
    return layer_norm(residual + branch_value, gain_row, shift_row)


def gelu_exact(values):
    return jax.nn.gelu(values, approximate=False)


def dot(left, right):
    return jnp.dot(left, right, preferred_element_type=F32)


def contract_rows(left, right):
    return lax.dot_general(left, right, (((0,), (0,)), ((), ())), preferred_element_type=F32)


def times_transpose(left, right):
    return lax.dot_general(left, right, (((1,), (1,)), ((), ())), preferred_element_type=F32)


def transpose_low(block):
    return block.astype(F32).T.astype(BF16)


def tile_branches(branch_index, process):
    for branch in range(4):
        pl.when(branch_index == branch)(functools.partial(process, 128 * branch))


def forward_kernel(call, count, heads, *refs):
    place_ref, query_ref, kv_ref, anchor_ref, row_ref, table_ref = refs[:6]
    refs = refs[6:]
    if call == 1:
        max_in, sum_in, mixed_in = refs[4:7]
        refs = refs[7:]
    exp_ref, bucket_ref, low_ref, max_ref, run_max, run_sum, mixed_t_ref = refs[:7]
    refs = refs[7:]
    if call == 1:
        mixed_ref, total_ref = refs[:2]
        refs = refs[2:]
    query_z, prob_ref, scale_ref = refs
    step = pl.program_id(0)
    branch_index = step // count
    tile_index = branch_index * (2 * count) + call * count + step % count

    @pl.when(step == 0)
    def _():
        query_t = transpose_low(query_ref[...])
        part = lax.broadcasted_iota(jnp.int32, (256, ROWS), 0) // 64
        for head in range(heads):
            query_z[head] = jnp.where(part == head, query_t.astype(F32), 0.0).astype(BF16)
        if call == 0:
            run_max[...] = jnp.full(run_max.shape, NEGATIVE, F32)
            run_sum[...] = jnp.zeros(run_sum.shape, F32)
            mixed_t_ref[...] = jnp.zeros(mixed_t_ref.shape, F32)
        else:
            run_max[...] = max_in[...]
            run_sum[...] = sum_in[...]
            mixed_t_ref[...] = mixed_in[...]

    place_sign = jnp.where(branch_index < 2, 1, -1)
    keys_values = kv_ref[...].reshape(TILE, 384)
    value_t = transpose_low(keys_values[:, 128:384])

    def process(offset):
        chunks = (ROWS - offset) // 128
        for head in range(heads):
            exp_ref[head, :, offset:] = dot(keys_values[:, 0:256], query_z[head, :, offset:])

        def bias_group(group, tops):
            start = pl.multiple_of(group * GROUP, GROUP)
            keys = anchor_ref[pl.ds(start, GROUP), :]
            row = start % 64 + lax.broadcasted_iota(jnp.int32, (GROUP, 128), 0)
            place = place_ref[tile_index * (TILE // 64) + start // 64] + place_sign * row
            new_tops = []
            for chunk in range(chunks):
                lanes = slice(offset + chunk * 128, offset + chunk * 128 + 128)
                relative = keys - row_ref[0:1, lanes]
                magnitude = jnp.abs(relative)
                bucket = jnp.minimum(magnitude, 8)
                for edge in FAR_EDGES:
                    bucket = bucket + jnp.where(magnitude >= edge, 1, 0)
                bucket = bucket + jnp.where(relative > 0, 16, 0)
                bucket_ref[pl.ds(start, GROUP), lanes] = bucket.astype(F32).astype(BF16)
                low_ref[pl.ds(start, GROUP), lanes] = (bucket & 3).astype(F32).astype(BF16)
                allowed = place < row_ref[1:2, lanes]
                for head in range(heads):
                    table = jnp.broadcast_to(table_ref[head : head + 1, :], (8, 128))
                    bias = jnp.concatenate(
                        [
                            jnp.take_along_axis(table, bucket[0:8], axis=1),
                            jnp.take_along_axis(table, bucket[8:16], axis=1),
                        ],
                        axis=0,
                    )
                    scores = exp_ref[head, pl.ds(start, GROUP), lanes] + bias
                    scores = jnp.where(allowed, scores, NEGATIVE)
                    exp_ref[head, pl.ds(start, GROUP), lanes] = scores
                    top = tops[chunk * heads + head]
                    new_tops.append(jnp.maximum(top, jnp.maximum(scores[0:8], scores[8:16])))
            return tuple(new_tops)

        tops = lax.fori_loop(
            0,
            TILE // GROUP,
            bias_group,
            tuple(jnp.full((8, 128), NEGATIVE, F32) for _ in range(chunks * heads)),
            unroll=8,
        )
        for chunk in range(chunks):
            lanes = slice(offset + chunk * 128, offset + chunk * 128 + 128)
            for head in range(heads):
                top = jnp.max(tops[chunk * heads + head], axis=0, keepdims=True)
                old = run_max[head : head + 1, lanes]
                new = jnp.maximum(old, top)
                scale_ref[head : head + 1, lanes] = jnp.exp(old - new)
                run_max[head : head + 1, lanes] = new
        max_ref[0] = run_max[...]

        def exp_group(group, sums):
            start = pl.multiple_of(group * GROUP, GROUP)
            new_sums = []
            for chunk in range(chunks):
                lanes = slice(offset + chunk * 128, offset + chunk * 128 + 128)
                for head in range(heads):
                    terms = jnp.exp(
                        exp_ref[head, pl.ds(start, GROUP), lanes] - run_max[head : head + 1, lanes]
                    )
                    exp_ref[head, pl.ds(start, GROUP), lanes] = terms
                    prob_ref[head, pl.ds(start, GROUP), lanes] = terms.astype(BF16)
                    new_sums.append(sums[chunk * heads + head] + (terms[0:8] + terms[8:16]))
            return tuple(new_sums)

        sums = lax.fori_loop(
            0,
            TILE // GROUP,
            exp_group,
            tuple(jnp.zeros((8, 128), F32) for _ in range(chunks * heads)),
        )
        for chunk in range(chunks):
            lanes = slice(offset + chunk * 128, offset + chunk * 128 + 128)
            for head in range(heads):
                run_sum[head : head + 1, lanes] = run_sum[head : head + 1, lanes] * scale_ref[
                    head : head + 1, lanes
                ] + jnp.sum(sums[chunk * heads + head], axis=0, keepdims=True)
        for head in range(heads):
            rows = slice(64 * head, 64 * head + 64)
            mixed_t_ref[rows, offset:] = mixed_t_ref[rows, offset:] * scale_ref[
                head : head + 1, offset:
            ] + dot(value_t[64 + 64 * head : 128 + 64 * head], prob_ref[head, :, offset:])

    tile_branches(branch_index, process)

    if call == 1:

        @pl.when(step == 4 * count - 1)
        def _():
            for head in range(heads):
                rows = slice(64 * head, 64 * head + 64)
                mixed_t_ref[rows, :] = mixed_t_ref[rows, :] / run_sum[head : head + 1, :]
                total_ref[head : head + 1, :] = run_max[head : head + 1, :] + jnp.log(
                    run_sum[head : head + 1, :]
                )
            mixed_ref[...] = mixed_t_ref[...].T.astype(BF16)


def attention_forward(
    call, query256, keys_values, key_anchor, block_places, row_info, tables, previous, heads
):
    count = keys_values.shape[0] // 2
    tiles = 8 * count
    total_keys = tiles * TILE

    def tile_of(s):
        return (s // count) * (2 * count) + call * count + s % count

    def whole(shape):
        return pl.BlockSpec(shape, lambda s, p: (0,) * len(shape))

    in_specs = [
        whole((ROWS, 256)),
        pl.BlockSpec((2, 2, 64, 384), lambda s, p: (s % count, s // count, 0, 0)),
        pl.BlockSpec((TILE, 128), lambda s, p: (tile_of(s), 0)),
        whole((8, ROWS)),
        whole((8, 128)),
    ]
    out_specs = [
        pl.BlockSpec((heads, TILE, ROWS), lambda s, p: (0, tile_of(s), 0)),
        pl.BlockSpec((TILE, ROWS), lambda s, p: (tile_of(s), 0)),
        pl.BlockSpec((TILE, ROWS), lambda s, p: (tile_of(s), 0)),
        pl.BlockSpec((1, 8, ROWS), lambda s, p: (tile_of(s), 0, 0)),
        whole((8, ROWS)),
        whole((8, ROWS)),
        whole((192, ROWS)),
    ]
    out_shape = [
        jax.ShapeDtypeStruct((heads, total_keys, ROWS), F32),
        jax.ShapeDtypeStruct((total_keys, ROWS), BF16),
        jax.ShapeDtypeStruct((total_keys, ROWS), BF16),
        jax.ShapeDtypeStruct((tiles, 8, ROWS), F32),
        jax.ShapeDtypeStruct((8, ROWS), F32),
        jax.ShapeDtypeStruct((8, ROWS), F32),
        jax.ShapeDtypeStruct((192, ROWS), F32),
    ]
    aliases = {}
    if call == 1:
        in_specs += [pl.BlockSpec(memory_space=pl.ANY)] * 4
        in_specs += [whole((8, ROWS)), whole((8, ROWS)), whole((192, ROWS))]
        out_specs += [whole((ROWS, 192)), whole((8, ROWS))]
        out_shape += [
            jax.ShapeDtypeStruct((ROWS, 192), BF16),
            jax.ShapeDtypeStruct((8, ROWS), F32),
        ]
        aliases = {6: 0, 7: 1, 8: 2, 9: 3}
    return pl.pallas_call(
        functools.partial(forward_kernel, call, count, heads),
        grid_spec=pltpu.PrefetchScalarGridSpec(
            num_scalar_prefetch=1,
            grid=(4 * count,),
            in_specs=in_specs,
            out_specs=out_specs,
            scratch_shapes=[
                pltpu.VMEM((heads, 256, ROWS), BF16),
                pltpu.VMEM((heads, TILE, ROWS), BF16),
                pltpu.VMEM((8, ROWS), F32),
            ],
        ),
        out_shape=out_shape,
        input_output_aliases=aliases,
        compiler_params=pltpu.CompilerParams(
            dimension_semantics=("arbitrary",), vmem_limit_bytes=32 << 20
        ),
        cost_estimate=pl.CostEstimate(
            flops=14 << 30, bytes_accessed=12 << 20, transcendentals=2 << 20
        ),
        name="attention_forward",
    )(block_places, query256, keys_values, key_anchor, row_info, tables, *previous)


def backward_kernel(branch, heads, *refs):
    refs = list(refs)
    if branch > 0:
        del refs[11:13]
    backward_tile(branch, heads, *refs)


def backward_tile(
    branch,
    heads,
    exp_ref,
    bucket_ref,
    low_ref,
    max_ref,
    total_ref,
    query_ref,
    grad_ref,
    mixed_t_ref,
    kv_ref,
    dquery_in,
    dtable_in,
    dquery_ref,
    dtable_ref,
    kept_ref,
    sent_ref,
    grad_z,
    query_n,
    grad_n,
    dprob_ref,
    dscore_ref,
    prob_ref,
    high_hot,
    low_parts,
    delta_ref,
    scale_ref,
):
    tile_index = pl.program_id(0)
    offset = 128 * branch
    chunks = (ROWS - offset) // 128

    @pl.when(tile_index == 0)
    def _():
        grad_t = grad_ref[offset:, :].astype(F32).T
        part = lax.broadcasted_iota(jnp.int32, (256, ROWS - offset), 0) // 64
        lane_part = lax.broadcasted_iota(jnp.int32, (ROWS - offset, 256), 1) // 64
        for head in range(heads):
            grad_z[head, :, offset:] = jnp.where(part == head + 1, grad_t, 0.0).astype(BF16)
            query_n[head, offset:, :] = jnp.where(
                lane_part == head, query_ref[offset:, :].astype(F32), 0.0
            ).astype(BF16)
            grad_n[head, offset:, :] = jnp.where(
                lane_part == head + 1, grad_ref[offset:, :].astype(F32), 0.0
            ).astype(BF16)
            delta_ref[head : head + 1, offset:] = jnp.sum(
                grad_t[64 + 64 * head : 128 + 64 * head]
                * mixed_t_ref[64 * head : 64 * head + 64, offset:],
                axis=0,
                keepdims=True,
            )
        if branch == 0:
            dquery_ref[...] = jnp.zeros(dquery_ref.shape, F32)
            dtable_ref[...] = jnp.zeros(dtable_ref.shape, F32)
        else:
            dquery_ref[...] = dquery_in[...]
            dtable_ref[...] = dtable_in[...]

    keys_values = kv_ref[...].reshape(TILE, 384)
    key_t = transpose_low(keys_values[:, 0:256])
    for head in range(heads):
        dprob_ref[head, :, offset:] = dot(keys_values[:, 128:384], grad_z[head, :, offset:])
        scale_ref[head : head + 1, offset:] = jnp.exp(
            max_ref[0, head : head + 1, offset:] - total_ref[head : head + 1, offset:]
        )

    def build(group, slot):
        start = pl.multiple_of(group * GROUP, GROUP)
        one = jnp.ones((GROUP, 128), BF16)
        zero = jnp.zeros((GROUP, 128), BF16)
        for chunk in range(chunks):
            lanes = slice(offset + chunk * 128, offset + chunk * 128 + 128)
            bucket = bucket_ref[pl.ds(start, GROUP), lanes]
            low = low_ref[pl.ds(start, GROUP), lanes]
            for high in range(8):
                hot = jnp.where(bucket >= jnp.asarray(4 * high, BF16), one, zero)
                high_hot[slot, GROUP * high : GROUP * high + GROUP, lanes] = hot
            matches = [low == jnp.asarray(value, BF16) for value in range(4)]
            for head in range(heads):
                prob = (
                    exp_ref[head, pl.ds(start, GROUP), lanes] * scale_ref[head : head + 1, lanes]
                )
                dscore = prob * (
                    dprob_ref[head, pl.ds(start, GROUP), lanes]
                    - delta_ref[head : head + 1, lanes]
                )
                dscore_low = dscore.astype(BF16)
                prob_ref[head, pl.ds(start, GROUP), lanes] = prob.astype(BF16)
                dscore_ref[head, pl.ds(start, GROUP), lanes] = dscore_low
                for value in range(4):
                    row = GROUP * (value * heads + head)
                    low_parts[slot, row : row + GROUP, lanes] = jnp.where(
                        matches[value], dscore_low, zero
                    )

    def product(slot):
        return times_transpose(high_hot[slot, :, offset:], low_parts[slot, :, offset:])

    groups = TILE // GROUP
    build(0, 0)
    build(1, 1)

    def step(index, carry):
        even = product(0) + product(1)
        build(4 * index + 2, 2)
        build(4 * index + 3, 3)
        odd = product(2) + product(3)
        following = jnp.minimum(4 * index + 4, groups - 2)
        build(following, 0)
        build(following + 1, 1)
        dtable_ref[...] = dtable_ref[...] + (even + odd)
        return carry

    lax.fori_loop(0, groups // 4, step, 0)
    dkey = jnp.zeros((TILE, 256), F32)
    dvalue = jnp.zeros((TILE, 256), F32)
    for head in range(heads):
        dkey = dkey + dot(dscore_ref[head, :, offset:], query_n[head, offset:, :])
        dvalue = dvalue + dot(prob_ref[head, :, offset:], grad_n[head, offset:, :])
        rows = slice(64 * head, 64 * head + 64)
        dquery_ref[rows, offset:] = dquery_ref[rows, offset:] + dot(
            key_t[rows], dscore_ref[head, :, offset:]
        )
    shape = (1, 2, 64, 128)
    parts = (dkey[:, 0:128], dkey[:, 128:256] + dvalue[:, 0:128], dvalue[:, 128:256])
    for i, value in enumerate(parts):
        lanes = slice(128 * i, 128 * i + 128)
        kept_ref[:, :, :, lanes] = value[:128].reshape(shape)
        sent_ref[:, :, :, lanes] = value[128:].astype(BF16).reshape(shape)


def attention_backward(branch, saved, query256, grad256, mixed_t, keys_values, carried, heads):
    exps, buckets, lows, maxima, totals = saved
    members = keys_values.shape[0]
    tiles = members // 2
    first = branch * tiles
    def whole(shape):
        return pl.BlockSpec(shape, lambda t: (0,) * len(shape))

    in_specs = [
        pl.BlockSpec((heads, TILE, ROWS), lambda t: (0, first + t, 0)),
        pl.BlockSpec((TILE, ROWS), lambda t: (first + t, 0)),
        pl.BlockSpec((TILE, ROWS), lambda t: (first + t, 0)),
        pl.BlockSpec((1, 8, ROWS), lambda t: (first + t, 0, 0)),
        whole((8, ROWS)),
        whole((ROWS, 256)),
        whole((ROWS, 256)),
        whole((192, ROWS)),
        pl.BlockSpec((2, 2, 64, 384), lambda t: (t, branch, 0, 0)),
    ]
    if branch == 0:
        carried = (totals, totals)
        in_specs += [whole((8, ROWS)), whole((8, ROWS))]
        aliases = {}
    else:
        in_specs += [
            whole((192, ROWS)),
            whole((128, 64 * heads)),
            pl.BlockSpec(memory_space=pl.ANY),
            pl.BlockSpec(memory_space=pl.ANY),
        ]
        aliases = {11: 2, 12: 3}
    return pl.pallas_call(
        functools.partial(backward_kernel, branch, heads),
        grid=(tiles,),
        in_specs=in_specs,
        out_specs=[
            whole((192, ROWS)),
            whole((128, 64 * heads)),
            pl.BlockSpec((1, 2, 64, 384), lambda t: (t, branch, 0, 0)),
            pl.BlockSpec((1, 2, 64, 384), lambda t: (t, branch, 0, 0)),
        ],
        out_shape=[
            jax.ShapeDtypeStruct((192, ROWS), F32),
            jax.ShapeDtypeStruct((128, 64 * heads), F32),
            jax.ShapeDtypeStruct((tiles, 8, 64, 384), F32),
            jax.ShapeDtypeStruct((tiles, 8, 64, 384), BF16),
        ],
        input_output_aliases=aliases,
        scratch_shapes=[
            pltpu.VMEM((heads, 256, ROWS), BF16),
            pltpu.VMEM((heads, ROWS, 256), BF16),
            pltpu.VMEM((heads, ROWS, 256), BF16),
            pltpu.VMEM((heads, TILE, ROWS), F32),
            pltpu.VMEM((heads, TILE, ROWS), BF16),
            pltpu.VMEM((heads, TILE, ROWS), BF16),
            pltpu.VMEM((4, 128, ROWS), BF16),
            pltpu.VMEM((4, 64 * heads, ROWS), BF16),
            pltpu.VMEM((8, ROWS), F32),
            pltpu.VMEM((8, ROWS), F32),
        ],
        compiler_params=pltpu.CompilerParams(
            dimension_semantics=("arbitrary",), vmem_limit_bytes=58 << 20
        ),
        cost_estimate=pl.CostEstimate(
            flops=8 << 30, bytes_accessed=6 << 20, transcendentals=1 << 18
        ),
        name="attention_backward",
    )(exps, buckets, lows, maxima, totals, query256, grad256, mixed_t, keys_values, *carried)


def arrange_kernel(half_rows, query_rows, plane_ref, *refs):
    block_refs, out_ref, rows_ref = refs[:4], refs[4], refs[5]
    rows_ref[...] = jnp.zeros(rows_ref.shape, F32)
    for distance in range(4):
        plane = plane_ref[0] ^ distance
        block = block_refs[distance][...].astype(F32)
        start = pl.multiple_of(plane * half_rows, half_rows)
        rows_ref[pl.ds(start, half_rows), 64:256] = block[:half_rows, 0:192]
        start = pl.multiple_of((7 - plane) * half_rows, half_rows)
        rows_ref[pl.ds(start, half_rows), 64:256] = block[:half_rows, 192:384]
        start = pl.multiple_of(8 * half_rows + plane * query_rows, 8)
        rows_ref[pl.ds(start, query_rows), 64:256] = block[half_rows:, 0:192]
    out_ref[...] = rows_ref[...].astype(BF16)


def arrange_rows(blocks, plane, half_rows, query_rows):
    return pl.pallas_call(
        functools.partial(arrange_kernel, half_rows, query_rows),
        in_specs=[pl.BlockSpec(memory_space=pltpu.SMEM)]
        + [pl.BlockSpec(memory_space=pltpu.VMEM)] * 4,
        out_specs=pl.BlockSpec(memory_space=pltpu.VMEM),
        out_shape=jax.ShapeDtypeStruct((ROWS, 256), BF16),
        scratch_shapes=[pltpu.VMEM((ROWS, 256), F32)],
        name="arrange_rows",
    )(plane[None], *blocks)


def widen_kernel(group, order_ref, near_ref, far_ref, *out_refs):
    step = pl.program_id(0) ^ (order_ref[0] // group)
    half_steps = pl.num_programs(0) // 2
    inner = order_ref[0] % group

    def from_pieces(pieces_ref):
        rows = pieces_ref.shape[-2]
        for k in range(group):
            start = 0
            for out_ref in out_refs:
                columns = out_ref.shape[-1]
                lanes = slice(start, start + columns)
                if len(pieces_ref.shape) == 4:
                    for s in range(2):
                        block = pieces_ref[k ^ inner, s ^ order_ref[1], :, lanes]
                        out_ref[s, k * rows : (k + 1) * rows, :] = block.astype(F32)
                else:
                    block = pieces_ref[k ^ inner, :, lanes]
                    out_ref[k * rows : (k + 1) * rows, :] = block.astype(F32)
                start += columns

    pl.when(step < half_steps)(lambda: from_pieces(near_ref))
    pl.when(step >= half_steps)(lambda: from_pieces(far_ref))


def widen_rows(near, far, order, columns):
    half, rows, width = near.shape[0], near.shape[-2], near.shape[-1]
    sides = near.shape[1:-2]
    group = min(4, half)
    if rows % 16 != 0:
        pieces = jnp.concatenate([near, far], axis=0)
        position = jnp.arange(2 * half, dtype=jnp.int32) ^ order[0]
        whole = jnp.take(pieces, position, axis=0).astype(F32)
        if sides:
            whole = jnp.swapaxes(jnp.where(order[1] == 1, whole[:, ::-1], whole), 0, 1)
        whole = whole.reshape(sides + (2 * half * rows, width))
        ends = [sum(columns[: i + 1]) for i in range(len(columns))]
        return [whole[..., end - c : end] for end, c in zip(ends, columns)]
    zeros = (0,) * (len(sides) + 2)
    half_steps = half // group

    def piece_map(part):
        def index(r, o):
            order_step = o[0] // group
            first = jnp.where(order_step >= half_steps, 1 - part, part) * half_steps
            inside = jnp.clip(r, first, first + half_steps - 1)
            return ((inside ^ order_step) % half_steps,) + zeros

        return index

    def out_map(r, o):
        return (0,) * len(sides) + (r, 0)

    return pl.pallas_call(
        functools.partial(widen_kernel, group),
        grid_spec=pltpu.PrefetchScalarGridSpec(
            num_scalar_prefetch=1,
            grid=(2 * half_steps,),
            in_specs=[pl.BlockSpec((group,) + near.shape[1:], piece_map(part)) for part in range(2)],
            out_specs=[pl.BlockSpec(sides + (group * rows, c), out_map) for c in columns],
        ),
        out_shape=[jax.ShapeDtypeStruct(sides + (2 * half * rows, c), F32) for c in columns],
        compiler_params=pltpu.CompilerParams(
            dimension_semantics=("arbitrary",), vmem_limit_bytes=24 << 20
        ),
        cost_estimate=pl.CostEstimate(
            flops=0, bytes_accessed=6 * near.size * 2, transcendentals=0
        ),
        name="widen_rows",
    )(order, near, far)


def widen_heads_kernel(count, order_ref, near_ref, far_ref, *out_refs):
    def from_pieces(pieces_ref):
        odd = order_ref[1] == 1
        first, second = pieces_ref[0, 0].astype(F32), pieces_ref[0, 1].astype(F32)
        low = jnp.where(odd, second, first)
        high = jnp.where(odd, first, second)
        size = low.shape[1] // 3
        for i, out_ref in enumerate(out_refs):
            lanes = slice(i * size, (i + 1) * size)
            out_ref[...] = jnp.concatenate([low[:, lanes], high[:, lanes]], axis=1)

    near = (pl.program_id(0) ^ order_ref[0]) < count // 2
    pl.when(near)(lambda: from_pieces(near_ref))
    pl.when(jnp.logical_not(near))(lambda: from_pieces(far_ref))


def widen_heads(near, far, order, odd):
    half, _, rows, width = near.shape
    count = 2 * half
    columns = 2 * width // 3

    def piece(part):
        def index(r, o):
            first = jnp.where(o[0] >= half, 1 - part, part) * half
            inside = jnp.clip(r, first, first + half - 1)
            return ((inside ^ o[0]) % half, 0, 0, 0)

        return index

    return pl.pallas_call(
        functools.partial(widen_heads_kernel, count),
        grid_spec=pltpu.PrefetchScalarGridSpec(
            num_scalar_prefetch=1,
            grid=(count,),
            in_specs=[pl.BlockSpec((1, 2, rows, width), piece(part)) for part in range(2)],
            out_specs=[pl.BlockSpec((rows, columns), lambda r, o: (r, 0))] * 3,
        ),
        out_shape=[jax.ShapeDtypeStruct((count * rows, columns), F32)] * 3,
        compiler_params=pltpu.CompilerParams(dimension_semantics=("arbitrary",)),
        cost_estimate=pl.CostEstimate(
            flops=0, bytes_accessed=12 * count * rows * width, transcendentals=0
        ),
        name="widen_heads",
    )(jnp.stack([order, odd]), near, far)


def pack_kernel(*refs):
    out_ref = refs[-1]
    rows = [ref[...].reshape(1, -1).astype(F32) for ref in refs[:8]]
    out_ref[...] = jnp.zeros(out_ref.shape, BF16)
    out_ref[0:8, :] = jnp.concatenate(rows, axis=0).astype(BF16)
    table = refs[8][...].astype(F32)
    lanes = jnp.zeros((table.shape[0], 128 - table.shape[1]), F32)
    out_ref[16:32, 0:128] = jnp.concatenate([table, lanes], axis=1).astype(BF16)


def pack_vectors(vectors, table):
    vmem = pl.BlockSpec(memory_space=pltpu.VMEM)
    return pl.pallas_call(
        pack_kernel,
        in_specs=[vmem] * 9,
        out_specs=vmem,
        out_shape=jax.ShapeDtypeStruct((32, vectors[0].shape[0]), BF16),
        name="pack_vectors",
    )(*vectors, table)


def unpack_kernel(heads, where_ref, own_ref, other_ref, full_ref, bias_ref, table_ref, turned_ref):
    side = where_ref[0] == 1
    own, other = own_ref[...].astype(F32), other_ref[...].astype(F32)
    low, high = jnp.where(side, other, own), jnp.where(side, own, other)
    full = jnp.concatenate([low[0:8], high[0:8]], axis=1)
    full_ref[...] = full
    both = jnp.concatenate([low[16:32, 0:128], high[16:32, 0:128]], axis=0)
    square = jnp.concatenate([both, jnp.zeros((96, 128), F32)], axis=0)
    turned_ref[...] = square.T
    bias_ref[...] = jnp.zeros(bias_ref.shape, F32)
    table_ref[...] = jnp.zeros(table_ref.shape, F32)
    for plane in range(4):

        @pl.when(where_ref[1] == plane)
        def _(plane=plane):
            lanes = slice(192 * plane, 192 * plane + 192)
            bias_ref[0:1, 0:192] = full[0:1, lanes]
            bias_ref[1:2, 192:384] = full[1:2, lanes]
            table_ref[0:heads, :] = turned_ref[heads * plane : heads * plane + heads, :]


def unpack_vectors(own, other, side, plane, heads):
    vmem = pl.BlockSpec(memory_space=pltpu.VMEM)
    half = own.shape[1]
    return pl.pallas_call(
        functools.partial(unpack_kernel, heads),
        in_specs=[pl.BlockSpec(memory_space=pltpu.SMEM)] + [vmem] * 2,
        out_specs=[vmem] * 3,
        out_shape=[
            jax.ShapeDtypeStruct((8, 2 * half), F32),
            jax.ShapeDtypeStruct((8, half), F32),
            jax.ShapeDtypeStruct((8, 128), F32),
        ],
        scratch_shapes=[pltpu.VMEM((128, 128), F32)],
        name="unpack_vectors",
    )(jnp.stack([side, plane]), own, other)


def finish_kernel(half_rows, query_rows, where_ref, dquery_ref, kv_ref, kv_far_ref, x_ref, *refs):
    block_refs, sent_ref, kept_ref, sums_ref, query_ref, value_ref, low_ref = (
        refs[:4],
        *refs[4:],
    )
    keys = 8 * half_rows
    value_ref[...] = kv_ref[...] + kv_far_ref[...].astype(F32)
    query = dquery_ref[...].T.astype(BF16).astype(F32) * 0.125
    query_ref[...] = query
    low_ref[...] = jnp.zeros(low_ref.shape, BF16)
    low_ref[:, 0:192] = query.astype(BF16)
    low_ref[0:keys, 192:576] = value_ref[...].astype(BF16)
    plane = where_ref[0]
    for distance in range(4):
        other = plane ^ distance
        block_ref = block_refs[distance]
        first = pl.multiple_of(other * half_rows, half_rows)
        second = pl.multiple_of((7 - other) * half_rows, half_rows)
        third = pl.multiple_of(keys + other * query_rows, 8)
        rows = half_rows + query_rows
        block_ref[0:half_rows, 0:192] = query_ref[pl.ds(first, half_rows), :].astype(BF16)
        block_ref[0:half_rows, 192:384] = query_ref[pl.ds(second, half_rows), :].astype(BF16)
        tail = query_ref[pl.ds(third, query_rows), :]
        tail = jnp.concatenate([tail, jnp.zeros_like(tail)], axis=1)
        content = jnp.concatenate(
            [value_ref[pl.ds(first, half_rows), :], value_ref[pl.ds(second, half_rows), :]], axis=0
        )
        block_ref[half_rows:, :] = jnp.concatenate([tail, content], axis=0).astype(BF16)
    width = x_ref.shape[1] // 2
    for target_ref, flip in ((sent_ref, 1), (kept_ref, 0)):
        start = pl.multiple_of((where_ref[1] ^ flip) * width, width)
        product = contract_rows(x_ref[:, pl.ds(start, width)], low_ref[...])
        target_ref[...] = product.astype(target_ref.dtype)
    rounded = low_ref[...].astype(F32)
    sums_ref[...] = jnp.zeros(sums_ref.shape, F32)
    sums_ref[0:1, :] = jnp.sum(rounded, axis=0, keepdims=True)


def finish_heads(dquery_t, kv, kv_far, plane_x, plane, core, half_rows, query_rows):
    keys = 8 * half_rows
    block_rows = half_rows + query_rows + 2 * half_rows
    width = plane_x.shape[1] // 2
    vmem = pl.BlockSpec(memory_space=pltpu.VMEM)
    return pl.pallas_call(
        functools.partial(finish_kernel, half_rows, query_rows),
        in_specs=[pl.BlockSpec(memory_space=pltpu.SMEM)] + [vmem] * 4,
        out_specs=[vmem] * 7,
        out_shape=[jax.ShapeDtypeStruct((block_rows, 384), BF16)] * 4
        + [
            jax.ShapeDtypeStruct((width, 576), BF16),
            jax.ShapeDtypeStruct((width, 576), F32),
            jax.ShapeDtypeStruct((8, 576), F32),
        ],
        scratch_shapes=[
            pltpu.VMEM((ROWS, 192), F32),
            pltpu.VMEM((keys, 384), F32),
            pltpu.VMEM((ROWS, 576), BF16),
        ],
        compiler_params=pltpu.CompilerParams(vmem_limit_bytes=32 << 20),
        cost_estimate=pl.CostEstimate(flops=1 << 30, bytes_accessed=6 << 20, transcendentals=0),
        name="finish_heads",
    )(jnp.stack([plane, core]), dquery_t, kv, kv_far, plane_x)


def after(value, *earlier):
    return lax.optimization_barrier((value,) + earlier)[0]


def row_major(value):
    return with_layout_constraint(value, Layout(major_to_minor=tuple(range(value.ndim))))


class Chain:
    def __init__(self, state, stages):
        self.state, self.stages = state, stages
        self.leave()

    def leave(self):
        if self.stages:
            self.sent, self.kept = self.stages[0][0](self.state)
            self.arrived = self.stages[0][1](self.sent)

    def advance(self, token):
        kept = jax.tree.map(lambda leaf: after(leaf, token), self.kept)
        self.state = self.stages[0][2](kept, self.arrived)
        self.stages = self.stages[1:]
        self.leave()
        return self.sent if self.stages else jax.tree.leaves(self.state)[0]

    def drain(self, token):
        while self.stages:
            token = self.advance(token)
        return token


def reverse_bits(value, count):
    result = jnp.zeros_like(value)
    bit, mirrored = 1, count // 2
    while bit < count:
        result = result + jnp.where((value & bit) != 0, mirrored, 0)
        bit, mirrored = bit * 2, mirrored // 2
    return result


def body(
    content,
    query_stream,
    token_order,
    targets,
    query_weight,
    key_weight,
    value_weight,
    output_weight,
    query_bias,
    value_bias,
    output_bias,
    bias_table,
    first_gain,
    first_shift,
    inner_weight,
    inner_bias,
    outer_weight,
    outer_bias,
    second_gain,
    second_shift,
    content_cotangent,
    query_cotangent,
):
    ctx = lax.axis_size("ctx")
    index = lax.axis_index("ctx")
    side = lax.axis_index("wt")
    members = ctx // 4
    plane = index // members
    member = index % members
    half_rows = content.shape[2]
    tok_rows = 2 * half_rows
    query_rows = query_stream.shape[1]
    rows_dev = tok_rows + query_rows
    width = content.shape[3]
    heads = bias_table.shape[1]
    my_heads = heads // 4
    head_width = my_heads * (width // heads)
    half_width = width // 2
    seq_length = tok_rows * ctx
    half_length = seq_length // 2
    order_row = token_order[0]
    target_row = targets[0]
    core_bit = (index & 1) == 1

    def swap(value, bit):
        return lax.ppermute(value, "ctx", [(i, i ^ bit) for i in range(ctx)])

    def swap_side(value):
        return lax.ppermute(value, "wt", [(0, 1), (1, 0)])

    def order_two(flag, mine, other, axis):
        low = jnp.where(flag, other, mine)
        high = jnp.where(flag, mine, other)
        return jnp.concatenate([low, high], axis=axis)

    def half_of_core(value):
        rows = value.shape[0] // 2
        return lax.dynamic_slice_in_dim(value, (index & 1) * rows, rows, 0)

    def both_cores(arrived):
        return order_two(core_bit, arrived, swap(arrived, 1), 0)

    def by_distance(blocks):
        flag = (plane & 1) == 1
        blocks = [jnp.where(flag, blocks[d ^ 1], blocks[d]) for d in range(4)]
        flag = (plane & 2) == 2
        return [jnp.where(flag, blocks[d ^ 2], blocks[d]) for d in range(4)]

    def exchange_planes(blocks):
        sent = by_distance(blocks)
        arrived = [sent[0]] + [swap(sent[d], d * members) for d in range(1, 4)]
        return by_distance(arrived)

    def pack_rows(rows):
        top = jnp.concatenate([rows[:half_rows], rows[half_rows:tok_rows]], axis=1)
        bottom = jnp.concatenate([rows[tok_rows:], jnp.zeros_like(rows[tok_rows:])], axis=1)
        return jnp.concatenate([top, bottom], axis=0)

    def unpack_rows(packed):
        return jnp.concatenate(
            [
                packed[:half_rows, :head_width],
                packed[:half_rows, head_width:],
                packed[half_rows:, :head_width],
            ],
            axis=0,
        )

    def plane_rows(blocks):
        pad = ROWS - 4 * rows_dev
        return jnp.concatenate(
            [blocks[d][:half_rows] for d in range(4)]
            + [blocks[3 - d][half_rows:tok_rows] for d in range(4)]
            + [blocks[d][tok_rows:] for d in range(4)]
            + [jnp.zeros((pad, blocks[0].shape[1]), blocks[0].dtype)],
            axis=0,
        )

    def split_rows(rows):
        blocks = []
        for d in range(4):
            parts = [
                rows[d * half_rows : (d + 1) * half_rows],
                rows[(7 - d) * half_rows : (8 - d) * half_rows],
            ]
            if rows.shape[0] > 4 * tok_rows:
                start = 4 * tok_rows + d * query_rows
                parts.append(rows[start : start + query_rows])
            blocks.append(jnp.concatenate(parts, axis=0))
        return blocks

    local_content = content[0].reshape(tok_rows, width)
    stacked = jnp.concatenate([local_content, query_stream[0]], axis=0)
    arrived_rows = [stacked] + [swap(stacked, d * members) for d in range(1, 4)]
    owner = plane // 2
    odd_plane = (plane & 1) == 1
    side_flag = side == 1
    shards = [query_weight, key_weight, value_weight]
    near_own = jnp.concatenate(
        [jnp.where(odd_plane, s[:, head_width:], s[:, :head_width]) for s in shards], axis=1
    )
    near_sent = half_of_core(near_own)
    near_other = both_cores(swap_side(near_sent))
    vectors = [
        query_bias,
        value_bias,
        output_bias,
        first_gain,
        first_shift,
        outer_bias,
        second_gain,
        second_shift,
    ]
    own_vectors = pack_vectors(vectors, bias_table)
    other_vectors = swap_side(own_vectors)
    full_vectors, head_bias, tables = unpack_vectors(
        own_vectors, other_vectors, side, plane, my_heads
    )
    (
        full_output_bias,
        full_first_gain,
        full_first_shift,
        full_outer_bias,
        full_second_gain,
        full_second_shift,
    ) = [full_vectors[i : i + 1] for i in range(2, 8)]
    buckets = 2 * bias_table.shape[0]

    places = jnp.arange(half_length, dtype=jnp.int32)
    key_place = jnp.concatenate(
        [places, (seq_length - 1 - places).reshape(4, -1)[::-1].reshape(-1)]
    )
    key_anchor = jnp.concatenate(
        [
            order_row[:half_length],
            order_row[half_length:][::-1].reshape(4, -1)[::-1].reshape(-1),
        ]
    )

    def of_member(array, count):
        return lax.dynamic_index_in_dim(
            array.reshape(-1, members, count), member, 1, keepdims=False
        ).reshape(-1)

    def by_member_distance(array):
        pieces = [array.reshape(8, members, -1)]
        bit = members // 2
        while bit >= 1:
            flag = (member & bit) != 0
            split = []
            for piece in pieces:
                size = piece.shape[1] // 2
                low, high = piece[:, :size], piece[:, size:]
                split.append(jnp.where(flag, high, low))
                split.append(jnp.where(flag, low, high))
            pieces = split
            bit //= 2
        return jnp.concatenate(pieces, axis=1)

    plane_targets = of_member(target_row, query_rows)
    target_anchor = jnp.sum(
        jnp.where(
            jnp.arange(seq_length, dtype=jnp.int32)[:, None] == plane_targets[None],
            order_row[:, None],
            0,
        ),
        axis=0,
    )
    pad_rows = ROWS - 4 * rows_dev
    row_anchor = jnp.concatenate(
        [of_member(key_anchor, half_rows), target_anchor, jnp.zeros((pad_rows,), jnp.int32)]
    )
    row_limit = jnp.concatenate(
        [
            of_member(key_place, half_rows) + 1,
            plane_targets,
            jnp.ones((pad_rows,), jnp.int32),
        ]
    )
    row_info = jnp.concatenate(
        [row_anchor[None], row_limit[None], jnp.zeros((6, ROWS), jnp.int32)], axis=0
    )

    def by_tile(array):
        parts = by_member_distance(array).reshape(4, 2, members // 2, 2, -1)
        return jnp.transpose(parts, (0, 2, 3, 1, 4)).reshape(-1)

    near_anchor = by_tile(key_anchor)
    key_anchor_wide = jnp.broadcast_to(near_anchor[:, None], (seq_length, 128))
    block_places = by_tile(key_place.reshape(-1, half_rows)[:, 0])
    head_weights = jnp.where(side == owner, near_own, near_other)
    plane_x = plane_rows(by_distance(arrived_rows))
    plane_kv = (
        dot(plane_x[: 4 * tok_rows], head_weights[:, head_width:]) + head_bias[1:2]
    ).astype(BF16)
    first_kv = plane_kv.reshape(1, 8, half_rows, 2 * head_width)
    far_kv = swap(first_kv, members // 2)
    bit = 1
    near_members = first_kv
    while bit < members // 2:
        near_members = jnp.concatenate([near_members, swap(near_members, bit)], axis=0)
        bit *= 2
    query_weights = jnp.pad(head_weights[:, :head_width], ((0, 0), (0, 256 - head_width)))
    query256 = ((dot(plane_x, query_weights) + head_bias[0:1, :256]) * 0.125).astype(BF16)

    output_early, outer_early, rest_own = lax.optimization_barrier(
        (
            output_weight,
            outer_weight,
            jnp.concatenate(
                [
                    jnp.where(odd_plane, s[:, :head_width], s[:, head_width:])
                    for s in lax.optimization_barrier(tuple(shards) + (plane_kv,))[:3]
                ],
                axis=1,
            ),
            query256,
        )
    )[:3]
    hidden_half = outer_weight.shape[0] // 2

    outer_sent = lax.dynamic_slice_in_dim(outer_early, (1 - side) * hidden_half, hidden_half, 0)
    output_arrived = swap_side(half_of_core(output_early))
    outer_arrived_half = swap_side(half_of_core(outer_sent))
    rest_arrived = swap_side(half_of_core(rest_own))

    forward_info = (key_anchor_wide, block_places, row_info, tables)
    first_half = attention_forward(0, query256, near_members, *forward_info, (), my_heads)
    far_members = far_kv
    bit = 1
    while bit < members // 2:
        far_members = jnp.concatenate([far_members, swap(far_members, bit)], axis=0)
        bit *= 2
    exps, bucket_ids, bucket_lows, maxima, _, _, mixed_t, mixed_plane, totals = attention_forward(
        1, query256, far_members, *forward_info, first_half, my_heads
    )
    keys_values = jnp.concatenate([near_members, far_members], axis=0)

    full_output = order_two(side_flag, output_weight, both_cores(after(output_arrived, mixed_plane)), 1)
    outer_kept = lax.dynamic_slice_in_dim(outer_weight, side * hidden_half, hidden_half, 0)
    outer_rows = order_two(side_flag, outer_kept, both_cores(after(outer_arrived_half, mixed_plane)), 1)
    rest_other = both_cores(after(rest_arrived, mixed_plane))
    full_qkv = []
    for i in range(3):
        lanes = slice(i * head_width, (i + 1) * head_width)
        other = order_two(odd_plane, near_other[:, lanes], rest_other[:, lanes], 1)
        full_qkv.append(order_two(side_flag, shards[i], other, 1))

    mixed_blocks = exchange_planes([pack_rows(block) for block in split_rows(mixed_plane)])
    mixed = jnp.concatenate([unpack_rows(block) for block in mixed_blocks], axis=1)
    branch = dot(mixed, full_output) + full_output_bias
    first_norm, first_back = jax.vjp(
        norm_of_sum, stacked.astype(F32), branch, full_first_gain, full_first_shift
    )
    first_low = first_norm.astype(BF16)
    both_first = jnp.concatenate([first_low, swap_side(first_low)], axis=0)
    inner_value = dot(both_first, inner_weight) + inner_bias.astype(F32)
    hidden_value, gelu_back = jax.vjp(gelu_exact, inner_value)
    hidden_low = hidden_value.astype(BF16)
    outer_part = dot(hidden_low, outer_rows)
    outer_arrived = swap_side(outer_part[rows_dev:].astype(BF16))
    outer_value = outer_part[:rows_dev] + outer_arrived.astype(F32) + full_outer_bias
    final_norm, second_back = jax.vjp(
        norm_of_sum, first_norm, outer_value, full_second_gain, full_second_shift
    )
    content_result = final_norm[:tok_rows].reshape(1, 2, half_rows, width).astype(BF16)
    query_result = final_norm[tok_rows:].reshape(1, query_rows, width).astype(BF16)
    cotangent = jnp.concatenate(
        [content_cotangent[0].reshape(tok_rows, width), query_cotangent[0]], axis=0
    )
    rest_grad, outer_grad, second_gain_grad, second_shift_grad = second_back(cotangent.astype(F32))
    outer_low = outer_grad.astype(BF16)
    both_outer = jnp.concatenate([outer_low, swap_side(outer_low)], axis=0)
    (inner_grad,) = gelu_back(times_transpose(both_outer, outer_rows))
    inner_low = inner_grad.astype(BF16)
    first_part = times_transpose(inner_low, inner_weight)
    first_arrived = swap_side(first_part[rows_dev:].astype(BF16))
    first_grad = rest_grad + (first_part[:rows_dev] + first_arrived.astype(F32))
    row_grad, branch_grad, first_gain_grad, first_shift_grad = first_back(first_grad)
    branch_low = branch_grad.astype(BF16)
    mixed_low = times_transpose(branch_low, full_output).astype(BF16)

    def to(bit):
        return lambda value: swap(value, bit)

    def leave_half(bit):
        def leave(parts):
            rows = parts[0].shape[0] // 2
            upper = jnp.where((index & bit) != 0, 1, 0)
            sent = [
                lax.dynamic_slice_in_dim(part, (1 - upper) * rows, rows, 0).astype(BF16)
                for part in parts
            ]
            return jnp.concatenate(sent, axis=1), parts

        return leave

    def add_half(bit):
        def add(parts, arrived):
            rows = parts[0].shape[0] // 2
            upper = jnp.where((index & bit) != 0, 1, 0)
            kept = [lax.dynamic_slice_in_dim(part, upper * rows, rows, 0) for part in parts]
            return [(kept[0].astype(F32) + arrived.astype(F32)).astype(kept[0].dtype)]

        return add

    def keep_all(state):
        return state, state

    def append(kept, arrived):
        return jnp.concatenate([kept, arrived], axis=0)

    bits = []
    bit = 1
    while bit < ctx:
        bits.append(bit)
        bit *= 2
    sum_stages = [(leave_half(bit), to(bit), add_half(bit)) for bit in bits]
    gather_stages = [(keep_all, to(bit), append) for bit in bits[::-1]]

    def leave_columns(parts):
        piece = parts[0].astype(BF16)
        left, right = piece[:, :half_width], piece[:, half_width:]
        return jnp.where(side_flag, left, right), jnp.where(side_flag, right, left)

    def pair_sides(kept, arrived):
        return jnp.stack([kept, arrived], axis=0)[None]

    def start_gather(parts):
        state = parts[0].astype(BF16)[None]
        return state, state

    core_half = index & 1

    def halves(left, right):
        size = left.shape[1] // 2
        parts = []
        for half in (1 - core_half, core_half):
            columns = lax.dynamic_slice_in_dim(left, half * size, size, 1)
            parts.append(contract_rows(columns, right).astype(BF16))
        return parts

    def add_pair(kept, arrived):
        return [(kept.astype(F32) + arrived.astype(F32)).astype(BF16)]

    first_stage = (lambda state: state, to(1), add_pair)
    outer_chain = Chain(
        halves(hidden_low, both_outer),
        [first_stage] + sum_stages[1:] + [(leave_columns, swap_side, pair_sides)] + gather_stages[:-1],
    )

    other_mixed = swap_side(after(mixed, inner_low))
    branch_left, branch_right = branch_low[:, :half_width], branch_low[:, half_width:]
    branch_kept = jnp.where(side_flag, branch_right, branch_left)
    inner_halves = halves(both_first, inner_low)
    branch_arrived = swap_side(after(jnp.where(side_flag, branch_left, branch_right), mixed_low))
    both_mixed = jnp.concatenate([mixed, other_mixed], axis=0)
    both_branch = jnp.concatenate([branch_kept, branch_arrived], axis=0)
    output_halves = halves(both_mixed, both_branch)
    joined_chain = Chain(
        [
            jnp.concatenate([inner, output], axis=1)
            for inner, output in zip(inner_halves, output_halves)
        ],
        [first_stage] + sum_stages[1:] + [(start_gather, to(bits[-1]), append)] + gather_stages[1:-1],
    )

    chains = {"O": outer_chain, "J": joined_chain}

    def run(order, token):
        for name in order:
            chain = chains.get(name)
            if chain is not None and chain.stages:
                token = chain.advance(token)
        return token

    grad_sent = by_distance(
        [
            pack_rows(mixed_low[:, d * head_width : (d + 1) * head_width])
            for d in range(4)
        ]
    )
    grad_blocks = [grad_sent[0]] + [swap(grad_sent[d], d * members) for d in range(1, 4)]
    token = run(GAPS[0], grad_sent[1])
    grad_blocks = lax.optimization_barrier(tuple(grad_blocks) + (token, joined_chain.sent))[:4]
    grad256 = arrange_rows(grad_blocks, plane, half_rows, query_rows)
    saved = (exps, bucket_ids, bucket_lows, maxima, totals)
    carried = None
    for call in range(4):
        if call == 0:
            token = run(GAPS[1], grad256)
            grad256 = after(grad256, token)
        else:
            token = run(GAPS[call + 1], carried[0])
            carried = (after(carried[0], token),) + carried[1:]
        carried = tuple(
            attention_backward(
                call, saved, query256, grad256, mixed_t, keys_values, carried, my_heads
            )
        )
    dquery_t, table_part, kv_kept, kv_sent = carried
    member_bits = [bit for bit in bits if bit < members]
    head_orders = TAIL.split("|")[0].split("K")
    token = run(head_orders[0], kv_sent)
    for bit in member_bits:
        kv_arrived = after(swap(kv_sent, bit), token)
        if bit < member_bits[-1]:
            pairs = (-1, 2, 8, half_rows, 2 * head_width)
            kept, arrived = kv_kept.reshape(pairs), kv_arrived.reshape(pairs)
            kv_sent = row_major((kept[:, 1] + arrived[:, 1].astype(F32)).astype(BF16))
            kv_kept = row_major(kept[:, 0] + arrived[:, 0].astype(F32))
        if bit == 1:
            token = run(head_orders[1], kv_sent)
    flat_kv = (8 * half_rows, 2 * head_width)
    *sent_distance, heads_sent, heads_kept, column_sums = finish_heads(
        dquery_t,
        kv_kept.reshape(flat_kv),
        after(kv_arrived, token).reshape(flat_kv),
        plane_x,
        plane,
        index & 1,
        half_rows,
        query_rows,
    )

    def add_first(kept, arrived):
        return [kept + arrived.astype(F32)]

    def leave_same(parts):
        return parts[0].astype(BF16), parts

    def add_side(kept, arrived):
        return (kept[0] + arrived.astype(F32)).astype(BF16)

    def choose_owner(kept, arrived):
        return jnp.where(owner == side, kept, arrived)[None]

    def append_plane(kept, arrived):
        return jnp.concatenate([kept, arrived], axis=0)[None]

    heads_chain = Chain(
        (heads_sent, heads_kept),
        [(lambda state: state, to(1), add_first)]
        + sum_stages[1 : len(member_bits)]
        + [
            (leave_same, swap_side, add_side),
            (keep_all, to(2 * members), choose_owner),
            (keep_all, to(members), append_plane),
        ]
        + [(keep_all, to(bit), append) for bit in member_bits[:0:-1]],
    )

    got_distance = [sent_distance[0]] + [
        swap(sent_distance[d], d * members) for d in range(1, 4)
    ]
    full_query, full_key, full_value = full_qkv

    blocks = table_part.reshape(8, GROUP, 4, my_heads, GROUP)
    same = jnp.eye(GROUP, dtype=F32)[None, :, None, None, :]
    table_cumulative = jnp.sum(blocks * same, axis=(1, 4))
    table_grad = table_cumulative - jnp.concatenate(
        [table_cumulative[1:], jnp.zeros_like(table_cumulative[:1])], axis=0
    )
    table_grad = table_grad.reshape(buckets, my_heads)

    def at_plane(values, axis):
        return jnp.concatenate(
            [jnp.where(plane == d, values, jnp.zeros_like(values)) for d in range(4)], axis=axis
        )

    inner_bias_part = jnp.sum(inner_low.astype(F32), axis=0)
    inner_bias_zero = jnp.zeros_like(inner_bias_part)
    late_small = jnp.concatenate(
        [
            at_plane(column_sums[0, :head_width], 0),
            at_plane(column_sums[0, 2 * head_width :], 0),
            jnp.sum(branch_low.astype(F32), axis=0),
            first_gain_grad.reshape(-1),
            first_shift_grad.reshape(-1),
            jnp.sum(outer_low.astype(F32), axis=0),
            second_gain_grad.reshape(-1),
            second_shift_grad.reshape(-1),
            jnp.where(side_flag, inner_bias_zero, inner_bias_part),
            jnp.where(side_flag, inner_bias_part, inner_bias_zero),
            at_plane(table_grad, 1).reshape(-1),
        ]
    )
    late_length = late_small.shape[0]
    late_small = jnp.pad(late_small, (0, -late_length % 1024)).reshape(-1, 128)

    def add_plain(kept, arrived):
        return kept + arrived

    late_chain = Chain(
        after(late_small, heads_chain.sent),
        [(keep_all, to(bit), add_plain) for bit in bits] + [(keep_all, swap_side, add_plain)],
    )

    chains["H"], chains["L"] = heads_chain, late_chain
    token = late_chain.sent
    row_order = jnp.stack([reverse_bits(index, ctx), side])
    for name in TAIL.split("|")[1]:
        if name == "X":
            arrived = lax.optimization_barrier(tuple(got_distance) + (token,))[:4]
            got_blocks = by_distance(arrived)
            packed_rows = half_rows + query_rows
            own_query = jnp.concatenate([unpack_rows(b[:packed_rows]) for b in got_blocks], axis=1)
            own_key = jnp.concatenate([b[packed_rows:, :head_width] for b in got_blocks], axis=1)
            own_value = jnp.concatenate([b[packed_rows:, head_width:] for b in got_blocks], axis=1)
            input_grad = row_grad + times_transpose(own_query, full_query)
            content_extra = times_transpose(own_key, full_key)
            content_extra = content_extra + times_transpose(own_value, full_value)
            content_gradient = input_grad[:tok_rows] + content_extra
            content_gradient = content_gradient.reshape(1, 2, half_rows, width)
            query_gradient = input_grad[tok_rows:].reshape(1, query_rows, width)
            token = content_gradient
        elif name in "ABC":
            chain = {"A": outer_chain, "B": joined_chain, "C": heads_chain}[name]
            token = chain.drain(token)
            near = chain.state
            if name == "A":
                far = after(swap(near, 1), token)
                outer_weight_grad = widen_rows(near, far, row_order, (half_width,))[0]
                outer_weight_grad = outer_weight_grad.reshape(2 * hidden_half, half_width)
                token = outer_weight_grad
            elif name == "B":
                far = after(swap(near, 1), token)
                inner_weight_grad, output_weight_grad = widen_rows(
                    near, far, row_order, (hidden_half, half_width)
                )
                token = inner_weight_grad
            else:
                far = after(swap(near, 1), token)
                qkv_grads = widen_heads(near, far, reverse_bits(member, members), plane & 1)
                token = qkv_grads[0]
        else:
            token = run(name, token)
    token = late_chain.drain(token)

    late_small = late_chain.state.reshape(-1)[:late_length]
    table_start = 8 * width + 2 * hidden_half
    table_all = late_small[table_start:].reshape(2, buckets // 2, heads)
    bias_table_grad = jnp.where(side_flag, table_all[1], table_all[0])

    def my_half(start, size):
        low = late_small[start : start + size]
        return jnp.where(side_flag, late_small[start + size : start + 2 * size], low)

    mine = [my_half(i * width, half_width) for i in range(8)]
    inner_bias_grad = my_half(8 * width, hidden_half)

    return (
        content_result,
        query_result,
        content_gradient,
        query_gradient,
        qkv_grads[0],
        qkv_grads[1],
        qkv_grads[2],
        output_weight_grad,
        mine[0],
        mine[1],
        mine[2],
        bias_table_grad,
        mine[3],
        mine[4],
        inner_weight_grad,
        inner_bias_grad,
        outer_weight_grad,
        mine[5],
        mine[6],
        mine[7],
    )


def solution(mesh):
    return jax.shard_map(
        body,
        mesh=mesh,
        in_specs=(
            P("wt", None, "ctx", None),
            P("wt", "ctx", None),
            P("wt", None),
            P("wt", None),
            P(None, "wt"),
            P(None, "wt"),
            P(None, "wt"),
            P(None, "wt"),
            P("wt"),
            P("wt"),
            P("wt"),
            P("wt", None),
            P("wt"),
            P("wt"),
            P(None, "wt"),
            P("wt"),
            P(None, "wt"),
            P("wt"),
            P("wt"),
            P("wt"),
            P("wt", None, "ctx", None),
            P("wt", "ctx", None),
        ),
        out_specs=(
            P("wt", None, "ctx", None),
            P("wt", "ctx", None),
            P("wt", None, "ctx", None),
            P("wt", "ctx", None),
            P(None, "wt"),
            P(None, "wt"),
            P(None, "wt"),
            P(None, "wt"),
            P("wt"),
            P("wt"),
            P("wt"),
            P("wt", None),
            P("wt"),
            P("wt"),
            P(None, "wt"),
            P("wt"),
            P(None, "wt"),
            P("wt"),
            P("wt"),
            P("wt"),
        ),
        check_vma=False,
    )
```

```python
import functools

import jax
import jax.numpy as jnp
from jax import lax
from jax.experimental import pallas as pl
from jax.experimental.layout import Layout, with_layout_constraint
from jax.experimental.pallas import tpu as pltpu
from jax.sharding import PartitionSpec as P

BF16 = jnp.bfloat16
F32 = jnp.float32
FAR_EDGES = (12, 16, 23, 32, 46, 64, 91)
NEGATIVE = -1e30
TILE = 256
ROWS = 640
GROUP = 16
GAPS = ['O', 'OJ', 'O', 'OJ', 'OJ']
TAIL = 'KJOK|HLHJOHXLJHLOHLBLHAC'


def layer_norm(hidden_rows, gain_row, shift_row):
    average = jnp.mean(hidden_rows, axis=-1, keepdims=True)
    centered = hidden_rows - average
    variance = jnp.mean(centered * centered, axis=-1, keepdims=True)
    return centered * lax.rsqrt(variance + 1e-05) * gain_row + shift_row


def norm_of_sum(residual, branch_value, gain_row, shift_row):
    return layer_norm(residual + branch_value, gain_row, shift_row)


def gelu_exact(values):
    return jax.nn.gelu(values, approximate=False)


def dot(left, right):
    return jnp.dot(left, right, preferred_element_type=F32)


def contract_rows(left, right):
    return lax.dot_general(left, right, (((0,), (0,)), ((), ())), preferred_element_type=F32)


def times_transpose(left, right):
    return lax.dot_general(left, right, (((1,), (1,)), ((), ())), preferred_element_type=F32)


def transpose_low(block):
    return block.astype(F32).T.astype(BF16)


def tile_branches(branch_index, process):
    for branch in range(4):
        pl.when(branch_index == branch)(functools.partial(process, 128 * branch))


def forward_kernel(call, count, heads, *refs):
    place_ref, query_ref, kv_ref, anchor_ref, row_ref, table_ref = refs[:6]
    refs = refs[6:]
    if call == 1:
        max_in, sum_in, mixed_in = refs[4:7]
        refs = refs[7:]
    exp_ref, bucket_ref, low_ref, max_ref, run_max, run_sum, mixed_t_ref = refs[:7]
    refs = refs[7:]
    if call == 1:
        mixed_ref, total_ref = refs[:2]
        refs = refs[2:]
    query_z, prob_ref, scale_ref = refs
    step = pl.program_id(0)
    branch_index = step // count
    tile_index = branch_index * (2 * count) + call * count + step % count

    @pl.when(step == 0)
    def _():
        query_t = transpose_low(query_ref[...])
        part = lax.broadcasted_iota(jnp.int32, (256, ROWS), 0) // 64
        for head in range(heads):
            query_z[head] = jnp.where(part == head, query_t.astype(F32), 0.0).astype(BF16)
        if call == 0:
            run_max[...] = jnp.full(run_max.shape, NEGATIVE, F32)
            run_sum[...] = jnp.zeros(run_sum.shape, F32)
            mixed_t_ref[...] = jnp.zeros(mixed_t_ref.shape, F32)
        else:
            run_max[...] = max_in[...]
            run_sum[...] = sum_in[...]
            mixed_t_ref[...] = mixed_in[...]

    place_sign = jnp.where(branch_index < 2, 1, -1)
    keys_values = kv_ref[...].reshape(TILE, 384)
    value_t = transpose_low(keys_values[:, 128:384])

    def process(offset):
        chunks = (ROWS - offset) // 128
        for head in range(heads):
            exp_ref[head, :, offset:] = dot(keys_values[:, 0:256], query_z[head, :, offset:])

        def bias_group(group, tops):
            start = pl.multiple_of(group * GROUP, GROUP)
            keys = anchor_ref[pl.ds(start, GROUP), :]
            row = start % 64 + lax.broadcasted_iota(jnp.int32, (GROUP, 128), 0)
            place = place_ref[tile_index * (TILE // 64) + start // 64] + place_sign * row
            new_tops = []
            for chunk in range(chunks):
                lanes = slice(offset + chunk * 128, offset + chunk * 128 + 128)
                relative = keys - row_ref[0:1, lanes]
                magnitude = jnp.abs(relative)
                bucket = jnp.minimum(magnitude, 8)
                for edge in FAR_EDGES:
                    bucket = bucket + jnp.where(magnitude >= edge, 1, 0)
                bucket = bucket + jnp.where(relative > 0, 16, 0)
                bucket_ref[pl.ds(start, GROUP), lanes] = bucket.astype(F32).astype(BF16)
                low_ref[pl.ds(start, GROUP), lanes] = (bucket & 3).astype(F32).astype(BF16)
                allowed = place < row_ref[1:2, lanes]
                for head in range(heads):
                    table = jnp.broadcast_to(table_ref[head : head + 1, :], (8, 128))
                    bias = jnp.concatenate(
                        [
                            jnp.take_along_axis(table, bucket[0:8], axis=1),
                            jnp.take_along_axis(table, bucket[8:16], axis=1),
                        ],
                        axis=0,
                    )
                    scores = exp_ref[head, pl.ds(start, GROUP), lanes] + bias
                    scores = jnp.where(allowed, scores, NEGATIVE)
                    exp_ref[head, pl.ds(start, GROUP), lanes] = scores
                    top = tops[chunk * heads + head]
                    new_tops.append(jnp.maximum(top, jnp.maximum(scores[0:8], scores[8:16])))
            return tuple(new_tops)

        tops = lax.fori_loop(
            0,
            TILE // GROUP,
            bias_group,
            tuple(jnp.full((8, 128), NEGATIVE, F32) for _ in range(chunks * heads)),
            unroll=4,
        )
        for chunk in range(chunks):
            lanes = slice(offset + chunk * 128, offset + chunk * 128 + 128)
            for head in range(heads):
                top = jnp.max(tops[chunk * heads + head], axis=0, keepdims=True)
                old = run_max[head : head + 1, lanes]
                new = jnp.maximum(old, top)
                scale_ref[head : head + 1, lanes] = jnp.exp(old - new)
                run_max[head : head + 1, lanes] = new
        max_ref[0] = run_max[...]

        def exp_group(group, sums):
            start = pl.multiple_of(group * GROUP, GROUP)
            new_sums = []
            for chunk in range(chunks):
                lanes = slice(offset + chunk * 128, offset + chunk * 128 + 128)
                for head in range(heads):
                    terms = jnp.exp(
                        exp_ref[head, pl.ds(start, GROUP), lanes] - run_max[head : head + 1, lanes]
                    )
                    exp_ref[head, pl.ds(start, GROUP), lanes] = terms
                    prob_ref[head, pl.ds(start, GROUP), lanes] = terms.astype(BF16)
                    new_sums.append(sums[chunk * heads + head] + (terms[0:8] + terms[8:16]))
            return tuple(new_sums)

        sums = lax.fori_loop(
            0,
            TILE // GROUP,
            exp_group,
            tuple(jnp.zeros((8, 128), F32) for _ in range(chunks * heads)),
        )
        for chunk in range(chunks):
            lanes = slice(offset + chunk * 128, offset + chunk * 128 + 128)
            for head in range(heads):
                run_sum[head : head + 1, lanes] = run_sum[head : head + 1, lanes] * scale_ref[
                    head : head + 1, lanes
                ] + jnp.sum(sums[chunk * heads + head], axis=0, keepdims=True)
        for head in range(heads):
            rows = slice(64 * head, 64 * head + 64)
            mixed_t_ref[rows, offset:] = mixed_t_ref[rows, offset:] * scale_ref[
                head : head + 1, offset:
            ] + dot(value_t[64 + 64 * head : 128 + 64 * head], prob_ref[head, :, offset:])

    tile_branches(branch_index, process)

    if call == 1:

        @pl.when(step == 4 * count - 1)
        def _():
            for head in range(heads):
                rows = slice(64 * head, 64 * head + 64)
                mixed_t_ref[rows, :] = mixed_t_ref[rows, :] / run_sum[head : head + 1, :]
                total_ref[head : head + 1, :] = run_max[head : head + 1, :] + jnp.log(
                    run_sum[head : head + 1, :]
                )
            mixed_ref[...] = mixed_t_ref[...].T.astype(BF16)


def attention_forward(
    call, query256, keys_values, key_anchor, block_places, row_info, tables, previous, heads
):
    count = keys_values.shape[0] // 2
    tiles = 8 * count
    total_keys = tiles * TILE

    def tile_of(s):
        return (s // count) * (2 * count) + call * count + s % count

    def whole(shape):
        return pl.BlockSpec(shape, lambda s, p: (0,) * len(shape))

    in_specs = [
        whole((ROWS, 256)),
        pl.BlockSpec((2, 2, 64, 384), lambda s, p: (s % count, s // count, 0, 0)),
        pl.BlockSpec((TILE, 128), lambda s, p: (tile_of(s), 0)),
        whole((8, ROWS)),
        whole((8, 128)),
    ]
    out_specs = [
        pl.BlockSpec((heads, TILE, ROWS), lambda s, p: (0, tile_of(s), 0)),
        pl.BlockSpec((TILE, ROWS), lambda s, p: (tile_of(s), 0)),
        pl.BlockSpec((TILE, ROWS), lambda s, p: (tile_of(s), 0)),
        pl.BlockSpec((1, 8, ROWS), lambda s, p: (tile_of(s), 0, 0)),
        whole((8, ROWS)),
        whole((8, ROWS)),
        whole((192, ROWS)),
    ]
    out_shape = [
        jax.ShapeDtypeStruct((heads, total_keys, ROWS), F32),
        jax.ShapeDtypeStruct((total_keys, ROWS), BF16),
        jax.ShapeDtypeStruct((total_keys, ROWS), BF16),
        jax.ShapeDtypeStruct((tiles, 8, ROWS), F32),
        jax.ShapeDtypeStruct((8, ROWS), F32),
        jax.ShapeDtypeStruct((8, ROWS), F32),
        jax.ShapeDtypeStruct((192, ROWS), F32),
    ]
    aliases = {}
    if call == 1:
        in_specs += [pl.BlockSpec(memory_space=pl.ANY)] * 4
        in_specs += [whole((8, ROWS)), whole((8, ROWS)), whole((192, ROWS))]
        out_specs += [whole((ROWS, 192)), whole((8, ROWS))]
        out_shape += [
            jax.ShapeDtypeStruct((ROWS, 192), BF16),
            jax.ShapeDtypeStruct((8, ROWS), F32),
        ]
        aliases = {6: 0, 7: 1, 8: 2, 9: 3}
    return pl.pallas_call(
        functools.partial(forward_kernel, call, count, heads),
        grid_spec=pltpu.PrefetchScalarGridSpec(
            num_scalar_prefetch=1,
            grid=(4 * count,),
            in_specs=in_specs,
            out_specs=out_specs,
            scratch_shapes=[
                pltpu.VMEM((heads, 256, ROWS), BF16),
                pltpu.VMEM((heads, TILE, ROWS), BF16),
                pltpu.VMEM((8, ROWS), F32),
            ],
        ),
        out_shape=out_shape,
        input_output_aliases=aliases,
        compiler_params=pltpu.CompilerParams(
            dimension_semantics=("arbitrary",), vmem_limit_bytes=32 << 20
        ),
        cost_estimate=pl.CostEstimate(
            flops=14 << 30, bytes_accessed=12 << 20, transcendentals=2 << 20
        ),
        name="attention_forward",
    )(block_places, query256, keys_values, key_anchor, row_info, tables, *previous)


def backward_kernel(branch, heads, *refs):
    refs = list(refs)
    if branch > 0:
        del refs[11:13]
    backward_tile(branch, heads, *refs)


def backward_tile(
    branch,
    heads,
    exp_ref,
    bucket_ref,
    low_ref,
    max_ref,
    total_ref,
    query_ref,
    grad_ref,
    mixed_t_ref,
    kv_ref,
    dquery_in,
    dtable_in,
    dquery_ref,
    dtable_ref,
    kept_ref,
    sent_ref,
    grad_z,
    query_n,
    grad_n,
    dprob_ref,
    dscore_ref,
    prob_ref,
    high_hot,
    low_parts,
    delta_ref,
    scale_ref,
):
    tile_index = pl.program_id(0)
    offset = 128 * branch
    chunks = (ROWS - offset) // 128

    @pl.when(tile_index == 0)
    def _():
        grad_t = grad_ref[offset:, :].astype(F32).T
        part = lax.broadcasted_iota(jnp.int32, (256, ROWS - offset), 0) // 64
        lane_part = lax.broadcasted_iota(jnp.int32, (ROWS - offset, 256), 1) // 64
        for head in range(heads):
            grad_z[head, :, offset:] = jnp.where(part == head + 1, grad_t, 0.0).astype(BF16)
            query_n[head, offset:, :] = jnp.where(
                lane_part == head, query_ref[offset:, :].astype(F32), 0.0
            ).astype(BF16)
            grad_n[head, offset:, :] = jnp.where(
                lane_part == head + 1, grad_ref[offset:, :].astype(F32), 0.0
            ).astype(BF16)
            delta_ref[head : head + 1, offset:] = jnp.sum(
                grad_t[64 + 64 * head : 128 + 64 * head]
                * mixed_t_ref[64 * head : 64 * head + 64, offset:],
                axis=0,
                keepdims=True,
            )
        if branch == 0:
            dquery_ref[...] = jnp.zeros(dquery_ref.shape, F32)
            dtable_ref[...] = jnp.zeros(dtable_ref.shape, F32)
        else:
            dquery_ref[...] = dquery_in[...]
            dtable_ref[...] = dtable_in[...]

    keys_values = kv_ref[...].reshape(TILE, 384)
    key_t = transpose_low(keys_values[:, 0:256])
    for head in range(heads):
        dprob_ref[head, :, offset:] = dot(keys_values[:, 128:384], grad_z[head, :, offset:])
        scale_ref[head : head + 1, offset:] = jnp.exp(
            max_ref[0, head : head + 1, offset:] - total_ref[head : head + 1, offset:]
        )

    def build(group, slot):
        start = pl.multiple_of(group * GROUP, GROUP)
        one = jnp.ones((GROUP, 128), BF16)
        zero = jnp.zeros((GROUP, 128), BF16)
        for chunk in range(chunks):
            lanes = slice(offset + chunk * 128, offset + chunk * 128 + 128)
            bucket = bucket_ref[pl.ds(start, GROUP), lanes]
            low = low_ref[pl.ds(start, GROUP), lanes]
            for high in range(8):
                hot = jnp.where(bucket >= jnp.asarray(4 * high, BF16), one, zero)
                high_hot[slot, GROUP * high : GROUP * high + GROUP, lanes] = hot
            matches = [low == jnp.asarray(value, BF16) for value in range(4)]
            for head in range(heads):
                prob = (
                    exp_ref[head, pl.ds(start, GROUP), lanes] * scale_ref[head : head + 1, lanes]
                )
                dscore = prob * (
                    dprob_ref[head, pl.ds(start, GROUP), lanes]
                    - delta_ref[head : head + 1, lanes]
                )
                dscore_low = dscore.astype(BF16)
                prob_ref[head, pl.ds(start, GROUP), lanes] = prob.astype(BF16)
                dscore_ref[head, pl.ds(start, GROUP), lanes] = dscore_low
                for value in range(4):
                    row = GROUP * (value * heads + head)
                    low_parts[slot, row : row + GROUP, lanes] = jnp.where(
                        matches[value], dscore_low, zero
                    )

    def product(slot):
        return times_transpose(high_hot[slot, :, offset:], low_parts[slot, :, offset:])

    groups = TILE // GROUP
    build(0, 0)
    build(1, 1)

    def step(index, carry):
        even = product(0) + product(1)
        build(4 * index + 2, 2)
        build(4 * index + 3, 3)
        odd = product(2) + product(3)
        following = jnp.minimum(4 * index + 4, groups - 2)
        build(following, 0)
        build(following + 1, 1)
        dtable_ref[...] = dtable_ref[...] + (even + odd)
        return carry

    lax.fori_loop(0, groups // 4, step, 0)
    dkey = jnp.zeros((TILE, 256), F32)
    dvalue = jnp.zeros((TILE, 256), F32)
    for head in range(heads):
        dkey = dkey + dot(dscore_ref[head, :, offset:], query_n[head, offset:, :])
        dvalue = dvalue + dot(prob_ref[head, :, offset:], grad_n[head, offset:, :])
        rows = slice(64 * head, 64 * head + 64)
        dquery_ref[rows, offset:] = dquery_ref[rows, offset:] + dot(
            key_t[rows], dscore_ref[head, :, offset:]
        )
    shape = (1, 2, 64, 128)
    parts = (dkey[:, 0:128], dkey[:, 128:256] + dvalue[:, 0:128], dvalue[:, 128:256])
    for i, value in enumerate(parts):
        lanes = slice(128 * i, 128 * i + 128)
        kept_ref[:, :, :, lanes] = value[:128].reshape(shape)
        sent_ref[:, :, :, lanes] = value[128:].astype(BF16).reshape(shape)


def attention_backward(branch, saved, query256, grad256, mixed_t, keys_values, carried, heads):
    exps, buckets, lows, maxima, totals = saved
    members = keys_values.shape[0]
    tiles = members // 2
    first = branch * tiles
    def whole(shape):
        return pl.BlockSpec(shape, lambda t: (0,) * len(shape))

    in_specs = [
        pl.BlockSpec((heads, TILE, ROWS), lambda t: (0, first + t, 0)),
        pl.BlockSpec((TILE, ROWS), lambda t: (first + t, 0)),
        pl.BlockSpec((TILE, ROWS), lambda t: (first + t, 0)),
        pl.BlockSpec((1, 8, ROWS), lambda t: (first + t, 0, 0)),
        whole((8, ROWS)),
        whole((ROWS, 256)),
        whole((ROWS, 256)),
        whole((192, ROWS)),
        pl.BlockSpec((2, 2, 64, 384), lambda t: (t, branch, 0, 0)),
    ]
    if branch == 0:
        carried = (totals, totals)
        in_specs += [whole((8, ROWS)), whole((8, ROWS))]
        aliases = {}
    else:
        in_specs += [
            whole((192, ROWS)),
            whole((128, 64 * heads)),
            pl.BlockSpec(memory_space=pl.ANY),
            pl.BlockSpec(memory_space=pl.ANY),
        ]
        aliases = {11: 2, 12: 3}
    return pl.pallas_call(
        functools.partial(backward_kernel, branch, heads),
        grid=(tiles,),
        in_specs=in_specs,
        out_specs=[
            whole((192, ROWS)),
            whole((128, 64 * heads)),
            pl.BlockSpec((1, 2, 64, 384), lambda t: (t, branch, 0, 0)),
            pl.BlockSpec((1, 2, 64, 384), lambda t: (t, branch, 0, 0)),
        ],
        out_shape=[
            jax.ShapeDtypeStruct((192, ROWS), F32),
            jax.ShapeDtypeStruct((128, 64 * heads), F32),
            jax.ShapeDtypeStruct((tiles, 8, 64, 384), F32),
            jax.ShapeDtypeStruct((tiles, 8, 64, 384), BF16),
        ],
        input_output_aliases=aliases,
        scratch_shapes=[
            pltpu.VMEM((heads, 256, ROWS), BF16),
            pltpu.VMEM((heads, ROWS, 256), BF16),
            pltpu.VMEM((heads, ROWS, 256), BF16),
            pltpu.VMEM((heads, TILE, ROWS), F32),
            pltpu.VMEM((heads, TILE, ROWS), BF16),
            pltpu.VMEM((heads, TILE, ROWS), BF16),
            pltpu.VMEM((4, 128, ROWS), BF16),
            pltpu.VMEM((4, 64 * heads, ROWS), BF16),
            pltpu.VMEM((8, ROWS), F32),
            pltpu.VMEM((8, ROWS), F32),
        ],
        compiler_params=pltpu.CompilerParams(
            dimension_semantics=("arbitrary",), vmem_limit_bytes=58 << 20
        ),
        cost_estimate=pl.CostEstimate(
            flops=5 << 30, bytes_accessed=6 << 20, transcendentals=1 << 18
        ),
        name="attention_backward",
    )(exps, buckets, lows, maxima, totals, query256, grad256, mixed_t, keys_values, *carried)


def arrange_kernel(half_rows, query_rows, plane_ref, *refs):
    block_refs, out_ref, rows_ref = refs[:4], refs[4], refs[5]
    rows_ref[...] = jnp.zeros(rows_ref.shape, F32)
    for distance in range(4):
        plane = plane_ref[0] ^ distance
        block = block_refs[distance][...].astype(F32)
        start = pl.multiple_of(plane * half_rows, half_rows)
        rows_ref[pl.ds(start, half_rows), 64:256] = block[:half_rows, 0:192]
        start = pl.multiple_of((7 - plane) * half_rows, half_rows)
        rows_ref[pl.ds(start, half_rows), 64:256] = block[:half_rows, 192:384]
        start = pl.multiple_of(8 * half_rows + plane * query_rows, 8)
        rows_ref[pl.ds(start, query_rows), 64:256] = block[half_rows:, 0:192]
    out_ref[...] = rows_ref[...].astype(BF16)


def arrange_rows(blocks, plane, half_rows, query_rows):
    return pl.pallas_call(
        functools.partial(arrange_kernel, half_rows, query_rows),
        in_specs=[pl.BlockSpec(memory_space=pltpu.SMEM)]
        + [pl.BlockSpec(memory_space=pltpu.VMEM)] * 4,
        out_specs=pl.BlockSpec(memory_space=pltpu.VMEM),
        out_shape=jax.ShapeDtypeStruct((ROWS, 256), BF16),
        scratch_shapes=[pltpu.VMEM((ROWS, 256), F32)],
        name="arrange_rows",
    )(plane[None], *blocks)


def widen_kernel(group, order_ref, near_ref, far_ref, *out_refs):
    step = pl.program_id(0) ^ (order_ref[0] // group)
    half_steps = pl.num_programs(0) // 2
    inner = order_ref[0] % group

    def from_pieces(pieces_ref):
        rows = pieces_ref.shape[-2]
        for k in range(group):
            start = 0
            for out_ref in out_refs:
                columns = out_ref.shape[-1]
                lanes = slice(start, start + columns)
                if len(pieces_ref.shape) == 4:
                    for s in range(2):
                        block = pieces_ref[k ^ inner, s ^ order_ref[1], :, lanes]
                        out_ref[s, k * rows : (k + 1) * rows, :] = block.astype(F32)
                else:
                    block = pieces_ref[k ^ inner, :, lanes]
                    out_ref[k * rows : (k + 1) * rows, :] = block.astype(F32)
                start += columns

    pl.when(step < half_steps)(lambda: from_pieces(near_ref))
    pl.when(step >= half_steps)(lambda: from_pieces(far_ref))


def widen_rows(near, far, order, columns):
    half, rows, width = near.shape[0], near.shape[-2], near.shape[-1]
    sides = near.shape[1:-2]
    group = min(4, half)
    if rows % 16 != 0:
        pieces = jnp.concatenate([near, far], axis=0)
        position = jnp.arange(2 * half, dtype=jnp.int32) ^ order[0]
        whole = jnp.take(pieces, position, axis=0).astype(F32)
        if sides:
            whole = jnp.swapaxes(jnp.where(order[1] == 1, whole[:, ::-1], whole), 0, 1)
        whole = whole.reshape(sides + (2 * half * rows, width))
        ends = [sum(columns[: i + 1]) for i in range(len(columns))]
        return [whole[..., end - c : end] for end, c in zip(ends, columns)]
    zeros = (0,) * (len(sides) + 2)
    half_steps = half // group

    def piece_map(part):
        def index(r, o):
            order_step = o[0] // group
            first = jnp.where(order_step >= half_steps, 1 - part, part) * half_steps
            inside = jnp.clip(r, first, first + half_steps - 1)
            return ((inside ^ order_step) % half_steps,) + zeros

        return index

    def out_map(r, o):
        return (0,) * len(sides) + (r, 0)

    return pl.pallas_call(
        functools.partial(widen_kernel, group),
        grid_spec=pltpu.PrefetchScalarGridSpec(
            num_scalar_prefetch=1,
            grid=(2 * half_steps,),
            in_specs=[pl.BlockSpec((group,) + near.shape[1:], piece_map(part)) for part in range(2)],
            out_specs=[pl.BlockSpec(sides + (group * rows, c), out_map) for c in columns],
        ),
        out_shape=[jax.ShapeDtypeStruct(sides + (2 * half * rows, c), F32) for c in columns],
        compiler_params=pltpu.CompilerParams(
            dimension_semantics=("arbitrary",), vmem_limit_bytes=24 << 20
        ),
        cost_estimate=pl.CostEstimate(
            flops=0, bytes_accessed=6 * near.size * 2, transcendentals=0
        ),
        name="widen_rows",
    )(order, near, far)


def widen_heads_kernel(count, order_ref, near_ref, far_ref, *out_refs):
    def from_pieces(pieces_ref):
        odd = order_ref[1] == 1
        first, second = pieces_ref[0, 0].astype(F32), pieces_ref[0, 1].astype(F32)
        low = jnp.where(odd, second, first)
        high = jnp.where(odd, first, second)
        size = low.shape[1] // 3
        for i, out_ref in enumerate(out_refs):
            lanes = slice(i * size, (i + 1) * size)
            out_ref[...] = jnp.concatenate([low[:, lanes], high[:, lanes]], axis=1)

    near = (pl.program_id(0) ^ order_ref[0]) < count // 2
    pl.when(near)(lambda: from_pieces(near_ref))
    pl.when(jnp.logical_not(near))(lambda: from_pieces(far_ref))


def widen_heads(near, far, order, odd):
    half, _, rows, width = near.shape
    count = 2 * half
    columns = 2 * width // 3

    def piece(part):
        def index(r, o):
            first = jnp.where(o[0] >= half, 1 - part, part) * half
            inside = jnp.clip(r, first, first + half - 1)
            return ((inside ^ o[0]) % half, 0, 0, 0)

        return index

    return pl.pallas_call(
        functools.partial(widen_heads_kernel, count),
        grid_spec=pltpu.PrefetchScalarGridSpec(
            num_scalar_prefetch=1,
            grid=(count,),
            in_specs=[pl.BlockSpec((1, 2, rows, width), piece(part)) for part in range(2)],
            out_specs=[pl.BlockSpec((rows, columns), lambda r, o: (r, 0))] * 3,
        ),
        out_shape=[jax.ShapeDtypeStruct((count * rows, columns), F32)] * 3,
        compiler_params=pltpu.CompilerParams(dimension_semantics=("arbitrary",)),
        cost_estimate=pl.CostEstimate(
            flops=0, bytes_accessed=12 * count * rows * width, transcendentals=0
        ),
        name="widen_heads",
    )(jnp.stack([order, odd]), near, far)


def pack_kernel(*refs):
    out_ref = refs[-1]
    rows = [ref[...].reshape(1, -1).astype(F32) for ref in refs[:8]]
    out_ref[...] = jnp.zeros(out_ref.shape, BF16)
    out_ref[0:8, :] = jnp.concatenate(rows, axis=0).astype(BF16)
    table = refs[8][...].astype(F32)
    lanes = jnp.zeros((table.shape[0], 128 - table.shape[1]), F32)
    out_ref[16:32, 0:128] = jnp.concatenate([table, lanes], axis=1).astype(BF16)


def pack_vectors(vectors, table):
    vmem = pl.BlockSpec(memory_space=pltpu.VMEM)
    return pl.pallas_call(
        pack_kernel,
        in_specs=[vmem] * 9,
        out_specs=vmem,
        out_shape=jax.ShapeDtypeStruct((32, vectors[0].shape[0]), BF16),
        name="pack_vectors",
    )(*vectors, table)


def unpack_kernel(heads, where_ref, own_ref, other_ref, full_ref, bias_ref, table_ref, turned_ref):
    side = where_ref[0] == 1
    own, other = own_ref[...].astype(F32), other_ref[...].astype(F32)
    low, high = jnp.where(side, other, own), jnp.where(side, own, other)
    full = jnp.concatenate([low[0:8], high[0:8]], axis=1)
    full_ref[...] = full
    both = jnp.concatenate([low[16:32, 0:128], high[16:32, 0:128]], axis=0)
    square = jnp.concatenate([both, jnp.zeros((96, 128), F32)], axis=0)
    turned_ref[...] = square.T
    bias_ref[...] = jnp.zeros(bias_ref.shape, F32)
    table_ref[...] = jnp.zeros(table_ref.shape, F32)
    for plane in range(4):

        @pl.when(where_ref[1] == plane)
        def _(plane=plane):
            lanes = slice(192 * plane, 192 * plane + 192)
            bias_ref[0:1, 0:192] = full[0:1, lanes]
            bias_ref[1:2, 192:384] = full[1:2, lanes]
            table_ref[0:heads, :] = turned_ref[heads * plane : heads * plane + heads, :]


def unpack_vectors(own, other, side, plane, heads):
    vmem = pl.BlockSpec(memory_space=pltpu.VMEM)
    half = own.shape[1]
    return pl.pallas_call(
        functools.partial(unpack_kernel, heads),
        in_specs=[pl.BlockSpec(memory_space=pltpu.SMEM)] + [vmem] * 2,
        out_specs=[vmem] * 3,
        out_shape=[
            jax.ShapeDtypeStruct((8, 2 * half), F32),
            jax.ShapeDtypeStruct((8, half), F32),
            jax.ShapeDtypeStruct((8, 128), F32),
        ],
        scratch_shapes=[pltpu.VMEM((128, 128), F32)],
        name="unpack_vectors",
    )(jnp.stack([side, plane]), own, other)


def finish_kernel(half_rows, query_rows, where_ref, dquery_ref, kv_ref, kv_far_ref, x_ref, *refs):
    block_refs, sent_ref, kept_ref, sums_ref, query_ref, value_ref, low_ref = (
        refs[:4],
        *refs[4:],
    )
    keys = 8 * half_rows
    value_ref[...] = kv_ref[...] + kv_far_ref[...].astype(F32)
    query = dquery_ref[...].T.astype(BF16).astype(F32) * 0.125
    query_ref[...] = query
    low_ref[...] = jnp.zeros(low_ref.shape, BF16)
    low_ref[:, 0:192] = query.astype(BF16)
    low_ref[0:keys, 192:576] = value_ref[...].astype(BF16)
    plane = where_ref[0]
    for distance in range(4):
        other = plane ^ distance
        block_ref = block_refs[distance]
        first = pl.multiple_of(other * half_rows, half_rows)
        second = pl.multiple_of((7 - other) * half_rows, half_rows)
        third = pl.multiple_of(keys + other * query_rows, 8)
        rows = half_rows + query_rows
        block_ref[0:half_rows, 0:192] = query_ref[pl.ds(first, half_rows), :].astype(BF16)
        block_ref[0:half_rows, 192:384] = query_ref[pl.ds(second, half_rows), :].astype(BF16)
        tail = query_ref[pl.ds(third, query_rows), :]
        tail = jnp.concatenate([tail, jnp.zeros_like(tail)], axis=1)
        content = jnp.concatenate(
            [value_ref[pl.ds(first, half_rows), :], value_ref[pl.ds(second, half_rows), :]], axis=0
        )
        block_ref[half_rows:, :] = jnp.concatenate([tail, content], axis=0).astype(BF16)
    width = x_ref.shape[1] // 2
    for target_ref, flip in ((sent_ref, 1), (kept_ref, 0)):
        start = pl.multiple_of((where_ref[1] ^ flip) * width, width)
        product = contract_rows(x_ref[:, pl.ds(start, width)], low_ref[...])
        target_ref[...] = product.astype(target_ref.dtype)
    rounded = low_ref[...].astype(F32)
    sums_ref[...] = jnp.zeros(sums_ref.shape, F32)
    sums_ref[0:1, :] = jnp.sum(rounded, axis=0, keepdims=True)


def finish_heads(dquery_t, kv, kv_far, plane_x, plane, core, half_rows, query_rows):
    keys = 8 * half_rows
    block_rows = half_rows + query_rows + 2 * half_rows
    width = plane_x.shape[1] // 2
    vmem = pl.BlockSpec(memory_space=pltpu.VMEM)
    return pl.pallas_call(
        functools.partial(finish_kernel, half_rows, query_rows),
        in_specs=[pl.BlockSpec(memory_space=pltpu.SMEM)] + [vmem] * 4,
        out_specs=[vmem] * 7,
        out_shape=[jax.ShapeDtypeStruct((block_rows, 384), BF16)] * 4
        + [
            jax.ShapeDtypeStruct((width, 576), BF16),
            jax.ShapeDtypeStruct((width, 576), F32),
            jax.ShapeDtypeStruct((8, 576), F32),
        ],
        scratch_shapes=[
            pltpu.VMEM((ROWS, 192), F32),
            pltpu.VMEM((keys, 384), F32),
            pltpu.VMEM((ROWS, 576), BF16),
        ],
        compiler_params=pltpu.CompilerParams(vmem_limit_bytes=32 << 20),
        cost_estimate=pl.CostEstimate(flops=1 << 30, bytes_accessed=6 << 20, transcendentals=0),
        name="finish_heads",
    )(jnp.stack([plane, core]), dquery_t, kv, kv_far, plane_x)


def after(value, *earlier):
    return lax.optimization_barrier((value,) + earlier)[0]


def row_major(value):
    return with_layout_constraint(value, Layout(major_to_minor=tuple(range(value.ndim))))


class Chain:
    def __init__(self, state, stages):
        self.state, self.stages = state, stages
        self.leave()

    def leave(self):
        if self.stages:
            self.sent, self.kept = self.stages[0][0](self.state)
            self.arrived = self.stages[0][1](self.sent)

    def advance(self, token):
        kept = jax.tree.map(lambda leaf: after(leaf, token), self.kept)
        self.state = self.stages[0][2](kept, self.arrived)
        self.stages = self.stages[1:]
        self.leave()
        return self.sent if self.stages else jax.tree.leaves(self.state)[0]

    def drain(self, token):
        while self.stages:
            token = self.advance(token)
        return token


def reverse_bits(value, count):
    result = jnp.zeros_like(value)
    bit, mirrored = 1, count // 2
    while bit < count:
        result = result + jnp.where((value & bit) != 0, mirrored, 0)
        bit, mirrored = bit * 2, mirrored // 2
    return result


def body(
    content,
    query_stream,
    token_order,
    targets,
    query_weight,
    key_weight,
    value_weight,
    output_weight,
    query_bias,
    value_bias,
    output_bias,
    bias_table,
    first_gain,
    first_shift,
    inner_weight,
    inner_bias,
    outer_weight,
    outer_bias,
    second_gain,
    second_shift,
    content_cotangent,
    query_cotangent,
):
    ctx = lax.axis_size("ctx")
    index = lax.axis_index("ctx")
    side = lax.axis_index("wt")
    members = ctx // 4
    plane = index // members
    member = index % members
    half_rows = content.shape[2]
    tok_rows = 2 * half_rows
    query_rows = query_stream.shape[1]
    rows_dev = tok_rows + query_rows
    width = content.shape[3]
    heads = bias_table.shape[1]
    my_heads = heads // 4
    head_width = my_heads * (width // heads)
    half_width = width // 2
    seq_length = tok_rows * ctx
    half_length = seq_length // 2
    order_row = token_order[0]
    target_row = targets[0]
    core_bit = (index & 1) == 1

    def swap(value, bit):
        return lax.ppermute(value, "ctx", [(i, i ^ bit) for i in range(ctx)])

    def swap_side(value):
        return lax.ppermute(value, "wt", [(0, 1), (1, 0)])

    def order_two(flag, mine, other, axis):
        low = jnp.where(flag, other, mine)
        high = jnp.where(flag, mine, other)
        return jnp.concatenate([low, high], axis=axis)

    def half_of_core(value):
        rows = value.shape[0] // 2
        return lax.dynamic_slice_in_dim(value, (index & 1) * rows, rows, 0)

    def both_cores(arrived):
        return order_two(core_bit, arrived, swap(arrived, 1), 0)

    def by_distance(blocks):
        flag = (plane & 1) == 1
        blocks = [jnp.where(flag, blocks[d ^ 1], blocks[d]) for d in range(4)]
        flag = (plane & 2) == 2
        return [jnp.where(flag, blocks[d ^ 2], blocks[d]) for d in range(4)]

    def exchange_planes(blocks):
        sent = by_distance(blocks)
        arrived = [sent[0]] + [swap(sent[d], d * members) for d in range(1, 4)]
        return by_distance(arrived)

    def pack_rows(rows):
        top = jnp.concatenate([rows[:half_rows], rows[half_rows:tok_rows]], axis=1)
        bottom = jnp.concatenate([rows[tok_rows:], jnp.zeros_like(rows[tok_rows:])], axis=1)
        return jnp.concatenate([top, bottom], axis=0)

    def unpack_rows(packed):
        return jnp.concatenate(
            [
                packed[:half_rows, :head_width],
                packed[:half_rows, head_width:],
                packed[half_rows:, :head_width],
            ],
            axis=0,
        )

    def plane_rows(blocks):
        pad = ROWS - 4 * rows_dev
        return jnp.concatenate(
            [blocks[d][:half_rows] for d in range(4)]
            + [blocks[3 - d][half_rows:tok_rows] for d in range(4)]
            + [blocks[d][tok_rows:] for d in range(4)]
            + [jnp.zeros((pad, blocks[0].shape[1]), blocks[0].dtype)],
            axis=0,
        )

    def split_rows(rows):
        blocks = []
        for d in range(4):
            parts = [
                rows[d * half_rows : (d + 1) * half_rows],
                rows[(7 - d) * half_rows : (8 - d) * half_rows],
            ]
            if rows.shape[0] > 4 * tok_rows:
                start = 4 * tok_rows + d * query_rows
                parts.append(rows[start : start + query_rows])
            blocks.append(jnp.concatenate(parts, axis=0))
        return blocks

    local_content = content[0].reshape(tok_rows, width)
    stacked = jnp.concatenate([local_content, query_stream[0]], axis=0)
    arrived_rows = [stacked] + [swap(stacked, d * members) for d in range(1, 4)]
    owner = plane // 2
    odd_plane = (plane & 1) == 1
    side_flag = side == 1
    shards = [query_weight, key_weight, value_weight]
    near_own = jnp.concatenate(
        [jnp.where(odd_plane, s[:, head_width:], s[:, :head_width]) for s in shards], axis=1
    )
    near_sent = half_of_core(near_own)
    near_other = both_cores(swap_side(near_sent))
    vectors = [
        query_bias,
        value_bias,
        output_bias,
        first_gain,
        first_shift,
        outer_bias,
        second_gain,
        second_shift,
    ]
    own_vectors = pack_vectors(vectors, bias_table)
    other_vectors = swap_side(own_vectors)
    full_vectors, head_bias, tables = unpack_vectors(
        own_vectors, other_vectors, side, plane, my_heads
    )
    (
        full_output_bias,
        full_first_gain,
        full_first_shift,
        full_outer_bias,
        full_second_gain,
        full_second_shift,
    ) = [full_vectors[i : i + 1] for i in range(2, 8)]
    buckets = 2 * bias_table.shape[0]

    places = jnp.arange(half_length, dtype=jnp.int32)
    key_place = jnp.concatenate(
        [places, (seq_length - 1 - places).reshape(4, -1)[::-1].reshape(-1)]
    )
    key_anchor = jnp.concatenate(
        [
            order_row[:half_length],
            order_row[half_length:][::-1].reshape(4, -1)[::-1].reshape(-1),
        ]
    )

    def of_member(array, count):
        return lax.dynamic_index_in_dim(
            array.reshape(-1, members, count), member, 1, keepdims=False
        ).reshape(-1)

    def by_member_distance(array):
        pieces = [array.reshape(8, members, -1)]
        bit = members // 2
        while bit >= 1:
            flag = (member & bit) != 0
            split = []
            for piece in pieces:
                size = piece.shape[1] // 2
                low, high = piece[:, :size], piece[:, size:]
                split.append(jnp.where(flag, high, low))
                split.append(jnp.where(flag, low, high))
            pieces = split
            bit //= 2
        return jnp.concatenate(pieces, axis=1)

    plane_targets = of_member(target_row, query_rows)
    target_anchor = jnp.sum(
        jnp.where(
            jnp.arange(seq_length, dtype=jnp.int32)[:, None] == plane_targets[None],
            order_row[:, None],
            0,
        ),
        axis=0,
    )
    pad_rows = ROWS - 4 * rows_dev
    row_anchor = jnp.concatenate(
        [of_member(key_anchor, half_rows), target_anchor, jnp.zeros((pad_rows,), jnp.int32)]
    )
    row_limit = jnp.concatenate(
        [
            of_member(key_place, half_rows) + 1,
            plane_targets,
            jnp.ones((pad_rows,), jnp.int32),
        ]
    )
    row_info = jnp.concatenate(
        [row_anchor[None], row_limit[None], jnp.zeros((6, ROWS), jnp.int32)], axis=0
    )

    def by_tile(array):
        parts = by_member_distance(array).reshape(4, 2, members // 2, 2, -1)
        return jnp.transpose(parts, (0, 2, 3, 1, 4)).reshape(-1)

    near_anchor = by_tile(key_anchor)
    key_anchor_wide = jnp.broadcast_to(near_anchor[:, None], (seq_length, 128))
    block_places = by_tile(key_place.reshape(-1, half_rows)[:, 0])
    head_weights = jnp.where(side == owner, near_own, near_other)
    plane_x = plane_rows(by_distance(arrived_rows))
    plane_kv = (
        dot(plane_x[: 4 * tok_rows], head_weights[:, head_width:]) + head_bias[1:2]
    ).astype(BF16)
    first_kv = plane_kv.reshape(1, 8, half_rows, 2 * head_width)
    far_kv = swap(first_kv, members // 2)
    bit = 1
    near_members = first_kv
    while bit < members // 2:
        near_members = jnp.concatenate([near_members, swap(near_members, bit)], axis=0)
        bit *= 2
    query_weights = jnp.pad(head_weights[:, :head_width], ((0, 0), (0, 256 - head_width)))
    query256 = ((dot(plane_x, query_weights) + head_bias[0:1, :256]) * 0.125).astype(BF16)

    output_early, outer_early, rest_own = lax.optimization_barrier(
        (
            output_weight,
            outer_weight,
            jnp.concatenate(
                [
                    jnp.where(odd_plane, s[:, :head_width], s[:, head_width:])
                    for s in lax.optimization_barrier(tuple(shards) + (plane_kv,))[:3]
                ],
                axis=1,
            ),
            query256,
        )
    )[:3]
    hidden_half = outer_weight.shape[0] // 2

    outer_sent = lax.dynamic_slice_in_dim(outer_early, (1 - side) * hidden_half, hidden_half, 0)
    output_arrived = swap_side(half_of_core(output_early))
    outer_arrived_half = swap_side(half_of_core(outer_sent))
    rest_arrived = swap_side(half_of_core(rest_own))

    forward_info = (key_anchor_wide, block_places, row_info, tables)
    first_half = attention_forward(0, query256, near_members, *forward_info, (), my_heads)
    far_members = far_kv
    bit = 1
    while bit < members // 2:
        far_members = jnp.concatenate([far_members, swap(far_members, bit)], axis=0)
        bit *= 2
    exps, bucket_ids, bucket_lows, maxima, _, _, mixed_t, mixed_plane, totals = attention_forward(
        1, query256, far_members, *forward_info, first_half, my_heads
    )
    keys_values = jnp.concatenate([near_members, far_members], axis=0)

    full_output = order_two(side_flag, output_weight, both_cores(after(output_arrived, mixed_plane)), 1)
    outer_kept = lax.dynamic_slice_in_dim(outer_weight, side * hidden_half, hidden_half, 0)
    outer_rows = order_two(side_flag, outer_kept, both_cores(after(outer_arrived_half, mixed_plane)), 1)
    rest_other = both_cores(after(rest_arrived, mixed_plane))
    full_qkv = []
    for i in range(3):
        lanes = slice(i * head_width, (i + 1) * head_width)
        other = order_two(odd_plane, near_other[:, lanes], rest_other[:, lanes], 1)
        full_qkv.append(order_two(side_flag, shards[i], other, 1))

    mixed_blocks = exchange_planes([pack_rows(block) for block in split_rows(mixed_plane)])
    mixed = jnp.concatenate([unpack_rows(block) for block in mixed_blocks], axis=1)
    branch = dot(mixed, full_output) + full_output_bias
    first_norm, first_back = jax.vjp(
        norm_of_sum, stacked.astype(F32), branch, full_first_gain, full_first_shift
    )
    first_low = first_norm.astype(BF16)
    both_first = jnp.concatenate([first_low, swap_side(first_low)], axis=0)
    inner_value = dot(both_first, inner_weight) + inner_bias.astype(F32)
    hidden_value, gelu_back = jax.vjp(gelu_exact, inner_value)
    hidden_low = hidden_value.astype(BF16)
    outer_part = dot(hidden_low, outer_rows)
    outer_arrived = swap_side(outer_part[rows_dev:].astype(BF16))
    outer_value = outer_part[:rows_dev] + outer_arrived.astype(F32) + full_outer_bias
    final_norm, second_back = jax.vjp(
        norm_of_sum, first_norm, outer_value, full_second_gain, full_second_shift
    )
    content_result = final_norm[:tok_rows].reshape(1, 2, half_rows, width).astype(BF16)
    query_result = final_norm[tok_rows:].reshape(1, query_rows, width).astype(BF16)
    cotangent = jnp.concatenate(
        [content_cotangent[0].reshape(tok_rows, width), query_cotangent[0]], axis=0
    )
    rest_grad, outer_grad, second_gain_grad, second_shift_grad = second_back(cotangent.astype(F32))
    outer_low = outer_grad.astype(BF16)
    both_outer = jnp.concatenate([outer_low, swap_side(outer_low)], axis=0)
    (inner_grad,) = gelu_back(times_transpose(both_outer, outer_rows))
    inner_low = inner_grad.astype(BF16)
    first_part = times_transpose(inner_low, inner_weight)
    first_arrived = swap_side(first_part[rows_dev:].astype(BF16))
    first_grad = rest_grad + (first_part[:rows_dev] + first_arrived.astype(F32))
    row_grad, branch_grad, first_gain_grad, first_shift_grad = first_back(first_grad)
    branch_low = branch_grad.astype(BF16)
    mixed_low = times_transpose(branch_low, full_output).astype(BF16)

    def to(bit):
        return lambda value: swap(value, bit)

    def leave_half(bit):
        def leave(parts):
            rows = parts[0].shape[0] // 2
            upper = jnp.where((index & bit) != 0, 1, 0)
            sent = [
                lax.dynamic_slice_in_dim(part, (1 - upper) * rows, rows, 0).astype(BF16)
                for part in parts
            ]
            return jnp.concatenate(sent, axis=1), parts

        return leave

    def add_half(bit):
        def add(parts, arrived):
            rows = parts[0].shape[0] // 2
            upper = jnp.where((index & bit) != 0, 1, 0)
            kept = [lax.dynamic_slice_in_dim(part, upper * rows, rows, 0) for part in parts]
            return [(kept[0].astype(F32) + arrived.astype(F32)).astype(kept[0].dtype)]

        return add

    def keep_all(state):
        return state, state

    def append(kept, arrived):
        return jnp.concatenate([kept, arrived], axis=0)

    bits = []
    bit = 1
    while bit < ctx:
        bits.append(bit)
        bit *= 2
    sum_stages = [(leave_half(bit), to(bit), add_half(bit)) for bit in bits]
    gather_stages = [(keep_all, to(bit), append) for bit in bits[::-1]]

    def leave_columns(parts):
        piece = parts[0].astype(BF16)
        left, right = piece[:, :half_width], piece[:, half_width:]
        return jnp.where(side_flag, left, right), jnp.where(side_flag, right, left)

    def pair_sides(kept, arrived):
        return jnp.stack([kept, arrived], axis=0)[None]

    def start_gather(parts):
        state = parts[0].astype(BF16)[None]
        return state, state

    core_half = index & 1

    def halves(left, right):
        size = left.shape[1] // 2
        parts = []
        for half in (1 - core_half, core_half):
            columns = lax.dynamic_slice_in_dim(left, half * size, size, 1)
            parts.append(contract_rows(columns, right).astype(BF16))
        return parts

    def add_pair(kept, arrived):
        return [(kept.astype(F32) + arrived.astype(F32)).astype(BF16)]

    first_stage = (lambda state: state, to(1), add_pair)
    outer_chain = Chain(
        halves(hidden_low, both_outer),
        [first_stage] + sum_stages[1:] + [(leave_columns, swap_side, pair_sides)] + gather_stages[:-1],
    )

    other_mixed = swap_side(after(mixed, inner_low))
    branch_left, branch_right = branch_low[:, :half_width], branch_low[:, half_width:]
    branch_kept = jnp.where(side_flag, branch_right, branch_left)
    inner_halves = halves(both_first, inner_low)
    branch_arrived = swap_side(after(jnp.where(side_flag, branch_left, branch_right), mixed_low))
    both_mixed = jnp.concatenate([mixed, other_mixed], axis=0)
    both_branch = jnp.concatenate([branch_kept, branch_arrived], axis=0)
    output_halves = halves(both_mixed, both_branch)
    joined_chain = Chain(
        [
            jnp.concatenate([inner, output], axis=1)
            for inner, output in zip(inner_halves, output_halves)
        ],
        [first_stage] + sum_stages[1:] + [(start_gather, to(bits[-1]), append)] + gather_stages[1:-1],
    )

    chains = {"O": outer_chain, "J": joined_chain}

    def run(order, token):
        for name in order:
            chain = chains.get(name)
            if chain is not None and chain.stages:
                token = chain.advance(token)
        return token

    grad_sent = by_distance(
        [
            pack_rows(mixed_low[:, d * head_width : (d + 1) * head_width])
            for d in range(4)
        ]
    )
    grad_blocks = [grad_sent[0]] + [swap(grad_sent[d], d * members) for d in range(1, 4)]
    token = run(GAPS[0], grad_sent[1])
    grad_blocks = lax.optimization_barrier(tuple(grad_blocks) + (token, joined_chain.sent))[:4]
    grad256 = arrange_rows(grad_blocks, plane, half_rows, query_rows)
    saved = (exps, bucket_ids, bucket_lows, maxima, totals)
    carried = None
    for call in range(4):
        if call == 0:
            token = run(GAPS[1], grad256)
            grad256 = after(grad256, token)
        else:
            token = run(GAPS[call + 1], carried[0])
            carried = (after(carried[0], token),) + carried[1:]
        carried = tuple(
            attention_backward(
                call, saved, query256, grad256, mixed_t, keys_values, carried, my_heads
            )
        )
    dquery_t, table_part, kv_kept, kv_sent = carried
    member_bits = [bit for bit in bits if bit < members]
    head_orders = TAIL.split("|")[0].split("K")
    token = run(head_orders[0], kv_sent)
    for bit in member_bits:
        kv_arrived = after(swap(kv_sent, bit), token)
        if bit < member_bits[-1]:
            pairs = (-1, 2, 8, half_rows, 2 * head_width)
            kept, arrived = kv_kept.reshape(pairs), kv_arrived.reshape(pairs)
            kv_sent = row_major((kept[:, 1] + arrived[:, 1].astype(F32)).astype(BF16))
            kv_kept = row_major(kept[:, 0] + arrived[:, 0].astype(F32))
        if bit == 1:
            token = run(head_orders[1], kv_sent)
    flat_kv = (8 * half_rows, 2 * head_width)
    *sent_distance, heads_sent, heads_kept, column_sums = finish_heads(
        dquery_t,
        kv_kept.reshape(flat_kv),
        after(kv_arrived, token).reshape(flat_kv),
        plane_x,
        plane,
        index & 1,
        half_rows,
        query_rows,
    )

    def add_first(kept, arrived):
        return [kept + arrived.astype(F32)]

    def leave_same(parts):
        return parts[0].astype(BF16), parts

    def add_side(kept, arrived):
        return (kept[0] + arrived.astype(F32)).astype(BF16)

    def choose_owner(kept, arrived):
        return jnp.where(owner == side, kept, arrived)[None]

    def append_plane(kept, arrived):
        return jnp.concatenate([kept, arrived], axis=0)[None]

    heads_chain = Chain(
        (heads_sent, heads_kept),
        [(lambda state: state, to(1), add_first)]
        + sum_stages[1 : len(member_bits)]
        + [
            (leave_same, swap_side, add_side),
            (keep_all, to(2 * members), choose_owner),
            (keep_all, to(members), append_plane),
        ]
        + [(keep_all, to(bit), append) for bit in member_bits[:0:-1]],
    )

    got_distance = [sent_distance[0]] + [
        swap(sent_distance[d], d * members) for d in range(1, 4)
    ]
    full_query, full_key, full_value = full_qkv

    blocks = table_part.reshape(8, GROUP, 4, my_heads, GROUP)
    same = jnp.eye(GROUP, dtype=F32)[None, :, None, None, :]
    table_cumulative = jnp.sum(blocks * same, axis=(1, 4))
    table_grad = table_cumulative - jnp.concatenate(
        [table_cumulative[1:], jnp.zeros_like(table_cumulative[:1])], axis=0
    )
    table_grad = table_grad.reshape(buckets, my_heads)

    def at_plane(values, axis):
        return jnp.concatenate(
            [jnp.where(plane == d, values, jnp.zeros_like(values)) for d in range(4)], axis=axis
        )

    inner_bias_part = jnp.sum(inner_low.astype(F32), axis=0)
    inner_bias_zero = jnp.zeros_like(inner_bias_part)
    late_small = jnp.concatenate(
        [
            at_plane(column_sums[0, :head_width], 0),
            at_plane(column_sums[0, 2 * head_width :], 0),
            jnp.sum(branch_low.astype(F32), axis=0),
            first_gain_grad.reshape(-1),
            first_shift_grad.reshape(-1),
            jnp.sum(outer_low.astype(F32), axis=0),
            second_gain_grad.reshape(-1),
            second_shift_grad.reshape(-1),
            jnp.where(side_flag, inner_bias_zero, inner_bias_part),
            jnp.where(side_flag, inner_bias_part, inner_bias_zero),
            at_plane(table_grad, 1).reshape(-1),
        ]
    )
    late_length = late_small.shape[0]
    late_small = jnp.pad(late_small, (0, -late_length % 1024)).reshape(-1, 128)

    def add_plain(kept, arrived):
        return kept + arrived

    late_chain = Chain(
        after(late_small, heads_chain.sent),
        [(keep_all, to(bit), add_plain) for bit in bits] + [(keep_all, swap_side, add_plain)],
    )

    chains["H"], chains["L"] = heads_chain, late_chain
    token = late_chain.sent
    row_order = jnp.stack([reverse_bits(index, ctx), side])
    for name in TAIL.split("|")[1]:
        if name == "X":
            arrived = lax.optimization_barrier(tuple(got_distance) + (token,))[:4]
            got_blocks = by_distance(arrived)
            packed_rows = half_rows + query_rows
            own_query = jnp.concatenate([unpack_rows(b[:packed_rows]) for b in got_blocks], axis=1)
            own_key = jnp.concatenate([b[packed_rows:, :head_width] for b in got_blocks], axis=1)
            own_value = jnp.concatenate([b[packed_rows:, head_width:] for b in got_blocks], axis=1)
            input_grad = row_grad + times_transpose(own_query, full_query)
            content_extra = times_transpose(own_key, full_key)
            content_extra = content_extra + times_transpose(own_value, full_value)
            content_gradient = input_grad[:tok_rows] + content_extra
            content_gradient = content_gradient.reshape(1, 2, half_rows, width)
            query_gradient = input_grad[tok_rows:].reshape(1, query_rows, width)
            token = content_gradient
        elif name in "ABC":
            chain = {"A": outer_chain, "B": joined_chain, "C": heads_chain}[name]
            token = chain.drain(token)
            near = chain.state
            if name == "A":
                far = after(swap(near, 1), token)
                outer_weight_grad = widen_rows(near, far, row_order, (half_width,))[0]
                outer_weight_grad = outer_weight_grad.reshape(2 * hidden_half, half_width)
                token = outer_weight_grad
            elif name == "B":
                far = after(swap(near, 1), token)
                inner_weight_grad, output_weight_grad = widen_rows(
                    near, far, row_order, (hidden_half, half_width)
                )
                token = inner_weight_grad
            else:
                far = after(swap(near, 1), token)
                qkv_grads = widen_heads(near, far, reverse_bits(member, members), plane & 1)
                token = qkv_grads[0]
        else:
            token = run(name, token)
    token = late_chain.drain(token)

    late_small = late_chain.state.reshape(-1)[:late_length]
    table_start = 8 * width + 2 * hidden_half
    table_all = late_small[table_start:].reshape(2, buckets // 2, heads)
    bias_table_grad = jnp.where(side_flag, table_all[1], table_all[0])

    def my_half(start, size):
        low = late_small[start : start + size]
        return jnp.where(side_flag, late_small[start + size : start + 2 * size], low)

    mine = [my_half(i * width, half_width) for i in range(8)]
    inner_bias_grad = my_half(8 * width, hidden_half)

    return (
        content_result,
        query_result,
        content_gradient,
        query_gradient,
        qkv_grads[0],
        qkv_grads[1],
        qkv_grads[2],
        output_weight_grad,
        mine[0],
        mine[1],
        mine[2],
        bias_table_grad,
        mine[3],
        mine[4],
        inner_weight_grad,
        inner_bias_grad,
        outer_weight_grad,
        mine[5],
        mine[6],
        mine[7],
    )


def solution(mesh):
    return jax.shard_map(
        body,
        mesh=mesh,
        in_specs=(
            P("wt", None, "ctx", None),
            P("wt", "ctx", None),
            P("wt", None),
            P("wt", None),
            P(None, "wt"),
            P(None, "wt"),
            P(None, "wt"),
            P(None, "wt"),
            P("wt"),
            P("wt"),
            P("wt"),
            P("wt", None),
            P("wt"),
            P("wt"),
            P(None, "wt"),
            P("wt"),
            P(None, "wt"),
            P("wt"),
            P("wt"),
            P("wt"),
            P("wt", None, "ctx", None),
            P("wt", "ctx", None),
        ),
        out_specs=(
            P("wt", None, "ctx", None),
            P("wt", "ctx", None),
            P("wt", None, "ctx", None),
            P("wt", "ctx", None),
            P(None, "wt"),
            P(None, "wt"),
            P(None, "wt"),
            P(None, "wt"),
            P("wt"),
            P("wt"),
            P("wt"),
            P("wt", None),
            P("wt"),
            P("wt"),
            P(None, "wt"),
            P("wt"),
            P(None, "wt"),
            P("wt"),
            P("wt"),
            P("wt"),
        ),
        check_vma=False,
    )
```
